32 devices in a mesh: dp: 8 (over z, x), slot: 4 (over y, core).
Axes of the slice: x: 2, y: 2, z: 4, core: 2. Of those that a mesh axis runs over, the one named last changes fastest.
Arguments:
- byte_ids: int32 [1024, 8], P('dp'), may hold values from 0 to 255
- seg_ids: int32 [8, 128], P('dp'), may hold values from 0 to 1, never falling along the last dimension, each value on 1 to 96 neighbouring positions
- embed_table: bfloat16 [256, 768], P('dp'), may hold values from -6 to 6
- slot_project: bfloat16 [8, 768, 768], P('slot', 'dp'), may hold values from -0.078125 to 0.078125
- patch_prenorm: bfloat16 [768], P('dp'), may hold values from 0.5 to 1.5
- patch_heads: bfloat16 [768, 2304], P('dp'), may hold values from -0.21875 to 0.21875
- patch_mixer: bfloat16 [768, 768], P('dp'), may hold values from -0.875 to 0.875
- patch_midnorm: bfloat16 [768], P('dp'), may hold values from 0.5 to 1.5
- patch_expand: bfloat16 [768, 3072], P('dp'), may hold values from -0.21875 to 0.21875
- patch_reduce: bfloat16 [3072, 768], P('dp'), may hold values from -0.109375 to 0.109375
- byte_prenorm: bfloat16 [768], P('dp'), may hold values from 0.5 to 1.5
- byte_heads: bfloat16 [768, 2304], P('dp'), may hold values from -0.21875 to 0.21875
- byte_mixer: bfloat16 [768, 768], P('dp'), may hold values from -0.4375 to 0.4375
- byte_midnorm: bfloat16 [768], P('dp'), may hold values from 0.5 to 1.5
- byte_expand: bfloat16 [768, 3072], P('dp'), may hold values from -0.21875 to 0.21875
- byte_reduce: bfloat16 [3072, 768], P('dp'), may hold values from -0.109375 to 0.109375
- d_output: bfloat16 [1024, 8, 768], P(('dp', 'slot')), may hold values from -6 to 6
Outputs:
- out_bytes: bfloat16 [1024, 8, 768], P(('dp', 'slot'))
- embed_grad: float32 [256, 768], P('dp')
- project_grad: float32 [8, 768, 768], P('slot', 'dp')
- patch_prenorm_grad: float32 [768], P('dp')
- patch_heads_grad: float32 [768, 2304], P('dp')
- patch_mixer_grad: float32 [768, 768], P('dp')
- patch_midnorm_grad: float32 [768], P('dp')
- patch_expand_grad: float32 [768, 3072], P('dp')
- patch_reduce_grad: float32 [3072, 768], P('dp')
- byte_prenorm_grad: float32 [768], P('dp')
- byte_heads_grad: float32 [768, 2304], P('dp')
- byte_mixer_grad: float32 [768, 768], P('dp')
- byte_midnorm_grad: float32 [768], P('dp')
- byte_expand_grad: float32 [768, 3072], P('dp')
- byte_reduce_grad: float32 [3072, 768], P('dp')
The draws below stay inside these ranges and needn't reach their ends.
Inputs may be any that keep to these rules, and one draw needn't show every extreme that they name: `seg_ids`: in each row the numbers never fall; each of the 2 sequences covers 1 to 96 patches.
All inputs are finite; a program needn't handle non-finite values.
Results may differ from the reference program's by a relative error of at most 0.03.
Values may be sent and summed in bfloat16 or wider, within the bound.
A program may use at most 192 MiB of HBM per device.

```python
import math
import jax
import jax.numpy as jnp
import numpy as np
from jax import lax

D = 768
HEAD_DIM = 64
FF = 3072
PATCH = 8
VOCAB = 256
SEQS = 2
GROUP_PATCHES = 128
GROUPS = 8
PATCHES = 1024
SEQ_MOST = 96


def plant(entries, own_key, smallest, top_value):
    longest = entries.shape.index(max(entries.shape))
    spots = []
    for shift in (0, 1):
        where = [jax.random.randint(jax.random.fold_in(own_key, axis), (), 0, length) for axis, length in enumerate(entries.shape)]
        where[longest] = (where[longest] + shift) % entries.shape[longest]
        spots.append(tuple(where))
    return entries.at[spots[0]].set(smallest).at[spots[1]].set(top_value)


def steps_of(key, extent, shards, low, high):
    factor_of = 1.0
    for axis_at, shards_of in shards:
        draws = jax.random.uniform(jax.random.fold_in(jax.random.fold_in(key, 6), axis_at), (shards_of,), jnp.float32, low / len(shards), high / len(shards))
        factor_of = factor_of * jnp.repeat(jnp.exp(draws), extent[axis_at] // shards_of).reshape((-1,) + (1,) * (len(extent) - 1 - axis_at))
    return factor_of


def rank_bounds(amount, lean):
    weights = [(1 << 20) // math.isqrt(grade ** lean) + 1 for grade in range(1, amount + 1)]
    deviation = 1 + sum(weights) // (1 << 30)
    return np.cumsum(np.array([max(1, weight // deviation) for weight in weights]))


def ranked_ids(rng, extent, amount, lean):
    grid = rank_bounds(amount, lean)
    pick = jax.random.randint(jax.random.fold_in(rng, 1), extent, 0, int(grid[amount - 1]))
    grade = jnp.searchsorted(jnp.asarray(grid, jnp.int32), pick, side="right")
    return jax.random.permutation(jax.random.fold_in(rng, 2), amount)[grade].astype(jnp.int32)


def profile(count, total, bound, skew):
    loads = [(1 << 20) // math.isqrt(grade ** skew) + 1 for grade in range(2, count + 1)]
    rest, holding = total - bound - (count - 1), [1] * (count - 1)
    while rest > 0:
        free = [i for i in range(count - 1) if holding[i] < bound]
        pool, budget = sum([loads[i] for i in free]), rest
        for i in free:
            more = min(bound - holding[i], max(1, budget * loads[i] // pool), rest)
            holding[i] = holding[i] + more
            rest = rest - more
    return np.array([bound] + holding)


def uneven_parts(own_key, amount, total, most, slope):
    if amount == 2:
        one = jax.random.randint(own_key, (), max(1, total - most), min(most, total - 1) + 1)
        return jnp.stack([one, total - one])
    lengths = jnp.asarray(profile(amount, total, most, slope), jnp.int32)
    twos = (amount - 1) // 2
    donor, sink = lengths[1:1 + 2 * twos:2], lengths[2:2 + 2 * twos:2]
    room = jnp.minimum(donor - 1, most - sink)
    moved = jax.random.randint(jax.random.fold_in(own_key, 1), (twos,), 0, 1 << 20) % (room + 1)
    lengths = lengths.at[1:1 + 2 * twos:2].set(donor - moved).at[2:2 + 2 * twos:2].set(sink + moved)
    return lengths[jax.random.permutation(jax.random.fold_in(own_key, 2), amount)]


def normal_values(rng, extent, deviation, most, pieces=(), kind=jnp.bfloat16):
    array = deviation * jax.random.normal(rng, extent, jnp.float32)
    if pieces:
        array = array * steps_of(rng, extent, pieces, -0.22, 0.18)
    return jnp.clip(array, -most, most).astype(kind)


def setup_inputs(seed: int = 0) -> dict:
    key_list = jax.random.split(jax.random.key(seed), 18)
    byte_ids = plant(ranked_ids(key_list[0], (PATCHES, PATCH), VOCAB, 2), jax.random.fold_in(key_list[0], 3), 0, VOCAB - 1).astype(jnp.int32)
    seg_ids = jax.vmap(lambda own: jnp.searchsorted(jnp.cumsum(uneven_parts(own, SEQS, GROUP_PATCHES, SEQ_MOST, 2)), jnp.arange(GROUP_PATCHES), side="right"))(jax.random.split(key_list[1], GROUPS)).reshape((GROUPS, GROUP_PATCHES)).astype(jnp.int32)
    embed_table = normal_values(key_list[2], (VOCAB, D), 1.0, 6.0, ((0, 8),))
    slot_project = normal_values(key_list[3], (PATCH, D, D), (PATCH * D) ** -0.5, 0.078125, ((0, 4), (1, 8)))
    patch_prenorm = jnp.clip(1.0 + 0.1 * jax.random.normal(key_list[4], (D,), jnp.float32), 0.5, 1.5).astype(jnp.bfloat16)
    patch_heads = normal_values(key_list[5], (D, 3 * D), D ** -0.5, 0.21875, ((0, 8),))
    patch_mixer = normal_values(key_list[6], (D, D), (D // 16) ** -0.5, 0.875, ((0, 8),))
    patch_midnorm = jnp.clip(1.0 + 0.1 * jax.random.normal(key_list[7], (D,), jnp.float32), 0.5, 1.5).astype(jnp.bfloat16)
    patch_expand = normal_values(key_list[8], (D, FF), D ** -0.5, 0.21875, ((0, 8),))
    patch_reduce = normal_values(key_list[9], (FF, D), FF ** -0.5, 0.109375, ((0, 8),))
    byte_prenorm = jnp.clip(1.0 + 0.1 * jax.random.normal(key_list[10], (D,), jnp.float32), 0.5, 1.5).astype(jnp.bfloat16)
    byte_heads = normal_values(key_list[11], (D, 3 * D), D ** -0.5, 0.21875, ((0, 8),))
    byte_mixer = normal_values(key_list[12], (D, D), (D // 4) ** -0.5, 0.4375, ((0, 8),))
    byte_midnorm = jnp.clip(1.0 + 0.1 * jax.random.normal(key_list[13], (D,), jnp.float32), 0.5, 1.5).astype(jnp.bfloat16)
    byte_expand = normal_values(key_list[14], (D, FF), D ** -0.5, 0.21875, ((0, 8),))
    byte_reduce = normal_values(key_list[15], (FF, D), FF ** -0.5, 0.109375, ((0, 8),))
    d_output = normal_values(key_list[16], (PATCHES, PATCH, D), 1.0, 6.0, ((0, 32),))
    return dict(byte_ids=byte_ids, seg_ids=seg_ids, embed_table=embed_table, slot_project=slot_project, patch_prenorm=patch_prenorm, patch_heads=patch_heads, patch_mixer=patch_mixer, patch_midnorm=patch_midnorm, patch_expand=patch_expand, patch_reduce=patch_reduce, byte_prenorm=byte_prenorm, byte_heads=byte_heads, byte_mixer=byte_mixer, byte_midnorm=byte_midnorm, byte_expand=byte_expand, byte_reduce=byte_reduce, d_output=d_output)


EPSILON = 1e-05
MASKED = -1000000000.0
HIGHEST = lax.Precision.HIGHEST

@jax.custom_vjp
def low(v):
    return lax.optimization_barrier(v.astype(jnp.bfloat16)).astype(jnp.float32)

@jax.custom_vjp
def low_back(v):
    return v

def low_keep(v):
    return (low(v), None)

def low_pass(kept, grad):
    return (grad,)

def back_keep(v):
    return (v, None)

def back_low(kept, grad):
    return (low(grad),)
low.defvjp(low_keep, low_pass)
low_back.defvjp(back_keep, back_low)

def norm_rows(values, gain_vec):
    center = lax.optimization_barrier(jnp.mean(values, axis=-1, keepdims=True))
    shifted = values - center
    spread = lax.optimization_barrier(jnp.mean(shifted * shifted, axis=-1, keepdims=True))
    return shifted * lax.rsqrt(spread + EPSILON) * gain_vec

def gelu_tanh(values):
    inside = 0.7978845608028654 * (values + 0.044715 * values * values * values)
    return 0.5 * values * (1.0 + jnp.tanh(inside))

def block(values, weights, allowed):
    gain_one, w_heads, w_mixer, gain_two, w_expand, w_reduce = weights
    batch, row_count, width = values.shape
    head_count = width // HEAD_DIM
    norm_one = low(norm_rows(values, gain_one))
    joined = low(low_back(jnp.einsum('bnd,df->bnf', norm_one, w_heads, precision=HIGHEST)))
    joined = joined.reshape(batch, row_count, 3, head_count, HEAD_DIM)
    queries = joined[:, :, 0]
    keyset = joined[:, :, 1]
    valueset = joined[:, :, 2]
    scores = low_back(jnp.einsum('bnhe,bmhe->bhnm', queries, keyset, precision=HIGHEST) * HEAD_DIM ** (-0.5))
    scores = jnp.where(allowed[:, None], scores, MASKED)
    highest = lax.optimization_barrier(jnp.max(scores, axis=-1, keepdims=True))
    exponents = jnp.exp(scores - highest)
    softened = low(exponents / lax.optimization_barrier(jnp.sum(exponents, axis=-1, keepdims=True)))
    mixture = low(low_back(jnp.einsum('bhnm,bmhe->bnhe', softened, valueset, precision=HIGHEST)))
    mixture = mixture.reshape(batch, row_count, width)
    middle = values + low_back(jnp.einsum('bnf,fd->bnd', mixture, w_mixer, precision=HIGHEST))
    norm_two = low(norm_rows(middle, gain_two))
    expanded = low_back(jnp.einsum('bnd,df->bnf', norm_two, w_expand, precision=HIGHEST))
    hidden = low(gelu_tanh(expanded))
    return middle + low_back(jnp.einsum('bnf,fd->bnd', hidden, w_reduce, precision=HIGHEST))

def reference(byte_ids, seg_ids, embed_table, slot_project, patch_prenorm, patch_heads, patch_mixer, patch_midnorm, patch_expand, patch_reduce, byte_prenorm, byte_heads, byte_mixer, byte_midnorm, byte_expand, byte_reduce, d_output):
    floats = [item.astype(jnp.float32) for item in (embed_table, slot_project, patch_prenorm, patch_heads, patch_mixer, patch_midnorm, patch_expand, patch_reduce, byte_prenorm, byte_heads, byte_mixer, byte_midnorm, byte_expand, byte_reduce)]
    grouped_ids = byte_ids.reshape(GROUPS, GROUP_PATCHES, PATCH)

    def forward(lookup, project, *weights):
        patch_weights = weights[:6]
        byte_weights = weights[6:]

        def one_group(inputs):
            byte_rows, segments = inputs
            tokens = lookup[byte_rows]
            flattened = tokens.reshape(GROUP_PATCHES, PATCH * D)
            patch_start = low_back(jnp.dot(flattened, project.reshape(PATCH * D, D), precision=HIGHEST, preferred_element_type=jnp.float32))
            ordinal = jnp.arange(GROUP_PATCHES, dtype=jnp.int32)
            allowed = (ordinal[:, None] >= ordinal[None, :]) & (segments[:, None] == segments[None, :])
            patch_out = block(patch_start[None], patch_weights, allowed[None])[0]
            positions = jnp.arange(PATCH, dtype=jnp.int32)
            causal = (positions[:, None] >= positions[None, :])[None]
            return block(tokens + patch_out[:, None, :], byte_weights, causal)
        return lax.map(jax.checkpoint(one_group), (grouped_ids, seg_ids))
    results, pullback = jax.vjp(forward, *floats)
    gradients = pullback(d_output.astype(jnp.float32).reshape(GROUPS, GROUP_PATCHES, PATCH, D))
    out_bytes = results.reshape(PATCHES, PATCH, D).astype(jnp.bfloat16)
    return (out_bytes, gradients[0], gradients[1], gradients[2], gradients[3], gradients[4], gradients[5], gradients[6], gradients[7], gradients[8], gradients[9], gradients[10], gradients[11], gradients[12], gradients[13])
```

```python
import functools
import math
from types import SimpleNamespace as NS

import jax
import jax.numpy as jnp
from jax import lax
from jax.experimental import pallas as pl
from jax.experimental.pallas import tpu as pltpu
from jax.sharding import PartitionSpec as P

MESH = pl.DeviceIdType.MESH
BF = jnp.bfloat16
F32 = jnp.float32
DP, SLOT = "dp", "slot"
SHARED, PRIVATE, ZONLY, SINGLE = range(4)

HEAD_DIM = 64


EPSILON = 1e-05
MASKED = -1000000000.0


def norm_rows(values, gain_vec):
    center = jnp.mean(values, axis=-1, keepdims=True)
    shifted = values - center
    spread = jnp.mean(shifted * shifted, axis=-1, keepdims=True)
    return shifted * lax.rsqrt(spread + EPSILON) * gain_vec


def gelu_tanh(values):
    inside = 0.7978845608028654 * (values + 0.044715 * values * values * values)
    return 0.5 * values * (1.0 + jnp.tanh(inside))


def attention(queries, keyset, valueset, allowed):
    scores = jnp.einsum(
        "bnhe,bmhe->bhnm", queries, keyset, preferred_element_type=jnp.float32
    ) * HEAD_DIM ** (-0.5)
    scores = jnp.where(allowed[:, None], scores, MASKED)
    highest = jnp.max(scores, axis=-1, keepdims=True)
    exponents = jnp.exp(scores - highest)
    totals = jnp.sum(exponents, axis=-1, keepdims=True)
    softened = (exponents / totals).astype(jnp.bfloat16)
    mixture = jnp.einsum("bhnm,bmhe->bnhe", softened, valueset, preferred_element_type=jnp.float32)
    return (mixture, highest + jnp.log(totals))


def attention_back(queries, keyset, valueset, allowed, logsum, d_mixture):
    scale_value = HEAD_DIM ** (-0.5)
    scores = (
        jnp.einsum("bnhe,bmhe->bhnm", queries, keyset, preferred_element_type=jnp.float32)
        * scale_value
    )
    scores = jnp.where(allowed[:, None], scores, MASKED)
    softened = jnp.exp(scores - logsum)
    d_soft = jnp.einsum("bnhe,bmhe->bhnm", d_mixture, valueset, preferred_element_type=jnp.float32)
    inside = jnp.sum(d_soft * softened, axis=-1, keepdims=True)
    d_scores = (softened * (d_soft - inside)).astype(jnp.bfloat16)
    d_queries = (
        jnp.einsum("bhnm,bmhe->bnhe", d_scores, keyset, preferred_element_type=jnp.float32)
        * scale_value
    )
    d_keys = (
        jnp.einsum("bhnm,bnhe->bmhe", d_scores, queries, preferred_element_type=jnp.float32)
        * scale_value
    )
    d_values = jnp.einsum(
        "bhnm,bnhe->bmhe",
        softened.astype(jnp.bfloat16),
        d_mixture,
        preferred_element_type=jnp.float32,
    )
    return (d_queries, d_keys, d_values)


def block_forward(values, weights, attend):
    gain_one, w_heads, w_mixer, gain_two, w_expand, w_reduce = weights
    batch, row_count, width = values.shape
    head_count = width // HEAD_DIM
    norm_one, back_one = jax.vjp(norm_rows, values, gain_one.astype(jnp.float32))
    norm_one = norm_one.astype(jnp.bfloat16)
    joined = jnp.einsum(
        "bnd,df->bnf", norm_one, w_heads, preferred_element_type=jnp.float32
    ).astype(jnp.bfloat16)
    joined = joined.reshape(batch, row_count, 3, head_count, HEAD_DIM)
    mixture, kept = attend(joined[:, :, 0], joined[:, :, 1], joined[:, :, 2])
    mixture = mixture.astype(jnp.bfloat16).reshape(batch, row_count, width)
    middle = values + jnp.einsum(
        "bnf,fd->bnd", mixture, w_mixer, preferred_element_type=jnp.float32
    )
    norm_two, back_two = jax.vjp(norm_rows, middle, gain_two.astype(jnp.float32))
    norm_two = norm_two.astype(jnp.bfloat16)
    expanded = jnp.einsum("bnd,df->bnf", norm_two, w_expand, preferred_element_type=jnp.float32)
    hidden, back_gelu = jax.vjp(gelu_tanh, expanded)
    hidden = hidden.astype(jnp.bfloat16)
    result = middle + jnp.einsum(
        "bnf,fd->bnd", hidden, w_reduce, preferred_element_type=jnp.float32
    )
    saved = (back_one, norm_one, joined, kept, mixture, back_two, norm_two, back_gelu, hidden)
    return (result, saved)


def block_backward(grad_out, weights, saved, attend_back):
    gain_one, w_heads, w_mixer, gain_two, w_expand, w_reduce = weights
    back_one, norm_one, joined, kept, mixture, back_two, norm_two, back_gelu, hidden = saved
    batch, row_count, width = grad_out.shape
    grad_low = grad_out.astype(jnp.bfloat16)
    reduce_grad = jnp.einsum("bnf,bnd->fd", hidden, grad_low, preferred_element_type=jnp.float32)
    d_hidden = jnp.einsum("bnd,fd->bnf", grad_low, w_reduce, preferred_element_type=jnp.float32)
    (d_expanded,) = back_gelu(d_hidden)
    d_expanded = d_expanded.astype(jnp.bfloat16)
    expand_grad = jnp.einsum(
        "bnd,bnf->df", norm_two, d_expanded, preferred_element_type=jnp.float32
    )
    d_norm_two = jnp.einsum("bnf,df->bnd", d_expanded, w_expand, preferred_element_type=jnp.float32)
    d_middle_part, midnorm_grad = back_two(d_norm_two)
    d_middle = grad_out + d_middle_part
    middle_low = d_middle.astype(jnp.bfloat16)
    mixer_grad = jnp.einsum("bnf,bnd->fd", mixture, middle_low, preferred_element_type=jnp.float32)
    d_mixture = jnp.einsum(
        "bnd,fd->bnf", middle_low, w_mixer, preferred_element_type=jnp.float32
    ).astype(jnp.bfloat16)
    d_mixture = d_mixture.reshape(batch, row_count, width // HEAD_DIM, HEAD_DIM)
    d_queries, d_keys, d_values = attend_back(
        joined[:, :, 0], joined[:, :, 1], joined[:, :, 2], kept, d_mixture
    )
    d_joined = (
        jnp.stack([d_queries, d_keys, d_values], axis=2)
        .reshape(batch, row_count, 3 * width)
        .astype(jnp.bfloat16)
    )
    heads_grad = jnp.einsum("bnd,bnf->df", norm_one, d_joined, preferred_element_type=jnp.float32)
    d_norm_one = jnp.einsum("bnf,df->bnd", d_joined, w_heads, preferred_element_type=jnp.float32)
    d_input_part, prenorm_grad = back_one(d_norm_one)
    return (
        d_middle + d_input_part,
        (prenorm_grad, heads_grad, mixer_grad, midnorm_grad, expand_grad, reduce_grad),
    )


def generic_local(
    byte_ids,
    seg_ids,
    embed_table,
    slot_project,
    patch_prenorm,
    patch_heads,
    patch_mixer,
    patch_midnorm,
    patch_expand,
    patch_reduce,
    byte_prenorm,
    byte_heads,
    byte_mixer,
    byte_midnorm,
    byte_expand,
    byte_reduce,
    d_output,
):
    slot_count = lax.axis_size(SLOT)
    slot_index = lax.axis_index(SLOT)
    group_rows = byte_ids.shape[0]
    own_rows = group_rows // slot_count
    patch_len = byte_ids.shape[1]
    slot_share = patch_len // slot_count
    gathered = (
        lax.all_gather(embed_table, DP, axis=0, tiled=True),
        lax.all_gather(slot_project, DP, axis=1, tiled=True),
        lax.all_gather(patch_prenorm, DP, axis=0, tiled=True),
        lax.all_gather(patch_heads, DP, axis=0, tiled=True),
        lax.all_gather(patch_mixer, DP, axis=0, tiled=True),
        lax.all_gather(patch_midnorm, DP, axis=0, tiled=True),
        lax.all_gather(patch_expand, DP, axis=0, tiled=True),
        lax.all_gather(patch_reduce, DP, axis=0, tiled=True),
        lax.all_gather(byte_prenorm, DP, axis=0, tiled=True),
        lax.all_gather(byte_heads, DP, axis=0, tiled=True),
        lax.all_gather(byte_mixer, DP, axis=0, tiled=True),
        lax.all_gather(byte_midnorm, DP, axis=0, tiled=True),
        lax.all_gather(byte_expand, DP, axis=0, tiled=True),
        lax.all_gather(byte_reduce, DP, axis=0, tiled=True),
    )
    lookup = gathered[0]
    project = gathered[1]
    patch_weights = gathered[2:8]
    byte_weights = gathered[8:14]
    vocab_size = lookup.shape[0]
    width = lookup.shape[1]
    head_count = width // HEAD_DIM
    vocab_iota = jnp.arange(vocab_size, dtype=jnp.int32)
    slot_bytes = lax.dynamic_slice_in_dim(byte_ids, slot_index * slot_share, slot_share, 1)
    slot_onehot = (slot_bytes[:, :, None] == vocab_iota).astype(jnp.bfloat16)
    slot_embed = jnp.einsum(
        "gpv,vd->gpd", slot_onehot, lookup, preferred_element_type=jnp.float32
    ).astype(jnp.bfloat16)
    rows_embed = slot_embed
    patch_start = lax.psum_scatter(
        jnp.einsum("cpd,pde->ce", rows_embed, project, preferred_element_type=jnp.float32).astype(
            jnp.bfloat16
        ),
        SLOT,
        scatter_dimension=0,
        tiled=True,
    ).astype(jnp.float32)
    segments = seg_ids[0]
    first_row = slot_index * own_rows
    query_pos = first_row + jnp.arange(own_rows, dtype=jnp.int32)
    key_pos = jnp.arange(group_rows, dtype=jnp.int32)
    query_seg = lax.dynamic_slice_in_dim(segments, first_row, own_rows, 0)
    allowed_patch = (
        (query_pos[:, None] >= key_pos[None, :]) & (query_seg[:, None] == segments[None, :])
    )[None]

    def attend_patch(queries, keyset, valueset):
        all_keys, all_values = (
            lax.all_gather(keyset.reshape(own_rows, width), SLOT, axis=0, tiled=True),
            lax.all_gather(valueset.reshape(own_rows, width), SLOT, axis=0, tiled=True),
        )
        all_keys = all_keys.reshape(1, group_rows, head_count, HEAD_DIM)
        all_values = all_values.reshape(1, group_rows, head_count, HEAD_DIM)
        mixture, logsum = attention(queries, all_keys, all_values, allowed_patch)
        return (mixture, (all_keys, all_values, logsum))

    def attend_patch_back(queries, keyset, valueset, kept, d_mixture):
        all_keys, all_values, logsum = kept
        d_queries, d_keys, d_values = attention_back(
            queries, all_keys, all_values, allowed_patch, logsum, d_mixture
        )
        own_keys, own_values = (
            lax.psum_scatter(
                d_keys.reshape(group_rows, width).astype(jnp.bfloat16),
                SLOT,
                scatter_dimension=0,
                tiled=True,
            ).astype(jnp.float32),
            lax.psum_scatter(
                d_values.reshape(group_rows, width).astype(jnp.bfloat16),
                SLOT,
                scatter_dimension=0,
                tiled=True,
            ).astype(jnp.float32),
        )
        return (d_queries, own_keys.reshape(keyset.shape), own_values.reshape(valueset.shape))

    patch_out, patch_saved = block_forward(patch_start[None], patch_weights, attend_patch)
    local_bytes = lax.dynamic_slice_in_dim(byte_ids, first_row, own_rows, 0)
    local_onehot = (local_bytes[:, :, None] == vocab_iota).astype(jnp.bfloat16)
    local_embed = jnp.einsum(
        "rpv,vd->rpd", local_onehot, lookup, preferred_element_type=jnp.float32
    )
    fine_input = local_embed + patch_out[0][:, None, :]
    tile_len = math.gcd(own_rows * patch_len, 128)
    tile_count = own_rows * patch_len // tile_len
    fine_input = fine_input.reshape(tile_count, tile_len, width)
    positions = jnp.arange(tile_len, dtype=jnp.int32)
    allowed_byte = (
        (positions[:, None] >= positions[None, :])
        & (positions[:, None] // patch_len == positions[None, :] // patch_len)
    )[None]

    def attend_byte(queries, keyset, valueset):
        return attention(queries, keyset, valueset, allowed_byte)

    def attend_byte_back(queries, keyset, valueset, kept, d_mixture):
        return attention_back(queries, keyset, valueset, allowed_byte, kept, d_mixture)

    byte_out, byte_saved = block_forward(fine_input, byte_weights, attend_byte)
    out_bytes = byte_out.reshape(own_rows, patch_len, width).astype(jnp.bfloat16)
    d_fine, byte_grads = block_backward(
        d_output.astype(jnp.float32).reshape(tile_count, tile_len, width),
        byte_weights,
        byte_saved,
        attend_byte_back,
    )
    d_fine = d_fine.reshape(own_rows, patch_len, width)
    d_patch = jnp.sum(d_fine, axis=1)[None]
    d_start, patch_grads = block_backward(d_patch, patch_weights, patch_saved, attend_patch_back)
    embed_local = jnp.einsum(
        "rpv,rpd->vd", local_onehot.astype(jnp.float32), d_fine, precision=lax.Precision.HIGHEST
    )
    portion = lax.all_gather(d_start[0].astype(jnp.bfloat16), SLOT, axis=0, tiled=True)
    rows_embed = slot_embed
    rows_hot = slot_onehot.astype(jnp.float32)
    proj_sum = jnp.einsum("cpd,ce->pde", rows_embed, portion, preferred_element_type=jnp.float32)
    d_rows = jnp.einsum("ce,pde->cpd", portion, project, preferred_element_type=jnp.float32)
    table_sum = jnp.einsum("cpv,cpd->vd", rows_hot, d_rows, precision=lax.Precision.HIGHEST)
    table_grad = embed_local + table_sum
    patch_pre, patch_qkv_grad, patch_mix, patch_mid, patch_exp, patch_red = patch_grads
    byte_pre, byte_qkv_grad, byte_mix, byte_mid, byte_exp, byte_red = byte_grads
    reduced = (
        lax.psum_scatter(table_grad, DP, scatter_dimension=0, tiled=True),
        lax.psum_scatter(patch_pre, DP, scatter_dimension=0, tiled=True),
        lax.psum_scatter(patch_qkv_grad, DP, scatter_dimension=0, tiled=True),
        lax.psum_scatter(patch_mix, DP, scatter_dimension=0, tiled=True),
        lax.psum_scatter(patch_mid, DP, scatter_dimension=0, tiled=True),
        lax.psum_scatter(patch_exp, DP, scatter_dimension=0, tiled=True),
        lax.psum_scatter(patch_red, DP, scatter_dimension=0, tiled=True),
        lax.psum_scatter(byte_pre, DP, scatter_dimension=0, tiled=True),
        lax.psum_scatter(byte_qkv_grad, DP, scatter_dimension=0, tiled=True),
        lax.psum_scatter(byte_mix, DP, scatter_dimension=0, tiled=True),
        lax.psum_scatter(byte_mid, DP, scatter_dimension=0, tiled=True),
        lax.psum_scatter(byte_exp, DP, scatter_dimension=0, tiled=True),
        lax.psum_scatter(byte_red, DP, scatter_dimension=0, tiled=True),
        lax.psum_scatter(proj_sum, DP, scatter_dimension=1, tiled=True),
    )
    shares = (
        lax.psum_scatter(
            reduced[0].astype(jnp.bfloat16), SLOT, scatter_dimension=0, tiled=True
        ).astype(jnp.float32),
        lax.psum_scatter(
            reduced[1].astype(jnp.bfloat16), SLOT, scatter_dimension=0, tiled=True
        ).astype(jnp.float32),
        lax.psum_scatter(
            reduced[2].astype(jnp.bfloat16), SLOT, scatter_dimension=0, tiled=True
        ).astype(jnp.float32),
        lax.psum_scatter(
            reduced[3].astype(jnp.bfloat16), SLOT, scatter_dimension=0, tiled=True
        ).astype(jnp.float32),
        lax.psum_scatter(
            reduced[4].astype(jnp.bfloat16), SLOT, scatter_dimension=0, tiled=True
        ).astype(jnp.float32),
        lax.psum_scatter(
            reduced[5].astype(jnp.bfloat16), SLOT, scatter_dimension=0, tiled=True
        ).astype(jnp.float32),
        lax.psum_scatter(
            reduced[6].astype(jnp.bfloat16), SLOT, scatter_dimension=0, tiled=True
        ).astype(jnp.float32),
        lax.psum_scatter(
            reduced[7].astype(jnp.bfloat16), SLOT, scatter_dimension=0, tiled=True
        ).astype(jnp.float32),
        lax.psum_scatter(
            reduced[8].astype(jnp.bfloat16), SLOT, scatter_dimension=0, tiled=True
        ).astype(jnp.float32),
        lax.psum_scatter(
            reduced[9].astype(jnp.bfloat16), SLOT, scatter_dimension=0, tiled=True
        ).astype(jnp.float32),
        lax.psum_scatter(
            reduced[10].astype(jnp.bfloat16), SLOT, scatter_dimension=0, tiled=True
        ).astype(jnp.float32),
        lax.psum_scatter(
            reduced[11].astype(jnp.bfloat16), SLOT, scatter_dimension=0, tiled=True
        ).astype(jnp.float32),
        lax.psum_scatter(
            reduced[12].astype(jnp.bfloat16), SLOT, scatter_dimension=0, tiled=True
        ).astype(jnp.float32),
    )
    summed = (
        lax.all_gather(shares[0].astype(jnp.bfloat16), SLOT, axis=0, tiled=True).astype(
            jnp.float32
        ),
        lax.all_gather(shares[1].astype(jnp.bfloat16), SLOT, axis=0, tiled=True).astype(
            jnp.float32
        ),
        lax.all_gather(shares[2].astype(jnp.bfloat16), SLOT, axis=0, tiled=True).astype(
            jnp.float32
        ),
        lax.all_gather(shares[3].astype(jnp.bfloat16), SLOT, axis=0, tiled=True).astype(
            jnp.float32
        ),
        lax.all_gather(shares[4].astype(jnp.bfloat16), SLOT, axis=0, tiled=True).astype(
            jnp.float32
        ),
        lax.all_gather(shares[5].astype(jnp.bfloat16), SLOT, axis=0, tiled=True).astype(
            jnp.float32
        ),
        lax.all_gather(shares[6].astype(jnp.bfloat16), SLOT, axis=0, tiled=True).astype(
            jnp.float32
        ),
        lax.all_gather(shares[7].astype(jnp.bfloat16), SLOT, axis=0, tiled=True).astype(
            jnp.float32
        ),
        lax.all_gather(shares[8].astype(jnp.bfloat16), SLOT, axis=0, tiled=True).astype(
            jnp.float32
        ),
        lax.all_gather(shares[9].astype(jnp.bfloat16), SLOT, axis=0, tiled=True).astype(
            jnp.float32
        ),
        lax.all_gather(shares[10].astype(jnp.bfloat16), SLOT, axis=0, tiled=True).astype(
            jnp.float32
        ),
        lax.all_gather(shares[11].astype(jnp.bfloat16), SLOT, axis=0, tiled=True).astype(
            jnp.float32
        ),
        lax.all_gather(shares[12].astype(jnp.bfloat16), SLOT, axis=0, tiled=True).astype(
            jnp.float32
        ),
    )
    proj_final = reduced[13]
    return (
        out_bytes,
        summed[0],
        proj_final,
        summed[1],
        summed[2],
        summed[3],
        summed[4],
        summed[5],
        summed[6],
        summed[7],
        summed[8],
        summed[9],
        summed[10],
        summed[11],
        summed[12],
    )


def generic_solution(mesh):
    placed = (
        P(DP, None),
        P(DP, None),
        P(DP, None),
        P(SLOT, DP, None),
        P(DP),
        P(DP, None),
        P(DP, None),
        P(DP),
        P(DP, None),
        P(DP, None),
        P(DP),
        P(DP, None),
        P(DP, None),
        P(DP),
        P(DP, None),
        P(DP, None),
        P((DP, SLOT), None, None),
    )
    return jax.shard_map(
        generic_local,
        mesh=mesh,
        in_specs=placed,
        out_specs=(
            P((DP, SLOT), None, None),
            P(DP, None),
            P(SLOT, DP, None),
            P(DP),
            P(DP, None),
            P(DP, None),
            P(DP),
            P(DP, None),
            P(DP, None),
            P(DP),
            P(DP, None),
            P(DP, None),
            P(DP),
            P(DP, None),
            P(DP, None),
        ),
        check_vma=False,
    )


W, SP = 4, 2
XD = 3 * SP
YD = XD + SP


class Gather:
    def __init__(self, chunks, sems):
        self.ch = chunks
        self.s = sems
        dp = lax.axis_index(DP); slot = lax.axis_index(SLOT)
        self.dp, self.slot = dp, slot
        self.z, self.x = dp // 2, dp % 2
        self.y, self.c = slot // 2, slot % 2
        self.xdev = (self.z * 2 + 1 - self.x, slot)
        self.ydev = (dp, (1 - self.y) * 2 + self.c)
        self.cdev = (dp, self.y * 2 + 1 - self.c)
        self.sent = []
    def zdev(self, d): return ((self.z + d) * 2 + self.x, self.slot)
    def barrier_peers(self):
        z = self.z
        return [(None, self.xdev), (None, self.ydev), (None, self.cdev), (z > 0, self.zdev(-1)), (z < 3, self.zdev(1))]
    def cp(self, src, dst, ss, rs, dev):
        return pltpu.make_async_remote_copy(src_ref=src, dst_ref=dst, send_sem=ss, recv_sem=rs, device_id=dev, device_id_type=MESH)
    def send(self, pred, *a):
        if pred is None: self.cp(*a).start()
        else:
            @pl.when(pred)
            def _(): self.cp(*a).start()
    def reg(self, t, oz, ox, y, c):
        k = self.ch[t]
        return k.dst(oz, ox, y, c)
    def start(self, t):
        k = self.ch[t]; z, x, y, c = self.z, self.x, self.y, self.c
        zs, zr, xs, xr = self.s.zs, self.s.zr, self.s.xs, self.s.xr
        src = k.src(y, c); dst = self.reg(t, z, x, y, c)
        one = k.kind == SINGLE
        mine = z == self.slot
        self.send((z < 3) & mine if one else z < 3, src, dst, zs.at[t, 0, z], zr.at[t, z], self.zdev(1))
        self.send((z > 0) & mine if one else z > 0, src, dst, zs.at[t, 1, z], zr.at[t, z], self.zdev(-1))
        if k.kind != ZONLY:
            self.send(mine if one else None, src, dst, xs.at[t, 0], xr.at[t, 0], self.xdev)
    def wait(self, ref, rs, ss):
        self.cp(ref, ref, ss, rs, (self.dp, self.slot)).wait_recv()
    def zarr(self, t, d):
        k = self.ch[t]; z, x, y, c = self.z, self.x, self.y, self.c; S = self.s
        for side in (-1, 1):
            oz = z + side * d
            ok = oz == self.slot if k.kind == SINGLE else (oz >= 0) & (oz <= 3)
            nxt = -side
            nok = (z + nxt >= 0) & (z + nxt <= 3)
            @pl.when(ok)
            def _():
                r = self.reg(t, oz, x, y, c)
                self.wait(r, S.zr.at[t, oz], S.zs.at[t, 0, z])
                if d < 3:
                    @pl.when(nok)
                    def _(): self.cp(r, r, S.zs.at[t, 0 if nxt == 1 else 1, oz], S.zr.at[t, oz], self.zdev(nxt)).start()
                if k.kind != ZONLY:
                    self.cp(r, r, S.xs.at[t, 0], S.xr.at[t, 0], self.xdev).start()
                if k.kind == SHARED:
                    q = k.pos
                    self.cp(r, r, S.ys.at[q, 0], S.yr.at[q, 0], self.ydev).start()
    def xarr(self, t):
        k = self.ch[t]; x, y, c = self.x, self.y, self.c; S = self.s
        if k.kind == ZONLY: return
        r = k.xall(1 - x, y, c)
        self.wait(r, S.xr.at[t, 0], S.xs.at[t, 0])
        if k.kind == SHARED:
            q = k.pos
            self.cp(r, r, S.ys.at[q, 1], S.yr.at[q, 1], self.ydev).start()
            r = k.all(y, c)
            self.cp(r, r, S.cs.at[q, 0], S.cr.at[q, 0], self.cdev).start()
    def yarr(self, t):
        k = self.ch[t]; x, y, c = self.x, self.y, self.c; S = self.s
        if k.kind != SHARED: return
        q = k.pos
        self.wait(k.three(1 - y, c), S.yr.at[q, 0], S.ys.at[q, 0])
        self.wait(k.xall(1 - x, 1 - y, c), S.yr.at[q, 1], S.ys.at[q, 1])
        r = k.all(1 - y, c)
        self.cp(r, r, S.cs.at[q, 1], S.cr.at[q, 1], self.cdev).start()
    def finish(self, t):
        k = self.ch[t]; y, c = self.y, self.c; S = self.s
        if k.kind != SHARED: return
        q = k.pos
        for h in (0, 1):
            self.wait(k.all(y if h == 0 else 1 - y, 1 - c), S.cr.at[q, h], S.cs.at[q, h])
    def drain(self, t):
        k = self.ch[t]; z, x, y, c = self.z, self.x, self.y, self.c; S = self.s
        r = self.reg(t, z, x, y, c)
        def ws(ss, r): self.cp(r, r, ss, ss, (self.dp, self.slot)).wait_send()
        if k.kind == SINGLE:
            @pl.when((z < 3) & (self.slot <= z))
            def _(): ws(S.zs.at[t, 0, self.slot], r)
            @pl.when((z > 0) & (self.slot >= z))
            def _(): ws(S.zs.at[t, 1, self.slot], r)
        else:
            for i in range(4):
                @pl.when((z < 3) & (i <= z))
                def _(): ws(S.zs.at[t, 0, i], r)
                @pl.when((z > 0) & (i >= z))
                def _(): ws(S.zs.at[t, 1, i], r)
        if k.kind != ZONLY: ws(S.xs.at[t, 0], k.xall(x, y, c))
        if k.kind == SHARED:
            q = k.pos
            ws(S.ys.at[q, 0], k.three(y, c)); ws(S.ys.at[q, 1], k.xall(1 - x, y, c))
            for h in (0, 1): ws(S.cs.at[q, h], k.all(y, c))
    def steps(self):
        n = len(self.ch)
        for t in range(min(W, n)): self.start(t)
        yield
        for i in range(n + YD):
            for d in (1, 2, 3):
                t = i - SP * (d - 1)
                if 0 <= t < n: self.zarr(t, d)
            if i + W < n: self.start(i + W)
            t = i - XD
            if 0 <= t < n: self.xarr(t)
            t = i - YD
            if 0 <= t < n: self.yarr(t)
            yield
        for t in range(n): self.finish(t)
        yield
        for t in range(n): self.drain(t)


def gather_sems(plan, count):
    T = len(plan)
    Q = max(1, sum(p[1] == SHARED for p in plan))
    D = pltpu.SemaphoreType.DMA
    return [D((T, 2, 4)), D((T, 4)), D((T, 1)), D((T, 1)), D((Q, 2)), D((Q, 2)), D((Q, 2)), D((Q, 2)), D((count,))]


def gather_chunks(plan, ins, outs):
    chunks = []
    pos = 0
    for (a, kind, j, c0, cw) in plan:
        i, o = ins[a], outs[a]
        if kind == SHARED:
            col = pl.ds(c0, cw)
            src = lambda y, c, i=i, j=j, col=col: i.at[j, y, c, :, col]
            dst = lambda oz, ox, y, c, o=o, j=j, col=col: o.at[oz, ox, j, y, c, :, col]
            xall = lambda ox, y, c, o=o, j=j, col=col: o.at[:, ox, j, y, c, :, col]
            al = lambda y, c, o=o, j=j, col=col: o.at[:, :, j, y, c, :, col]
            three = lambda y, c, o=o, j=j, col=col: o.at[pl.ds(0, 3), 0, j, y, c, :, col]
            chunks.append(NS(kind=kind, src=src, dst=dst, pos=pos, xall=xall, all=al, three=three))
            pos += 1
            continue
        src = lambda y, c, i=i, j=j: i.at[j]
        if kind == PRIVATE:
            dst = lambda oz, ox, y, c, o=o, j=j: o.at[j, oz, ox]
            xall = lambda ox, y, c, o=o, j=j: o.at[j, :, ox]
        elif kind == ZONLY:
            dst = lambda oz, ox, y, c, o=o, j=j: o.at[j, oz]
            xall = None
        else:
            dst = lambda oz, ox, y, c, o=o, j=j: o.at[j, ox]
            xall = lambda ox, y, c, o=o, j=j: o.at[j, ox]
        chunks.append(NS(kind=kind, src=src, dst=dst, xall=xall))
    return chunks


def gather_kernel(plan, nin, *refs):
    ins = refs[:nin]
    outs = refs[nin : 2 * nin]
    bounce = refs[2 * nin : 3 * nin]
    zs, zr, xs, xr, ys, yr, cs, cr, ls = refs[3 * nin :]
    sems = NS(zs=zs, zr=zr, xs=xs, xr=xr, ys=ys, yr=yr, cs=cs, cr=cr, ls=ls)
    g = Gather(gather_chunks(plan, ins, outs), sems)
    bar = pltpu.get_barrier_semaphore()
    for pred, dev in g.barrier_peers():
        def sig(dev=dev): pl.semaphore_signal(bar, inc=1, device_id=dev, device_id_type=MESH)
        if pred is None: sig()
        else: pl.when(pred)(sig)
    inner = (g.z > 0) & (g.z < 3)
    @pl.when(inner)
    def _(): pl.semaphore_wait(bar, 5)
    @pl.when(jnp.logical_not(inner))
    def _(): pl.semaphore_wait(bar, 4)
    st = g.steps()
    next(st)
    kinds = {p[0]: p[1] for p in plan}
    def inside(a):
        i = ins[a].at[:, :, g.c] if kinds[a] == SHARED else ins[a]
        return pltpu.make_async_copy(i, bounce[a], sems.ls.at[a])
    def outside(a):
        o, kind = outs[a], kinds[a]
        if kind == SHARED: o = o.at[g.z, g.x, :, :, g.c]
        elif kind == PRIVATE: o = o.at[:, g.z, g.x]
        elif kind == ZONLY: o = o.at[:, g.z]
        else: o = o.at[:, g.x]
        return pltpu.make_async_copy(bounce[a], o, sems.ls.at[a])
    def each(fn):
        for a in range(nin):
            if kinds[a] == SINGLE:
                @pl.when(g.z == g.slot)
                def _(): fn(a)
            else: fn(a)
    each(lambda a: inside(a).start())
    def turn(a):
        inside(a).wait()
        outside(a).start()
    each(turn)
    next(st)
    each(lambda a: outside(a).wait())
    for _ in st: pass


def gather_all(arrs, kinds, plan, cid, name):
    outs = []
    bounce = []
    for a, k in zip(arrs, kinds):
        bounce.append(pltpu.VMEM(a.shape[:2] + a.shape[3:] if k == SHARED else a.shape, a.dtype))
        if k == SHARED: s = (4, 2) + a.shape
        elif k == PRIVATE: s = (a.shape[0], 4, 2) + a.shape[1:]
        elif k == ZONLY: s = (a.shape[0], 4) + a.shape[1:]
        else: s = (a.shape[0], 2) + a.shape[1:]
        outs.append(jax.ShapeDtypeStruct(s, a.dtype))
    hbm = pl.BlockSpec(memory_space=pl.ANY)
    return pl.pallas_call(
        functools.partial(gather_kernel, plan, len(arrs)),
        out_shape=outs,
        in_specs=[hbm] * len(arrs),
        out_specs=[hbm] * len(outs),
        scratch_shapes=bounce + gather_sems(plan, len(arrs)),
        compiler_params=pltpu.CompilerParams(collective_id=cid, has_side_effects=True, vmem_limit_bytes=40 * 2**20),
        name=name,
    )(*arrs)


DIM = 768
SPR = 2


class Reduce:
    def __init__(self, chunks):
        self.ch = chunks
        dp = lax.axis_index(DP); slot = lax.axis_index(SLOT)
        self.dp, self.slot = dp, slot
        self.z, self.x = dp // 2, dp % 2
        self.y, self.c = slot // 2, slot % 2
        self.xdev = (self.z * 2 + 1 - self.x, slot)
        self.ydev = (dp, (1 - self.y) * 2 + self.c)
        self.cdev = (dp, self.y * 2 + 1 - self.c)
        self.ycdev = (dp, (1 - self.y) * 2 + 1 - self.c)
    def zdev(self, k): return (((self.z + k) % 4) * 2 + self.x, self.slot)
    def peers(self): return [self.xdev, self.ydev, self.cdev, self.ycdev, self.zdev(1), self.zdev(2), self.zdev(3)]
    def cp(self, src, dst, sems, i, dev):
        return pltpu.make_async_remote_copy(src_ref=src, dst_ref=dst, send_sem=sems[0].at[i], recv_sem=sems[1].at[i], device_id=dev, device_id_type=MESH)
    def ccopy(self, k): return self.cp(k.g(1 - self.c), k.rc, k.sem, 0, self.cdev)
    def load(self, k): return pltpu.make_async_copy(k.g(self.c) if k.kind == SHARED else k.g, k.own, k.lsem.at[0])
    def ycopy(self, k): return self.cp(k.own.at[:, :, 1 - self.y], k.ry, k.sem, 1, self.ydev)
    def cur(self, k, oz, ox):
        return k.own.at[oz, ox, self.y] if k.kind == SHARED else k.own.at[oz, ox]
    def xcopy(self, k):
        src = k.own.at[:, 1 - self.x, self.y] if k.kind == SHARED else k.own.at[:, 1 - self.x]
        return self.cp(src, k.rx, k.sem, 2, self.xdev)
    def zcopy(self, k, d):
        return self.cp(self.cur(k, (self.z + d) % 4, self.x), k.rz.at[d - 1], k.sem, 2 + d, self.zdev(d))
    def fcopy(self, k, i):
        y, c = self.y, self.c
        if i == 0: return self.cp(k.fin, k.out(y, c), k.sem, 6, self.ydev)
        if i == 1: return self.cp(k.fin, k.out(y, c), k.sem, 7, self.cdev)
        return self.cp(k.out(1 - y, c), k.out(1 - y, c), k.sem, 8, self.cdev)
    def put(self, k): return pltpu.make_async_copy(k.fin, k.out(self.y, self.c), k.lsem.at[1])
    def s0(self, k):
        self.load(k).start()
        if k.kind == SHARED: self.ccopy(k).start()
    def s1(self, k):
        self.load(k).wait()
        if k.kind != SHARED: return
        self.ccopy(k).wait_recv()
        own, rc = k.own, k.rc
        @pl.loop(0, 4)
        def _(i):
            own[i] = own[i] + rc[i]
        self.ycopy(k).start()
    def s2(self, k):
        if k.kind == SHARED:
            self.ycopy(k).wait_recv()
            own, ry = k.own, k.ry
            @pl.loop(0, 4)
            def _(i):
                own[i, :, self.y] = own[i, :, self.y] + ry[i]
        self.xcopy(k).start()
    def s3(self, k):
        self.xcopy(k).wait_recv()
        rx = k.rx
        @pl.loop(0, 4)
        def _(i):
            r = self.cur(k, i, self.x)
            r[...] = r[...] + rx[i]
        for d in (1, 3, 2): self.zcopy(k, d).start()
    def s4(self, k):
        for d in (1, 3, 2): self.zcopy(k, d).wait_recv()
        rz = k.rz; f = jnp.float32
        k.fin[...] = (self.cur(k, self.z, self.x)[...].astype(f) + rz[0].astype(f) + rz[1].astype(f) + rz[2].astype(f)).astype(jnp.bfloat16)
        self.put(k).start()
        self.fcopy(k, 0).start(); self.fcopy(k, 1).start()
    def s5(self, k):
        self.fcopy(k, 0).wait_recv()
        self.fcopy(k, 2).start()
    def s6(self, k):
        self.fcopy(k, 1).wait_recv(); self.fcopy(k, 2).wait_recv()
        if k.kind == SHARED: self.ccopy(k).wait_send(); self.ycopy(k).wait_send()
        self.xcopy(k).wait_send()
        for d in (1, 2, 3): self.zcopy(k, d).wait_send()
        for i in range(3): self.fcopy(k, i).wait_send()
        self.put(k).wait()
    def steps(self):
        n = len(self.ch)
        for k in self.ch: self.s0(k)
        yield
        st = [self.s1, self.s2, self.s3, self.s4, self.s5]
        for i in range(n + SPR * 4):
            for q, fn in enumerate(st):
                t = i - SPR * q
                if 0 <= t < n: fn(self.ch[t])
            yield
        for k in self.ch: self.s6(k)

class Mixer:
    def __init__(self, r, g, own, rx, rz, fin, out, ss, rs, ls):
        self.r, self.g, self.own, self.rx, self.rz, self.fin, self.out, self.ss, self.rs, self.ls = r, g, own, rx, rz, fin, out, ss, rs, ls
    def xc(self):
        r = self.r
        return r.cp(self.own.at[1 - r.x], self.rx, (self.ss, self.rs), 0, r.xdev)
    def zc(self, d):
        r = self.r
        return r.cp(self.own.at[r.x], self.rz.at[d - 1], (self.ss, self.rs), d, (r.slot * 2 + r.x, r.slot))
    def bc(self, i):
        r = self.r
        return r.cp(self.fin, self.out, (self.ss, self.rs), 4 + i, (r.ydev, r.cdev, r.ycdev)[i])
    def steps(self):
        r = self.r
        ld = pltpu.make_async_copy(self.g, self.own, self.ls.at[0])
        ld.start(); ld.wait()
        self.xc().start(); yield
        self.xc().wait_recv()
        self.own[r.x] = self.own[r.x] + self.rx[...]
        for d in (1, 2, 3):
            @pl.when((r.z + d) % 4 == r.slot)
            def _(): self.zc(d).start()
        yield; yield; yield
        put = pltpu.make_async_copy(self.fin, self.out, self.ls.at[1])
        @pl.when(r.z == r.slot)
        def _():
            f = jnp.float32
            for d in (1, 2, 3): self.zc(d).wait_recv()
            self.fin[...] = (self.own[r.x].astype(f) + self.rz[0].astype(f) + self.rz[1].astype(f) + self.rz[2].astype(f)).astype(jnp.bfloat16)
            put.start()
            for i in range(3): self.bc(i).start()
        yield; yield
        self.xc().wait_send()
        for d in (1, 2, 3):
            @pl.when((r.z + d) % 4 == r.slot)
            def _(): self.zc(d).wait_send()
        @pl.when(r.z == r.slot)
        def _():
            for i in range(3): self.bc(i).wait_send()
            put.wait()
        for i, s in enumerate((r.ydev[1], r.cdev[1], r.ycdev[1])):
            @pl.when(r.z == s)
            def _(): self.bc(i).wait_recv()

def reduce_kernel(plan, nin, *refs):
    ins = refs[:nin]; outs = refs[nin:2 * nin]; rest = list(refs[2 * nin:])
    ns = sum(p[1] == SHARED for p in plan); npv = len(plan) - ns
    take = lambda: rest.pop(0)
    s_own, s_rc, s_ry, s_rx, s_rz, s_fin = (take() for _ in range(6))
    pv = [[take() for _ in range(4)] for _ in range(npv)]
    m_own, m_rx, m_rz, m_fin = (take() for _ in range(4))
    ss, rs, ls, mss, mrs, mls = (take() for _ in range(6))
    chunks = []; a = b = 0
    for t, (i, kind, j, cb) in enumerate(plan):
        g, o = ins[i], outs[i]
        if kind == SHARED:
            col = pl.ds(cb * DIM, DIM)
            chunks.append(NS(kind=kind, g=lambda c, g=g, j=j, col=col: g.at[:, :, j, :, c, :, col], out=lambda y, c, o=o, j=j, col=col: o.at[j, y, c, :, col],
                               own=s_own.at[a], rc=s_rc.at[a], ry=s_ry.at[a], rx=s_rx.at[a], rz=s_rz.at[a], fin=s_fin.at[a]))
            a += 1
        else:
            p = pv[b]; b += 1
            chunks.append(NS(kind=kind, g=g.at[j], out=lambda y, c, o=o, j=j: o.at[j, y, c], own=p[0], rx=p[1], rz=p[2], fin=p[3]))
        chunks[-1].sem = (ss.at[t], rs.at[t]); chunks[-1].lsem = ls.at[t]
    r = Reduce(chunks)
    bar = pltpu.get_barrier_semaphore()
    for dev in r.peers(): pl.semaphore_signal(bar, inc=1, device_id=dev, device_id_type=MESH)
    pl.semaphore_wait(bar, 7)
    m = Mixer(r, ins[-1], m_own, m_rx, m_rz, m_fin, outs[-1], mss, mrs, mls)
    g1, g2 = r.steps(), m.steps()
    while True:
        e1 = next(g1, 0); e2 = next(g2, 0)
        if e1 == 0 and e2 == 0: break

def reduce_all(arrs, kinds, plan, mixer):
    outs = []
    for a, k in zip(arrs, kinds):
        outs.append(jax.ShapeDtypeStruct(a.shape[2:] if k == SHARED else (a.shape[0], 2, 2) + a.shape[3:], a.dtype))
    outs.append(jax.ShapeDtypeStruct(mixer.shape[1:], mixer.dtype))
    D = pltpu.SemaphoreType.DMA
    B = jnp.bfloat16
    ns = sum(p[1] == SHARED for p in plan)
    u = 24
    V = lambda *s: pltpu.VMEM(s, B)
    scr = [V(ns, 4, 2, 2, u, DIM), V(ns, 4, 2, 2, u, DIM), V(ns, 4, 2, u, DIM), V(ns, 4, u, DIM), V(ns, 3, u, DIM), V(ns, u, DIM)]
    for (i, k, j, cb) in plan:
        if k != SHARED:
            r, C = arrs[i].shape[3:]
            scr += [V(4, 2, r, C), V(4, r, C), V(3, r, C), V(r, C)]
    r, C = mixer.shape[1:]
    scr += [V(2, r, C), V(r, C), V(3, r, C), V(r, C)]
    T = len(plan)
    scr += [D((T, 9)), D((T, 9)), D((T, 2)), D((7,)), D((7,)), D((2,))]
    al = list(arrs) + [mixer]
    return pl.pallas_call(
        functools.partial(reduce_kernel, plan, len(al)), out_shape=outs,
        in_specs=[pl.BlockSpec(memory_space=pl.ANY)] * len(al),
        out_specs=[pl.BlockSpec(memory_space=pl.ANY)] * len(outs),
        scratch_shapes=scr,
        compiler_params=pltpu.CompilerParams(collective_id=1, has_side_effects=True, vmem_limit_bytes=60 * 2**20),
        name="reduce_grads",
    )(*al)


def sum_kernel(with_x, p_ref, o_ref, rx, s0, rc, s1, ry, fin, rf, ss, rs):
    dp = lax.axis_index(DP)
    slot = lax.axis_index(SLOT)
    z, x, y, c = dp // 2, dp % 2, slot // 2, slot % 2
    xdev = (z * 2 + 1 - x, slot)
    ydev = (dp, (1 - y) * 2 + c)
    cdev = (dp, y * 2 + 1 - c)
    peers = [ydev, cdev] + ([xdev] if with_x else [])
    bar = pltpu.get_barrier_semaphore()
    for d in peers:
        pl.semaphore_signal(bar, inc=1, device_id=d, device_id_type=MESH)
    pl.semaphore_wait(bar, len(peers))

    def rc_(src, dst, i, dev):
        return pltpu.make_async_remote_copy(src_ref=src, dst_ref=dst, send_sem=ss.at[i], recv_sem=rs.at[i], device_id=dev, device_id_type=MESH)

    cps = []
    if with_x:
        a = rc_(p_ref.at[1 - x], rx, 0, xdev)
        a.start()
        a.wait_recv()
        cps.append(a)
        s0[...] = (p_ref[x].astype(F32) + rx[...].astype(F32)).astype(BF)
        base = s0
    else:
        base = p_ref
    b = rc_(base.at[1 - c], rc, 1, cdev)
    b.start()
    b.wait_recv()
    s1[...] = (base[c].astype(F32) + rc[...].astype(F32)).astype(BF)
    d = rc_(s1, ry, 2, ydev)
    d.start()
    d.wait_recv()
    total = (s1[...].astype(F32) + ry[...].astype(F32)).astype(BF)
    fin[...] = total
    e = rc_(fin, rf, 3, cdev)
    e.start()
    o_ref[c] = total.astype(F32)
    e.wait_recv()
    o_ref[1 - c] = rf[...].astype(F32)
    for k in cps + [b, d, e]:
        k.wait_send()


def slot_sum(part, cid, with_x=False):
    rows, width = part.shape[-2] // 2, part.shape[-1]
    shape = part.shape[:-2] + (2, rows, width)
    V = lambda *s: pltpu.VMEM(s, BF)
    D = pltpu.SemaphoreType.DMA
    vm = pl.BlockSpec(memory_space=pltpu.VMEM)
    out = pl.pallas_call(
        functools.partial(sum_kernel, with_x),
        out_shape=jax.ShapeDtypeStruct((2, rows, width), F32),
        in_specs=[vm],
        out_specs=vm,
        scratch_shapes=[V(2, rows, width), V(2, rows, width)] + [V(rows, width)] * 5 + [D((4,)), D((4,))],
        compiler_params=pltpu.CompilerParams(collective_id=cid, has_side_effects=True),
        name="slot_sum",
    )(part.reshape(shape))
    return out.reshape(2 * rows, width)


def slot_gather_kernel(p_ref, o_ref, sy, ss, rs):
    dp = lax.axis_index(DP)
    slot = lax.axis_index(SLOT)
    y, c = slot // 2, slot % 2
    ydev = (dp, (1 - y) * 2 + c)
    cdev = (dp, y * 2 + 1 - c)
    bar = pltpu.get_barrier_semaphore()
    for d in (ydev, cdev):
        pl.semaphore_signal(bar, inc=1, device_id=d, device_id_type=MESH)
    pl.semaphore_wait(bar, 2)

    def rc_(src, dst, i, dev):
        return pltpu.make_async_remote_copy(src_ref=src, dst_ref=dst, send_sem=ss.at[i], recv_sem=rs.at[i], device_id=dev, device_id_type=MESH)

    a = rc_(p_ref, o_ref.at[slot], 0, ydev)
    b = rc_(p_ref, o_ref.at[slot], 1, cdev)
    a.start()
    b.start()
    o_ref[slot] = p_ref[...]
    theirs = o_ref.at[ydev[1]]
    a.wait_recv()
    e = rc_(theirs, theirs, 2, cdev)
    e.start()
    b.wait_recv()
    e.wait_recv()
    for k in (a, b, e):
        k.wait_send()


def slot_gather(part, cid):
    D = pltpu.SemaphoreType.DMA
    vm = pl.BlockSpec(memory_space=pltpu.VMEM)
    out = pl.pallas_call(
        slot_gather_kernel,
        out_shape=jax.ShapeDtypeStruct((4,) + part.shape, part.dtype),
        in_specs=[vm],
        out_specs=vm,
        scratch_shapes=[pltpu.VMEM((8, 128), BF), D((3,)), D((3,))],
        compiler_params=pltpu.CompilerParams(collective_id=cid, has_side_effects=True),
        name="slot_gather",
    )(part)
    return out.reshape(4 * part.shape[0], part.shape[1])


def mm(spec, a, b):
    return jnp.einsum(spec, a, b, preferred_element_type=F32)


def local(
    byte_ids,
    seg_ids,
    embed_table,
    slot_project,
    patch_prenorm,
    patch_heads,
    patch_mixer,
    patch_midnorm,
    patch_expand,
    patch_reduce,
    byte_prenorm,
    byte_heads,
    byte_mixer,
    byte_midnorm,
    byte_expand,
    byte_reduce,
    d_output,
):
    dp = lax.axis_index(DP)
    slot = lax.axis_index(SLOT)
    x = dp % 2
    group_rows, patch_len = byte_ids.shape
    own_rows = group_rows // 4
    vocab_part, width = embed_table.shape
    vocab = vocab_part * 8
    share = width // 8
    ff = patch_expand.shape[1]
    quarter = share // 4
    pick = lambda v, axis: lax.dynamic_index_in_dim(v, slot, axis, keepdims=False)
    gains = jnp.concatenate([patch_prenorm, patch_midnorm, byte_prenorm, byte_midnorm])[None]
    gains = jnp.pad(gains, ((0, share - vocab_part - 1), (0, width - 4 * share)))
    misc = jnp.concatenate([embed_table, gains], axis=0)
    heads_own = pick(patch_heads.reshape(share, 3, 4, width // 4), 2).reshape(1, share, 3 * width // 4)
    expand_own = pick(patch_expand.reshape(share, 8, 4, share), 2).reshape(1, share, width)
    reduce_own = pick(patch_reduce.reshape(4, share, width), 0)[None]
    shared = lambda v: v.reshape(v.shape[0] // share, 2, 2, quarter, v.shape[1])
    arrs = [
        shared(misc), byte_ids.T[None], slot_project, heads_own, expand_own, reduce_own, patch_mixer[None],
        shared(byte_heads), shared(byte_mixer), shared(byte_expand), shared(byte_reduce),
    ]
    kinds = [SHARED, PRIVATE, ZONLY, PRIVATE, PRIVATE, PRIVATE, SINGLE] + [SHARED] * 4
    plan = [(0, SHARED, 0, 0, width), (1, PRIVATE, 0, 0, 0)]
    plan += [(7, SHARED, 0, i * width, width) for i in range(3)] + [(8, SHARED, 0, 0, width)]
    plan += [(9, SHARED, 0, i * width, width) for i in range(4)] + [(10, SHARED, i, 0, width) for i in range(4)]
    plan += [(3, PRIVATE, 0, 0, 0), (6, SINGLE, 0, 0, 0), (4, PRIVATE, 0, 0, 0), (5, PRIVATE, 0, 0, 0)]
    plan += [(2, ZONLY, 0, 0, 0), (2, ZONLY, 1, 0, 0)]
    full = gather_all(arrs, kinds, plan, 0, "gather_weights")
    misc_all = full[0].reshape(8, share, width)
    lookup = misc_all[:, :vocab_part].reshape(vocab, width)
    gains_all = misc_all[:, vocab_part, : 4 * share].reshape(8, 4, share).transpose(1, 0, 2).reshape(4, width)
    gains_all = gains_all.astype(F32)
    ids_all = full[1].reshape(8, patch_len, group_rows)
    project = full[2].reshape(2, 4 * share, width)
    p_heads = full[3].reshape(width, 3 * width // 4)
    p_expand = full[4].reshape(width, width)
    p_reduce = full[5].reshape(width, width)
    p_mixer = full[6].reshape(width // 4, width)
    b_heads = full[7].reshape(width, 3 * width)
    b_mixer = full[8].reshape(width, width)
    b_expand = full[9].reshape(width, ff)
    b_reduce = full[10].reshape(ff, width)
    vocab_iota = jnp.arange(vocab, dtype=jnp.int32)
    hot = lambda ids: (ids[..., None] == vocab_iota).astype(BF)

    z_ids = lax.dynamic_slice_in_dim(ids_all, (dp // 2) * 2, 2, 0)
    pair_ids = lax.dynamic_slice_in_dim(z_ids, slot * 2, 2, 1)
    lookup_parts = lookup.reshape(vocab, 4, 2, share)
    lookup_x = lax.dynamic_index_in_dim(lookup_parts, x, 2, keepdims=False).reshape(vocab, 4 * share)
    pair_tokens = mm("xpgv,vf->xpgf", hot(pair_ids), lookup_x).astype(BF)
    start_part = mm("xpgf,pfe->xge", pair_tokens, project).astype(BF)
    start = slot_sum(start_part, 2, True)

    segments = seg_ids[0]
    pos = jnp.arange(group_rows, dtype=jnp.int32)
    allowed_patch = ((pos[:, None] >= pos[None, :]) & (segments[:, None] == segments[None, :]))[None]
    heads = 3 * width // 4
    head_count = width // 4 // HEAD_DIM
    norm_one, back_one = jax.vjp(norm_rows, start, gains_all[0])
    norm_one = norm_one.astype(BF)
    joined = mm("nd,df->nf", norm_one, p_heads).astype(BF).reshape(1, group_rows, 3, head_count, HEAD_DIM)
    mixture, logsum = attention(joined[:, :, 0], joined[:, :, 1], joined[:, :, 2], allowed_patch)
    mixture = mixture.astype(BF).reshape(group_rows, width // 4)
    middle = start + slot_sum(mm("nf,fd->nd", mixture, p_mixer).astype(BF), 3)
    norm_two, back_two = jax.vjp(norm_rows, middle, gains_all[1])
    norm_two = norm_two.astype(BF)
    expanded = mm("nd,df->nf", norm_two, p_expand)
    hidden, back_gelu = jax.vjp(gelu_tanh, expanded)
    hidden = hidden.astype(BF)
    patch_out = middle + slot_sum(mm("nf,fd->nd", hidden, p_reduce).astype(BF), 4)

    first_row = slot * own_rows
    own_out = lax.dynamic_slice_in_dim(patch_out, first_row, own_rows, 0)
    local_bytes = lax.dynamic_slice_in_dim(byte_ids, first_row, own_rows, 0)
    local_onehot = hot(local_bytes)
    local_embed = mm("rpv,vd->rpd", local_onehot, lookup)
    fine_input = local_embed + own_out[:, None, :]
    tile_len = math.gcd(own_rows * patch_len, 128)
    tile_count = own_rows * patch_len // tile_len
    fine_input = fine_input.reshape(tile_count, tile_len, width)
    positions = jnp.arange(tile_len, dtype=jnp.int32)
    allowed_byte = (
        (positions[:, None] >= positions[None, :])
        & (positions[:, None] // patch_len == positions[None, :] // patch_len)
    )[None]

    def attend_byte(queries, keyset, valueset):
        return attention(queries, keyset, valueset, allowed_byte)

    def attend_byte_back(queries, keyset, valueset, kept, d_mixture):
        return attention_back(queries, keyset, valueset, allowed_byte, kept, d_mixture)

    byte_weights = (gains_all[2], b_heads, b_mixer, gains_all[3], b_expand, b_reduce)
    byte_out, byte_saved = block_forward(fine_input, byte_weights, attend_byte)
    out_bytes = byte_out.reshape(own_rows, patch_len, width).astype(BF)
    d_fine, byte_grads = block_backward(
        d_output.astype(F32).reshape(tile_count, tile_len, width), byte_weights, byte_saved, attend_byte_back
    )
    d_fine = d_fine.reshape(own_rows, patch_len, width)

    g_low = slot_gather(jnp.sum(d_fine, axis=1).astype(BF), 7)
    grad = g_low.astype(F32)
    g_reduce = mm("nf,nd->fd", hidden, g_low).astype(BF)
    (d_expanded,) = back_gelu(mm("nd,fd->nf", g_low, p_reduce))
    d_expanded = d_expanded.astype(BF)
    g_expand = mm("nd,nf->df", norm_two, d_expanded).astype(BF)
    d_norm_two = slot_sum(mm("nf,df->nd", d_expanded, p_expand).astype(BF), 5)
    d_middle_part, g_midnorm = back_two(d_norm_two)
    d_middle = grad + d_middle_part
    middle_low = d_middle.astype(BF)
    g_mixer = mm("nf,nd->fd", mixture, middle_low).astype(BF)
    d_mixture = mm("nd,fd->nf", middle_low, p_mixer).astype(BF).reshape(1, group_rows, head_count, HEAD_DIM)
    d_joined = attention_back(joined[:, :, 0], joined[:, :, 1], joined[:, :, 2], allowed_patch, logsum, d_mixture)
    d_joined = jnp.stack(d_joined, axis=2).reshape(group_rows, heads).astype(BF)
    g_heads = mm("nd,nf->df", norm_one, d_joined).astype(BF)
    d_norm_one = slot_sum(mm("nf,df->nd", d_joined, p_heads).astype(BF), 6)
    d_start_part, g_prenorm = back_one(d_norm_one)
    d_start = (d_middle + d_start_part).astype(BF)

    rows_all = gather_all(
        [d_start.reshape(1, 2, 2, group_rows // 4, width)], [SHARED],
        [(0, SHARED, 0, i * (width // 3), width // 3) for i in range(3)], 8, "gather_d_start",
    )[0].reshape(8 * group_rows, width)
    slot_ids = lax.dynamic_slice_in_dim(ids_all, slot * 2, 2, 1).transpose(1, 0, 2).reshape(2, 8 * group_rows)
    by_value = mm("pgv,ge->pve", hot(slot_ids), rows_all).astype(BF)
    lookup_own = lax.dynamic_index_in_dim(lookup.reshape(vocab, 8, share), dp, 1, keepdims=False)
    project_grad = mm("vf,pve->pfe", lookup_own, by_value)
    project_wide = lax.dynamic_update_slice_in_dim(jnp.zeros((2, width, width), BF), slot_project, dp * share, 1)
    table_grad = mm("pve,pfe->vf", by_value, project_wide)
    low_fine = d_fine.astype(BF)
    rest_fine = (d_fine - low_fine.astype(F32)).astype(BF)
    table_grad = table_grad + mm("rpv,rpd->vd", local_onehot, low_fine) + mm("rpv,rpd->vd", local_onehot, rest_fine)

    first = (slot == 0).astype(F32)
    byte_pre, byte_qkv, byte_mix, byte_mid, byte_exp, byte_red = byte_grads
    gain_grads = jnp.stack([g_prenorm * first, g_midnorm * first, byte_pre, byte_mid])
    gain_grads = gain_grads.reshape(4, 8, share).transpose(1, 0, 2).reshape(8, 1, 4 * share)
    gain_grads = jnp.pad(gain_grads, ((0, 0), (0, share - vocab_part - 1), (0, width - 4 * share)))
    misc_grad = jnp.concatenate([table_grad.reshape(8, vocab_part, width), gain_grads], axis=1)
    grouped = lambda v: v.astype(BF).reshape(4, 2, v.shape[0] // width, 2, 2, quarter, v.shape[1])
    private = lambda v: v.reshape(1, 4, 2, share, v.shape[1])
    garr = [
        misc_grad.astype(BF).reshape(4, 2, 1, 2, 2, quarter, width),
        grouped(byte_qkv), grouped(byte_mix), grouped(byte_exp), grouped(byte_red),
        private(g_heads), private(g_expand), private(g_reduce),
    ]
    gkinds = [SHARED] * 5 + [PRIVATE] * 3
    bplan = [(4, SHARED, i, 0) for i in range(4)] + [(3, SHARED, 0, i) for i in range(4)]
    bplan += [(2, SHARED, 0, 0)] + [(1, SHARED, 0, i) for i in range(3)]
    gplan = bplan[:3] + [(7, PRIVATE, 0, 0)] + bplan[3:6] + [(6, PRIVATE, 0, 0)] + bplan[6:9]
    gplan += [(5, PRIVATE, 0, 0)] + bplan[9:] + [(0, SHARED, 0, 0)]
    res = reduce_all(garr, gkinds, gplan, g_mixer.reshape(2, share, width))
    misc_out = res[0].reshape(share, width).astype(F32)
    gain_out = misc_out[vocab_part, : 4 * share].reshape(4, share)
    out_heads = res[5].reshape(4, share, 3, width // 4).transpose(1, 2, 0, 3).reshape(share, 3 * width)
    out_expand = res[6].reshape(4, share, 8, share).transpose(1, 2, 0, 3).reshape(share, ff)
    return (
        out_bytes,
        misc_out[:vocab_part],
        project_grad,
        gain_out[0],
        out_heads.astype(F32),
        res[8].astype(F32),
        gain_out[1],
        out_expand.astype(F32),
        res[7].reshape(4 * share, width).astype(F32),
        gain_out[2],
        res[1].reshape(share, 3 * width).astype(F32),
        res[2].reshape(share, width).astype(F32),
        gain_out[3],
        res[3].reshape(share, ff).astype(F32),
        res[4].reshape(4 * share, width).astype(F32),
    )


def solution(mesh):
    if (mesh.shape[DP], mesh.shape[SLOT]) != (8, 4):
        return generic_solution(mesh)
    placed = (P(DP, None), P(DP, None), P(DP, None), P(SLOT, DP, None)) + (
        P(DP), P(DP, None), P(DP, None), P(DP), P(DP, None), P(DP, None),
    ) * 2 + (P((DP, SLOT), None, None),)
    outs = (P((DP, SLOT), None, None), P(DP, None), P(SLOT, DP, None)) + (
        P(DP), P(DP, None), P(DP, None), P(DP), P(DP, None), P(DP, None),
    ) * 2
    return jax.shard_map(local, mesh=mesh, in_specs=placed, out_specs=outs, check_vma=False)
```

```python
import functools
import math
from types import SimpleNamespace as NS

import jax
import jax.numpy as jnp
from jax import lax
from jax.experimental import pallas as pl
from jax.experimental.pallas import tpu as pltpu
from jax.sharding import PartitionSpec as P

MESH = pl.DeviceIdType.MESH
BF = jnp.bfloat16
F32 = jnp.float32
DP, SLOT = "dp", "slot"
SHARED, PRIVATE, ZONLY, SINGLE = range(4)

HEAD_DIM = 64


EPSILON = 1e-05
MASKED = -1000000000.0


def norm_rows(values, gain_vec):
    center = jnp.mean(values, axis=-1, keepdims=True)
    shifted = values - center
    spread = jnp.mean(shifted * shifted, axis=-1, keepdims=True)
    return shifted * lax.rsqrt(spread + EPSILON) * gain_vec


def gelu_tanh(values):
    inside = 0.7978845608028654 * (values + 0.044715 * values * values * values)
    return 0.5 * values * (1.0 + jnp.tanh(inside))


def attention(queries, keyset, valueset, allowed):
    scores = jnp.einsum(
        "bnhe,bmhe->bhnm", queries, keyset, preferred_element_type=jnp.float32
    ) * HEAD_DIM ** (-0.5)
    scores = jnp.where(allowed[:, None], scores, MASKED)
    highest = jnp.max(scores, axis=-1, keepdims=True)
    exponents = jnp.exp(scores - highest)
    totals = jnp.sum(exponents, axis=-1, keepdims=True)
    softened = (exponents / totals).astype(jnp.bfloat16)
    mixture = jnp.einsum("bhnm,bmhe->bnhe", softened, valueset, preferred_element_type=jnp.float32)
    return (mixture, highest + jnp.log(totals))


def attention_back(queries, keyset, valueset, allowed, logsum, d_mixture):
    scale_value = HEAD_DIM ** (-0.5)
    scores = (
        jnp.einsum("bnhe,bmhe->bhnm", queries, keyset, preferred_element_type=jnp.float32)
        * scale_value
    )
    scores = jnp.where(allowed[:, None], scores, MASKED)
    softened = jnp.exp(scores - logsum)
    d_soft = jnp.einsum("bnhe,bmhe->bhnm", d_mixture, valueset, preferred_element_type=jnp.float32)
    inside = jnp.sum(d_soft * softened, axis=-1, keepdims=True)
    d_scores = (softened * (d_soft - inside)).astype(jnp.bfloat16)
    d_queries = (
        jnp.einsum("bhnm,bmhe->bnhe", d_scores, keyset, preferred_element_type=jnp.float32)
        * scale_value
    )
    d_keys = (
        jnp.einsum("bhnm,bnhe->bmhe", d_scores, queries, preferred_element_type=jnp.float32)
        * scale_value
    )
    d_values = jnp.einsum(
        "bhnm,bnhe->bmhe",
        softened.astype(jnp.bfloat16),
        d_mixture,
        preferred_element_type=jnp.float32,
    )
    return (d_queries, d_keys, d_values)


def block_forward(values, weights, attend):
    gain_one, w_heads, w_mixer, gain_two, w_expand, w_reduce = weights
    batch, row_count, width = values.shape
    head_count = width // HEAD_DIM
    norm_one, back_one = jax.vjp(norm_rows, values, gain_one.astype(jnp.float32))
    norm_one = norm_one.astype(jnp.bfloat16)
    joined = jnp.einsum(
        "bnd,df->bnf", norm_one, w_heads, preferred_element_type=jnp.float32
    ).astype(jnp.bfloat16)
    joined = joined.reshape(batch, row_count, 3, head_count, HEAD_DIM)
    mixture, kept = attend(joined[:, :, 0], joined[:, :, 1], joined[:, :, 2])
    mixture = mixture.astype(jnp.bfloat16).reshape(batch, row_count, width)
    middle = values + jnp.einsum(
        "bnf,fd->bnd", mixture, w_mixer, preferred_element_type=jnp.float32
    )
    norm_two, back_two = jax.vjp(norm_rows, middle, gain_two.astype(jnp.float32))
    norm_two = norm_two.astype(jnp.bfloat16)
    expanded = jnp.einsum("bnd,df->bnf", norm_two, w_expand, preferred_element_type=jnp.float32)
    hidden, back_gelu = jax.vjp(gelu_tanh, expanded)
    hidden = hidden.astype(jnp.bfloat16)
    result = middle + jnp.einsum(
        "bnf,fd->bnd", hidden, w_reduce, preferred_element_type=jnp.float32
    )
    saved = (back_one, norm_one, joined, kept, mixture, back_two, norm_two, back_gelu, hidden)
    return (result, saved)


def block_backward(grad_out, weights, saved, attend_back):
    gain_one, w_heads, w_mixer, gain_two, w_expand, w_reduce = weights
    back_one, norm_one, joined, kept, mixture, back_two, norm_two, back_gelu, hidden = saved
    batch, row_count, width = grad_out.shape
    grad_low = grad_out.astype(jnp.bfloat16)
    reduce_grad = jnp.einsum("bnf,bnd->fd", hidden, grad_low, preferred_element_type=jnp.float32)
    d_hidden = jnp.einsum("bnd,fd->bnf", grad_low, w_reduce, preferred_element_type=jnp.float32)
    (d_expanded,) = back_gelu(d_hidden)
    d_expanded = d_expanded.astype(jnp.bfloat16)
    expand_grad = jnp.einsum(
        "bnd,bnf->df", norm_two, d_expanded, preferred_element_type=jnp.float32
    )
    d_norm_two = jnp.einsum("bnf,df->bnd", d_expanded, w_expand, preferred_element_type=jnp.float32)
    d_middle_part, midnorm_grad = back_two(d_norm_two)
    d_middle = grad_out + d_middle_part
    middle_low = d_middle.astype(jnp.bfloat16)
    mixer_grad = jnp.einsum("bnf,bnd->fd", mixture, middle_low, preferred_element_type=jnp.float32)
    d_mixture = jnp.einsum(
        "bnd,fd->bnf", middle_low, w_mixer, preferred_element_type=jnp.float32
    ).astype(jnp.bfloat16)
    d_mixture = d_mixture.reshape(batch, row_count, width // HEAD_DIM, HEAD_DIM)
    d_queries, d_keys, d_values = attend_back(
        joined[:, :, 0], joined[:, :, 1], joined[:, :, 2], kept, d_mixture
    )
    d_joined = (
        jnp.stack([d_queries, d_keys, d_values], axis=2)
        .reshape(batch, row_count, 3 * width)
        .astype(jnp.bfloat16)
    )
    heads_grad = jnp.einsum("bnd,bnf->df", norm_one, d_joined, preferred_element_type=jnp.float32)
    d_norm_one = jnp.einsum("bnf,df->bnd", d_joined, w_heads, preferred_element_type=jnp.float32)
    d_input_part, prenorm_grad = back_one(d_norm_one)
    return (
        d_middle + d_input_part,
        (prenorm_grad, heads_grad, mixer_grad, midnorm_grad, expand_grad, reduce_grad),
    )


def generic_local(
    byte_ids,
    seg_ids,
    embed_table,
    slot_project,
    patch_prenorm,
    patch_heads,
    patch_mixer,
    patch_midnorm,
    patch_expand,
    patch_reduce,
    byte_prenorm,
    byte_heads,
    byte_mixer,
    byte_midnorm,
    byte_expand,
    byte_reduce,
    d_output,
):
    slot_count = lax.axis_size(SLOT)
    slot_index = lax.axis_index(SLOT)
    group_rows = byte_ids.shape[0]
    own_rows = group_rows // slot_count
    patch_len = byte_ids.shape[1]
    slot_share = patch_len // slot_count
    gathered = (
        lax.all_gather(embed_table, DP, axis=0, tiled=True),
        lax.all_gather(slot_project, DP, axis=1, tiled=True),
        lax.all_gather(patch_prenorm, DP, axis=0, tiled=True),
        lax.all_gather(patch_heads, DP, axis=0, tiled=True),
        lax.all_gather(patch_mixer, DP, axis=0, tiled=True),
        lax.all_gather(patch_midnorm, DP, axis=0, tiled=True),
        lax.all_gather(patch_expand, DP, axis=0, tiled=True),
        lax.all_gather(patch_reduce, DP, axis=0, tiled=True),
        lax.all_gather(byte_prenorm, DP, axis=0, tiled=True),
        lax.all_gather(byte_heads, DP, axis=0, tiled=True),
        lax.all_gather(byte_mixer, DP, axis=0, tiled=True),
        lax.all_gather(byte_midnorm, DP, axis=0, tiled=True),
        lax.all_gather(byte_expand, DP, axis=0, tiled=True),
        lax.all_gather(byte_reduce, DP, axis=0, tiled=True),
    )
    lookup = gathered[0]
    project = gathered[1]
    patch_weights = gathered[2:8]
    byte_weights = gathered[8:14]
    vocab_size = lookup.shape[0]
    width = lookup.shape[1]
    head_count = width // HEAD_DIM
    vocab_iota = jnp.arange(vocab_size, dtype=jnp.int32)
    slot_bytes = lax.dynamic_slice_in_dim(byte_ids, slot_index * slot_share, slot_share, 1)
    slot_onehot = (slot_bytes[:, :, None] == vocab_iota).astype(jnp.bfloat16)
    slot_embed = jnp.einsum(
        "gpv,vd->gpd", slot_onehot, lookup, preferred_element_type=jnp.float32
    ).astype(jnp.bfloat16)
    rows_embed = slot_embed
    patch_start = lax.psum_scatter(
        jnp.einsum("cpd,pde->ce", rows_embed, project, preferred_element_type=jnp.float32).astype(
            jnp.bfloat16
        ),
        SLOT,
        scatter_dimension=0,
        tiled=True,
    ).astype(jnp.float32)
    segments = seg_ids[0]
    first_row = slot_index * own_rows
    query_pos = first_row + jnp.arange(own_rows, dtype=jnp.int32)
    key_pos = jnp.arange(group_rows, dtype=jnp.int32)
    query_seg = lax.dynamic_slice_in_dim(segments, first_row, own_rows, 0)
    allowed_patch = (
        (query_pos[:, None] >= key_pos[None, :]) & (query_seg[:, None] == segments[None, :])
    )[None]

    def attend_patch(queries, keyset, valueset):
        all_keys, all_values = (
            lax.all_gather(keyset.reshape(own_rows, width), SLOT, axis=0, tiled=True),
            lax.all_gather(valueset.reshape(own_rows, width), SLOT, axis=0, tiled=True),
        )
        all_keys = all_keys.reshape(1, group_rows, head_count, HEAD_DIM)
        all_values = all_values.reshape(1, group_rows, head_count, HEAD_DIM)
        mixture, logsum = attention(queries, all_keys, all_values, allowed_patch)
        return (mixture, (all_keys, all_values, logsum))

    def attend_patch_back(queries, keyset, valueset, kept, d_mixture):
        all_keys, all_values, logsum = kept
        d_queries, d_keys, d_values = attention_back(
            queries, all_keys, all_values, allowed_patch, logsum, d_mixture
        )
        own_keys, own_values = (
            lax.psum_scatter(
                d_keys.reshape(group_rows, width).astype(jnp.bfloat16),
                SLOT,
                scatter_dimension=0,
                tiled=True,
            ).astype(jnp.float32),
            lax.psum_scatter(
                d_values.reshape(group_rows, width).astype(jnp.bfloat16),
                SLOT,
                scatter_dimension=0,
                tiled=True,
            ).astype(jnp.float32),
        )
        return (d_queries, own_keys.reshape(keyset.shape), own_values.reshape(valueset.shape))

    patch_out, patch_saved = block_forward(patch_start[None], patch_weights, attend_patch)
    local_bytes = lax.dynamic_slice_in_dim(byte_ids, first_row, own_rows, 0)
    local_onehot = (local_bytes[:, :, None] == vocab_iota).astype(jnp.bfloat16)
    local_embed = jnp.einsum(
        "rpv,vd->rpd", local_onehot, lookup, preferred_element_type=jnp.float32
    )
    fine_input = local_embed + patch_out[0][:, None, :]
    tile_len = math.gcd(own_rows * patch_len, 128)
    tile_count = own_rows * patch_len // tile_len
    fine_input = fine_input.reshape(tile_count, tile_len, width)
    positions = jnp.arange(tile_len, dtype=jnp.int32)
    allowed_byte = (
        (positions[:, None] >= positions[None, :])
        & (positions[:, None] // patch_len == positions[None, :] // patch_len)
    )[None]

    def attend_byte(queries, keyset, valueset):
        return attention(queries, keyset, valueset, allowed_byte)

    def attend_byte_back(queries, keyset, valueset, kept, d_mixture):
        return attention_back(queries, keyset, valueset, allowed_byte, kept, d_mixture)

    byte_out, byte_saved = block_forward(fine_input, byte_weights, attend_byte)
    out_bytes = byte_out.reshape(own_rows, patch_len, width).astype(jnp.bfloat16)
    d_fine, byte_grads = block_backward(
        d_output.astype(jnp.float32).reshape(tile_count, tile_len, width),
        byte_weights,
        byte_saved,
        attend_byte_back,
    )
    d_fine = d_fine.reshape(own_rows, patch_len, width)
    d_patch = jnp.sum(d_fine, axis=1)[None]
    d_start, patch_grads = block_backward(d_patch, patch_weights, patch_saved, attend_patch_back)
    embed_local = jnp.einsum(
        "rpv,rpd->vd", local_onehot.astype(jnp.float32), d_fine, precision=lax.Precision.HIGHEST
    )
    portion = lax.all_gather(d_start[0].astype(jnp.bfloat16), SLOT, axis=0, tiled=True)
    rows_embed = slot_embed
    rows_hot = slot_onehot.astype(jnp.float32)
    proj_sum = jnp.einsum("cpd,ce->pde", rows_embed, portion, preferred_element_type=jnp.float32)
    d_rows = jnp.einsum("ce,pde->cpd", portion, project, preferred_element_type=jnp.float32)
    table_sum = jnp.einsum("cpv,cpd->vd", rows_hot, d_rows, precision=lax.Precision.HIGHEST)
    table_grad = embed_local + table_sum
    patch_pre, patch_qkv_grad, patch_mix, patch_mid, patch_exp, patch_red = patch_grads
    byte_pre, byte_qkv_grad, byte_mix, byte_mid, byte_exp, byte_red = byte_grads
    reduced = (
        lax.psum_scatter(table_grad, DP, scatter_dimension=0, tiled=True),
        lax.psum_scatter(patch_pre, DP, scatter_dimension=0, tiled=True),
        lax.psum_scatter(patch_qkv_grad, DP, scatter_dimension=0, tiled=True),
        lax.psum_scatter(patch_mix, DP, scatter_dimension=0, tiled=True),
        lax.psum_scatter(patch_mid, DP, scatter_dimension=0, tiled=True),
        lax.psum_scatter(patch_exp, DP, scatter_dimension=0, tiled=True),
        lax.psum_scatter(patch_red, DP, scatter_dimension=0, tiled=True),
        lax.psum_scatter(byte_pre, DP, scatter_dimension=0, tiled=True),
        lax.psum_scatter(byte_qkv_grad, DP, scatter_dimension=0, tiled=True),
        lax.psum_scatter(byte_mix, DP, scatter_dimension=0, tiled=True),
        lax.psum_scatter(byte_mid, DP, scatter_dimension=0, tiled=True),
        lax.psum_scatter(byte_exp, DP, scatter_dimension=0, tiled=True),
        lax.psum_scatter(byte_red, DP, scatter_dimension=0, tiled=True),
        lax.psum_scatter(proj_sum, DP, scatter_dimension=1, tiled=True),
    )
    shares = (
        lax.psum_scatter(
            reduced[0].astype(jnp.bfloat16), SLOT, scatter_dimension=0, tiled=True
        ).astype(jnp.float32),
        lax.psum_scatter(
            reduced[1].astype(jnp.bfloat16), SLOT, scatter_dimension=0, tiled=True
        ).astype(jnp.float32),
        lax.psum_scatter(
            reduced[2].astype(jnp.bfloat16), SLOT, scatter_dimension=0, tiled=True
        ).astype(jnp.float32),
        lax.psum_scatter(
            reduced[3].astype(jnp.bfloat16), SLOT, scatter_dimension=0, tiled=True
        ).astype(jnp.float32),
        lax.psum_scatter(
            reduced[4].astype(jnp.bfloat16), SLOT, scatter_dimension=0, tiled=True
        ).astype(jnp.float32),
        lax.psum_scatter(
            reduced[5].astype(jnp.bfloat16), SLOT, scatter_dimension=0, tiled=True
        ).astype(jnp.float32),
        lax.psum_scatter(
            reduced[6].astype(jnp.bfloat16), SLOT, scatter_dimension=0, tiled=True
        ).astype(jnp.float32),
        lax.psum_scatter(
            reduced[7].astype(jnp.bfloat16), SLOT, scatter_dimension=0, tiled=True
        ).astype(jnp.float32),
        lax.psum_scatter(
            reduced[8].astype(jnp.bfloat16), SLOT, scatter_dimension=0, tiled=True
        ).astype(jnp.float32),
        lax.psum_scatter(
            reduced[9].astype(jnp.bfloat16), SLOT, scatter_dimension=0, tiled=True
        ).astype(jnp.float32),
        lax.psum_scatter(
            reduced[10].astype(jnp.bfloat16), SLOT, scatter_dimension=0, tiled=True
        ).astype(jnp.float32),
        lax.psum_scatter(
            reduced[11].astype(jnp.bfloat16), SLOT, scatter_dimension=0, tiled=True
        ).astype(jnp.float32),
        lax.psum_scatter(
            reduced[12].astype(jnp.bfloat16), SLOT, scatter_dimension=0, tiled=True
        ).astype(jnp.float32),
    )
    summed = (
        lax.all_gather(shares[0].astype(jnp.bfloat16), SLOT, axis=0, tiled=True).astype(
            jnp.float32
        ),
        lax.all_gather(shares[1].astype(jnp.bfloat16), SLOT, axis=0, tiled=True).astype(
            jnp.float32
        ),
        lax.all_gather(shares[2].astype(jnp.bfloat16), SLOT, axis=0, tiled=True).astype(
            jnp.float32
        ),
        lax.all_gather(shares[3].astype(jnp.bfloat16), SLOT, axis=0, tiled=True).astype(
            jnp.float32
        ),
        lax.all_gather(shares[4].astype(jnp.bfloat16), SLOT, axis=0, tiled=True).astype(
            jnp.float32
        ),
        lax.all_gather(shares[5].astype(jnp.bfloat16), SLOT, axis=0, tiled=True).astype(
            jnp.float32
        ),
        lax.all_gather(shares[6].astype(jnp.bfloat16), SLOT, axis=0, tiled=True).astype(
            jnp.float32
        ),
        lax.all_gather(shares[7].astype(jnp.bfloat16), SLOT, axis=0, tiled=True).astype(
            jnp.float32
        ),
        lax.all_gather(shares[8].astype(jnp.bfloat16), SLOT, axis=0, tiled=True).astype(
            jnp.float32
        ),
        lax.all_gather(shares[9].astype(jnp.bfloat16), SLOT, axis=0, tiled=True).astype(
            jnp.float32
        ),
        lax.all_gather(shares[10].astype(jnp.bfloat16), SLOT, axis=0, tiled=True).astype(
            jnp.float32
        ),
        lax.all_gather(shares[11].astype(jnp.bfloat16), SLOT, axis=0, tiled=True).astype(
            jnp.float32
        ),
        lax.all_gather(shares[12].astype(jnp.bfloat16), SLOT, axis=0, tiled=True).astype(
            jnp.float32
        ),
    )
    proj_final = reduced[13]
    return (
        out_bytes,
        summed[0],
        proj_final,
        summed[1],
        summed[2],
        summed[3],
        summed[4],
        summed[5],
        summed[6],
        summed[7],
        summed[8],
        summed[9],
        summed[10],
        summed[11],
        summed[12],
    )


def generic_solution(mesh):
    placed = (
        P(DP, None),
        P(DP, None),
        P(DP, None),
        P(SLOT, DP, None),
        P(DP),
        P(DP, None),
        P(DP, None),
        P(DP),
        P(DP, None),
        P(DP, None),
        P(DP),
        P(DP, None),
        P(DP, None),
        P(DP),
        P(DP, None),
        P(DP, None),
        P((DP, SLOT), None, None),
    )
    return jax.shard_map(
        generic_local,
        mesh=mesh,
        in_specs=placed,
        out_specs=(
            P((DP, SLOT), None, None),
            P(DP, None),
            P(SLOT, DP, None),
            P(DP),
            P(DP, None),
            P(DP, None),
            P(DP),
            P(DP, None),
            P(DP, None),
            P(DP),
            P(DP, None),
            P(DP, None),
            P(DP),
            P(DP, None),
            P(DP, None),
        ),
        check_vma=False,
    )


W, SP = 4, 2
XD = 3 * SP
YD = XD + SP


class Gather:
    def __init__(self, chunks, sems):
        self.ch = chunks
        self.s = sems
        dp = lax.axis_index(DP); slot = lax.axis_index(SLOT)
        self.dp, self.slot = dp, slot
        self.z, self.x = dp // 2, dp % 2
        self.y, self.c = slot // 2, slot % 2
        self.xdev = (self.z * 2 + 1 - self.x, slot)
        self.ydev = (dp, (1 - self.y) * 2 + self.c)
        self.cdev = (dp, self.y * 2 + 1 - self.c)
        self.sent = []
    def zdev(self, d): return ((self.z + d) * 2 + self.x, self.slot)
    def barrier_peers(self):
        z = self.z
        return [(None, self.xdev), (None, self.ydev), (None, self.cdev), (z > 0, self.zdev(-1)), (z < 3, self.zdev(1))]
    def cp(self, src, dst, ss, rs, dev):
        return pltpu.make_async_remote_copy(src_ref=src, dst_ref=dst, send_sem=ss, recv_sem=rs, device_id=dev, device_id_type=MESH)
    def send(self, pred, *a):
        if pred is None: self.cp(*a).start()
        else:
            @pl.when(pred)
            def _(): self.cp(*a).start()
    def reg(self, t, oz, ox, y, c):
        k = self.ch[t]
        return k.dst(oz, ox, y, c)
    def start(self, t):
        k = self.ch[t]; z, x, y, c = self.z, self.x, self.y, self.c
        zs, zr, xs, xr = self.s.zs, self.s.zr, self.s.xs, self.s.xr
        src = k.src(y, c); dst = self.reg(t, z, x, y, c)
        one = k.kind == SINGLE
        mine = z == self.slot
        self.send((z < 3) & mine if one else z < 3, src, dst, zs.at[t, 0, z], zr.at[t, z], self.zdev(1))
        self.send((z > 0) & mine if one else z > 0, src, dst, zs.at[t, 1, z], zr.at[t, z], self.zdev(-1))
        if k.kind != ZONLY:
            self.send(mine if one else None, src, dst, xs.at[t, 0], xr.at[t, 0], self.xdev)
    def wait(self, ref, rs, ss):
        self.cp(ref, ref, ss, rs, (self.dp, self.slot)).wait_recv()
    def zarr(self, t, d):
        k = self.ch[t]; z, x, y, c = self.z, self.x, self.y, self.c; S = self.s
        for side in (-1, 1):
            oz = z + side * d
            ok = oz == self.slot if k.kind == SINGLE else (oz >= 0) & (oz <= 3)
            nxt = -side
            nok = (z + nxt >= 0) & (z + nxt <= 3)
            @pl.when(ok)
            def _():
                r = self.reg(t, oz, x, y, c)
                self.wait(r, S.zr.at[t, oz], S.zs.at[t, 0, z])
                if d < 3:
                    @pl.when(nok)
                    def _(): self.cp(r, r, S.zs.at[t, 0 if nxt == 1 else 1, oz], S.zr.at[t, oz], self.zdev(nxt)).start()
                if k.kind != ZONLY:
                    self.cp(r, r, S.xs.at[t, 0], S.xr.at[t, 0], self.xdev).start()
                if k.kind == SHARED:
                    q = k.pos
                    self.cp(r, r, S.ys.at[q, 0], S.yr.at[q, 0], self.ydev).start()
    def xarr(self, t):
        k = self.ch[t]; x, y, c = self.x, self.y, self.c; S = self.s
        if k.kind == ZONLY: return
        r = k.xall(1 - x, y, c)
        self.wait(r, S.xr.at[t, 0], S.xs.at[t, 0])
        if k.kind == SHARED:
            q = k.pos
            self.cp(r, r, S.ys.at[q, 1], S.yr.at[q, 1], self.ydev).start()
            r = k.all(y, c)
            self.cp(r, r, S.cs.at[q, 0], S.cr.at[q, 0], self.cdev).start()
    def yarr(self, t):
        k = self.ch[t]; x, y, c = self.x, self.y, self.c; S = self.s
        if k.kind != SHARED: return
        q = k.pos
        self.wait(k.three(1 - y, c), S.yr.at[q, 0], S.ys.at[q, 0])
        self.wait(k.xall(1 - x, 1 - y, c), S.yr.at[q, 1], S.ys.at[q, 1])
        r = k.all(1 - y, c)
        self.cp(r, r, S.cs.at[q, 1], S.cr.at[q, 1], self.cdev).start()
    def finish(self, t):
        k = self.ch[t]; y, c = self.y, self.c; S = self.s
        if k.kind != SHARED: return
        q = k.pos
        for h in (0, 1):
            self.wait(k.all(y if h == 0 else 1 - y, 1 - c), S.cr.at[q, h], S.cs.at[q, h])
    def drain(self, t):
        k = self.ch[t]; z, x, y, c = self.z, self.x, self.y, self.c; S = self.s
        r = self.reg(t, z, x, y, c)
        def ws(ss, r): self.cp(r, r, ss, ss, (self.dp, self.slot)).wait_send()
        if k.kind == SINGLE:
            @pl.when((z < 3) & (self.slot <= z))
            def _(): ws(S.zs.at[t, 0, self.slot], r)
            @pl.when((z > 0) & (self.slot >= z))
            def _(): ws(S.zs.at[t, 1, self.slot], r)
        else:
            for i in range(4):
                @pl.when((z < 3) & (i <= z))
                def _(): ws(S.zs.at[t, 0, i], r)
                @pl.when((z > 0) & (i >= z))
                def _(): ws(S.zs.at[t, 1, i], r)
        if k.kind != ZONLY: ws(S.xs.at[t, 0], k.xall(x, y, c))
        if k.kind == SHARED:
            q = k.pos
            ws(S.ys.at[q, 0], k.three(y, c)); ws(S.ys.at[q, 1], k.xall(1 - x, y, c))
            for h in (0, 1): ws(S.cs.at[q, h], k.all(y, c))
    def steps(self):
        n = len(self.ch)
        for t in range(min(W, n)): self.start(t)
        yield
        for i in range(n + YD):
            for d in (1, 2, 3):
                t = i - SP * (d - 1)
                if 0 <= t < n: self.zarr(t, d)
            if i + W < n: self.start(i + W)
            t = i - XD
            if 0 <= t < n: self.xarr(t)
            t = i - YD
            if 0 <= t < n: self.yarr(t)
            yield


def gather_sems(plan, count):
    T = len(plan)
    Q = max(1, sum(p[1] == SHARED for p in plan))
    D = pltpu.SemaphoreType.DMA
    return [D((T, 2, 4)), D((T, 4)), D((T, 1)), D((T, 1)), D((Q, 2)), D((Q, 2)), D((Q, 2)), D((Q, 2)), D((count,))]


def gather_chunks(plan, ins, outs):
    chunks = []
    pos = 0
    for (a, kind, j, c0, cw) in plan:
        i, o = ins[a], outs[a]
        if kind == SHARED:
            col = pl.ds(c0, cw)
            src = lambda y, c, i=i, j=j, col=col: i.at[j, y, c, :, col]
            dst = lambda oz, ox, y, c, o=o, j=j, col=col: o.at[oz, ox, j, y, c, :, col]
            xall = lambda ox, y, c, o=o, j=j, col=col: o.at[:, ox, j, y, c, :, col]
            al = lambda y, c, o=o, j=j, col=col: o.at[:, :, j, y, c, :, col]
            three = lambda y, c, o=o, j=j, col=col: o.at[pl.ds(0, 3), 0, j, y, c, :, col]
            chunks.append(NS(kind=kind, src=src, dst=dst, pos=pos, xall=xall, all=al, three=three))
            pos += 1
            continue
        src = lambda y, c, i=i, j=j: i.at[j]
        if kind == PRIVATE:
            dst = lambda oz, ox, y, c, o=o, j=j: o.at[j, oz, ox]
            xall = lambda ox, y, c, o=o, j=j: o.at[j, :, ox]
        elif kind == ZONLY:
            dst = lambda oz, ox, y, c, o=o, j=j: o.at[j, oz]
            xall = None
        else:
            dst = lambda oz, ox, y, c, o=o, j=j: o.at[j, ox]
            xall = lambda ox, y, c, o=o, j=j: o.at[j, ox]
        chunks.append(NS(kind=kind, src=src, dst=dst, xall=xall))
    return chunks


def gather_enter(g, peers=()):
    bar = pltpu.get_barrier_semaphore()
    for pred, dev in g.barrier_peers():
        def sig(dev=dev): pl.semaphore_signal(bar, inc=1, device_id=dev, device_id_type=MESH)
        if pred is None: sig()
        else: pl.when(pred)(sig)
    inner = (g.z > 0) & (g.z < 3)
    @pl.when(inner)
    def _(): pl.semaphore_wait(bar, 5)
    @pl.when(jnp.logical_not(inner))
    def _(): pl.semaphore_wait(bar, 4)


def gather_own(g, plan, ins, outs, bounce, sems):
    kinds = {p[0]: p[1] for p in plan}
    def inside(a):
        i = ins[a].at[:, :, g.c] if kinds[a] == SHARED else ins[a]
        return pltpu.make_async_copy(i, bounce[a], sems.ls.at[a])
    def outside(a):
        o, kind = outs[a], kinds[a]
        if kind == SHARED: o = o.at[g.z, g.x, :, :, g.c]
        elif kind == PRIVATE: o = o.at[:, g.z, g.x]
        elif kind == ZONLY: o = o.at[:, g.z]
        else: o = o.at[:, g.x]
        return pltpu.make_async_copy(bounce[a], o, sems.ls.at[a])
    def each(fn):
        for a in range(len(ins)):
            if kinds[a] == SINGLE:
                @pl.when(g.z == g.slot)
                def _(): fn(a)
            else: fn(a)
    def turn(a):
        inside(a).wait()
        outside(a).start()
    return (lambda: each(lambda a: inside(a).start())), (lambda: each(turn)), (lambda: each(lambda a: outside(a).wait()))


def gather_kernel(plan, nin, *refs):
    ins = refs[:nin]
    outs = refs[nin : 2 * nin]
    bounce = refs[2 * nin : 3 * nin]
    zs, zr, xs, xr, ys, yr, cs, cr, ls = refs[3 * nin :]
    sems = NS(zs=zs, zr=zr, xs=xs, xr=xr, ys=ys, yr=yr, cs=cs, cr=cr, ls=ls)
    g = Gather(gather_chunks(plan, ins, outs), sems)
    gather_enter(g)
    st = g.steps()
    next(st)
    own_start, own_turn, own_wait = gather_own(g, plan, ins, outs, bounce, sems)
    own_start()
    own_turn()
    next(st)
    own_wait()
    for _ in st: pass
    for t in range(len(plan)): g.finish(t)
    for t in range(len(plan)): g.drain(t)


def gather_shapes(arrs, kinds):
    outs = []
    bounce = []
    for a, k in zip(arrs, kinds):
        bounce.append(pltpu.VMEM(a.shape[:2] + a.shape[3:] if k == SHARED else a.shape, a.dtype))
        if k == SHARED: s = (4, 2) + a.shape
        elif k == PRIVATE: s = (a.shape[0], 4, 2) + a.shape[1:]
        elif k == ZONLY: s = (a.shape[0], 4) + a.shape[1:]
        else: s = (a.shape[0], 2) + a.shape[1:]
        outs.append(jax.ShapeDtypeStruct(s, a.dtype))
    return outs, bounce


def gather_all(arrs, kinds, plan, cid, name):
    outs, bounce = gather_shapes(arrs, kinds)
    hbm = pl.BlockSpec(memory_space=pl.ANY)
    return pl.pallas_call(
        functools.partial(gather_kernel, plan, len(arrs)),
        out_shape=outs,
        in_specs=[hbm] * len(arrs),
        out_specs=[hbm] * len(outs),
        scratch_shapes=bounce + gather_sems(plan, len(arrs)),
        compiler_params=pltpu.CompilerParams(collective_id=cid, has_side_effects=True, vmem_limit_bytes=40 * 2**20),
        name=name,
    )(*arrs)


DIM = 768
SPR = 2


class Reduce:
    def __init__(self, chunks):
        self.ch = chunks
        dp = lax.axis_index(DP); slot = lax.axis_index(SLOT)
        self.dp, self.slot = dp, slot
        self.z, self.x = dp // 2, dp % 2
        self.y, self.c = slot // 2, slot % 2
        self.xdev = (self.z * 2 + 1 - self.x, slot)
        self.ydev = (dp, (1 - self.y) * 2 + self.c)
        self.cdev = (dp, self.y * 2 + 1 - self.c)
        self.ycdev = (dp, (1 - self.y) * 2 + 1 - self.c)
    def zdev(self, k): return (((self.z + k) % 4) * 2 + self.x, self.slot)
    def peers(self): return [self.xdev, self.ydev, self.cdev, self.ycdev, self.zdev(1), self.zdev(2), self.zdev(3)]
    def cp(self, src, dst, sems, i, dev):
        return pltpu.make_async_remote_copy(src_ref=src, dst_ref=dst, send_sem=sems[0].at[i], recv_sem=sems[1].at[i], device_id=dev, device_id_type=MESH)
    def ccopy(self, k): return self.cp(k.g(1 - self.c), k.rc, k.sem, 0, self.cdev)
    def load(self, k): return pltpu.make_async_copy(k.g(self.c) if k.kind == SHARED else k.g, k.own, k.lsem.at[0])
    def ycopy(self, k): return self.cp(k.own.at[:, :, 1 - self.y], k.ry, k.sem, 1, self.ydev)
    def cur(self, k, oz, ox):
        return k.own.at[oz, ox, self.y] if k.kind == SHARED else k.own.at[oz, ox]
    def xcopy(self, k):
        src = k.own.at[:, 1 - self.x, self.y] if k.kind == SHARED else k.own.at[:, 1 - self.x]
        return self.cp(src, k.rx, k.sem, 2, self.xdev)
    def zcopy(self, k, d):
        return self.cp(self.cur(k, (self.z + d) % 4, self.x), k.rz.at[d - 1], k.sem, 2 + d, self.zdev(d))
    def fcopy(self, k, i):
        y, c = self.y, self.c
        if i == 0: return self.cp(k.fin, k.out(y, c), k.sem, 6, self.ydev)
        if i == 1: return self.cp(k.fin, k.out(y, c), k.sem, 7, self.cdev)
        return self.cp(k.out(1 - y, c), k.out(1 - y, c), k.sem, 8, self.cdev)
    def put(self, k): return pltpu.make_async_copy(k.fin, k.out(self.y, self.c), k.lsem.at[1])
    def s0(self, k):
        self.load(k).start()
        if k.kind == SHARED: self.ccopy(k).start()
    def s1(self, k):
        self.load(k).wait()
        if k.kind != SHARED: return
        self.ccopy(k).wait_recv()
        own, rc = k.own, k.rc
        @pl.loop(0, 4)
        def _(i):
            own[i] = own[i] + rc[i]
        self.ycopy(k).start()
    def s2(self, k):
        if k.kind == SHARED:
            self.ycopy(k).wait_recv()
            own, ry = k.own, k.ry
            @pl.loop(0, 4)
            def _(i):
                own[i, :, self.y] = own[i, :, self.y] + ry[i]
        self.xcopy(k).start()
    def s3(self, k):
        self.xcopy(k).wait_recv()
        rx = k.rx
        @pl.loop(0, 4)
        def _(i):
            r = self.cur(k, i, self.x)
            r[...] = r[...] + rx[i]
        for d in (1, 3, 2): self.zcopy(k, d).start()
    def s4(self, k):
        for d in (1, 3, 2): self.zcopy(k, d).wait_recv()
        rz = k.rz; f = jnp.float32
        k.fin[...] = (self.cur(k, self.z, self.x)[...].astype(f) + rz[0].astype(f) + rz[1].astype(f) + rz[2].astype(f)).astype(jnp.bfloat16)
        self.put(k).start()
        self.fcopy(k, 0).start(); self.fcopy(k, 1).start()
    def s5(self, k):
        self.fcopy(k, 0).wait_recv()
        self.fcopy(k, 2).start()
    def s6(self, k):
        self.fcopy(k, 1).wait_recv(); self.fcopy(k, 2).wait_recv()
        if k.kind == SHARED: self.ccopy(k).wait_send(); self.ycopy(k).wait_send()
        self.xcopy(k).wait_send()
        for d in (1, 2, 3): self.zcopy(k, d).wait_send()
        for i in range(3): self.fcopy(k, i).wait_send()
        self.put(k).wait()
    def steps(self):
        n = len(self.ch)
        for k in self.ch: self.s0(k)
        yield
        st = [self.s1, self.s2, self.s3, self.s4, self.s5]
        for i in range(n + SPR * 4):
            for q, fn in enumerate(st):
                t = i - SPR * q
                if 0 <= t < n: fn(self.ch[t])
            yield
        for k in self.ch: self.s6(k)

class Mixer:
    def __init__(self, r, g, own, rx, rz, fin, out, ss, rs, ls):
        self.r, self.g, self.own, self.rx, self.rz, self.fin, self.out, self.ss, self.rs, self.ls = r, g, own, rx, rz, fin, out, ss, rs, ls
    def xc(self):
        r = self.r
        return r.cp(self.own.at[1 - r.x], self.rx, (self.ss, self.rs), 0, r.xdev)
    def zc(self, d):
        r = self.r
        return r.cp(self.own.at[r.x], self.rz.at[d - 1], (self.ss, self.rs), d, (r.slot * 2 + r.x, r.slot))
    def bc(self, i):
        r = self.r
        return r.cp(self.fin, self.out, (self.ss, self.rs), 4 + i, (r.ydev, r.cdev, r.ycdev)[i])
    def steps(self):
        r = self.r
        ld = pltpu.make_async_copy(self.g, self.own, self.ls.at[0])
        ld.start(); ld.wait()
        self.xc().start(); yield
        self.xc().wait_recv()
        self.own[r.x] = self.own[r.x] + self.rx[...]
        for d in (1, 2, 3):
            @pl.when((r.z + d) % 4 == r.slot)
            def _(): self.zc(d).start()
        yield; yield; yield
        put = pltpu.make_async_copy(self.fin, self.out, self.ls.at[1])
        @pl.when(r.z == r.slot)
        def _():
            f = jnp.float32
            for d in (1, 2, 3): self.zc(d).wait_recv()
            self.fin[...] = (self.own[r.x].astype(f) + self.rz[0].astype(f) + self.rz[1].astype(f) + self.rz[2].astype(f)).astype(jnp.bfloat16)
            put.start()
            for i in range(3): self.bc(i).start()
        yield; yield
        self.xc().wait_send()
        for d in (1, 2, 3):
            @pl.when((r.z + d) % 4 == r.slot)
            def _(): self.zc(d).wait_send()
        @pl.when(r.z == r.slot)
        def _():
            for i in range(3): self.bc(i).wait_send()
            put.wait()
        for i, s in enumerate((r.ydev[1], r.cdev[1], r.ycdev[1])):
            @pl.when(r.z == s)
            def _(): self.bc(i).wait_recv()

def reduce_kernel(plan, nin, *refs):
    ins = refs[:nin]; outs = refs[nin:2 * nin]; rest = list(refs[2 * nin:])
    ns = sum(p[1] == SHARED for p in plan); npv = len(plan) - ns
    take = lambda: rest.pop(0)
    s_own, s_rc, s_ry, s_rx, s_rz, s_fin = (take() for _ in range(6))
    pv = [[take() for _ in range(4)] for _ in range(npv)]
    m_own, m_rx, m_rz, m_fin = (take() for _ in range(4))
    ss, rs, ls, mss, mrs, mls = (take() for _ in range(6))
    chunks = []; a = b = 0
    for t, (i, kind, j, cb) in enumerate(plan):
        g, o = ins[i], outs[i]
        if kind == SHARED:
            col = pl.ds(cb * DIM, DIM)
            chunks.append(NS(kind=kind, g=lambda c, g=g, j=j, col=col: g.at[:, :, j, :, c, :, col], out=lambda y, c, o=o, j=j, col=col: o.at[j, y, c, :, col],
                               own=s_own.at[a], rc=s_rc.at[a], ry=s_ry.at[a], rx=s_rx.at[a], rz=s_rz.at[a], fin=s_fin.at[a]))
            a += 1
        else:
            p = pv[b]; b += 1
            chunks.append(NS(kind=kind, g=g.at[j], out=lambda y, c, o=o, j=j: o.at[j, y, c], own=p[0], rx=p[1], rz=p[2], fin=p[3]))
        chunks[-1].sem = (ss.at[t], rs.at[t]); chunks[-1].lsem = ls.at[t]
    r = Reduce(chunks)
    bar = pltpu.get_barrier_semaphore()
    for dev in r.peers(): pl.semaphore_signal(bar, inc=1, device_id=dev, device_id_type=MESH)
    pl.semaphore_wait(bar, 7)
    m = Mixer(r, ins[-1], m_own, m_rx, m_rz, m_fin, outs[-1], mss, mrs, mls)
    g1, g2 = r.steps(), m.steps()
    while True:
        e1 = next(g1, 0); e2 = next(g2, 0)
        if e1 == 0 and e2 == 0: break

def reduce_all(arrs, kinds, plan, mixer):
    outs = []
    for a, k in zip(arrs, kinds):
        outs.append(jax.ShapeDtypeStruct(a.shape[2:] if k == SHARED else (a.shape[0], 2, 2) + a.shape[3:], a.dtype))
    outs.append(jax.ShapeDtypeStruct(mixer.shape[1:], mixer.dtype))
    D = pltpu.SemaphoreType.DMA
    B = jnp.bfloat16
    ns = sum(p[1] == SHARED for p in plan)
    u = 24
    V = lambda *s: pltpu.VMEM(s, B)
    scr = [V(ns, 4, 2, 2, u, DIM), V(ns, 4, 2, 2, u, DIM), V(ns, 4, 2, u, DIM), V(ns, 4, u, DIM), V(ns, 3, u, DIM), V(ns, u, DIM)]
    for (i, k, j, cb) in plan:
        if k != SHARED:
            r, C = arrs[i].shape[3:]
            scr += [V(4, 2, r, C), V(4, r, C), V(3, r, C), V(r, C)]
    r, C = mixer.shape[1:]
    scr += [V(2, r, C), V(r, C), V(3, r, C), V(r, C)]
    T = len(plan)
    scr += [D((T, 9)), D((T, 9)), D((T, 2)), D((7,)), D((7,)), D((2,))]
    al = list(arrs) + [mixer]
    return pl.pallas_call(
        functools.partial(reduce_kernel, plan, len(al)), out_shape=outs,
        in_specs=[pl.BlockSpec(memory_space=pl.ANY)] * len(al),
        out_specs=[pl.BlockSpec(memory_space=pl.ANY)] * len(outs),
        scratch_shapes=scr,
        compiler_params=pltpu.CompilerParams(collective_id=1, has_side_effects=True, vmem_limit_bytes=60 * 2**20),
        name="reduce_grads",
    )(*al)


def sum_kernel(with_x, p_ref, o_ref, rx, s0, rc, s1, ry, fin, rf, ss, rs):
    dp = lax.axis_index(DP)
    slot = lax.axis_index(SLOT)
    z, x, y, c = dp // 2, dp % 2, slot // 2, slot % 2
    xdev = (z * 2 + 1 - x, slot)
    ydev = (dp, (1 - y) * 2 + c)
    cdev = (dp, y * 2 + 1 - c)
    peers = [ydev, cdev] + ([xdev] if with_x else [])
    bar = pltpu.get_barrier_semaphore()
    for d in peers:
        pl.semaphore_signal(bar, inc=1, device_id=d, device_id_type=MESH)
    pl.semaphore_wait(bar, len(peers))

    def rc_(src, dst, i, dev):
        return pltpu.make_async_remote_copy(src_ref=src, dst_ref=dst, send_sem=ss.at[i], recv_sem=rs.at[i], device_id=dev, device_id_type=MESH)

    cps = []
    if with_x:
        a = rc_(p_ref.at[1 - x], rx, 0, xdev)
        a.start()
        a.wait_recv()
        cps.append(a)
        s0[...] = (p_ref[x].astype(F32) + rx[...].astype(F32)).astype(BF)
        base = s0
    else:
        base = p_ref
    b = rc_(base.at[1 - c], rc, 1, cdev)
    b.start()
    b.wait_recv()
    s1[...] = (base[c].astype(F32) + rc[...].astype(F32)).astype(BF)
    d = rc_(s1, ry, 2, ydev)
    d.start()
    d.wait_recv()
    total = (s1[...].astype(F32) + ry[...].astype(F32)).astype(BF)
    fin[...] = total
    e = rc_(fin, rf, 3, cdev)
    e.start()
    o_ref[c] = total.astype(F32)
    e.wait_recv()
    o_ref[1 - c] = rf[...].astype(F32)
    for k in cps + [b, d, e]:
        k.wait_send()


def slot_sum(part, cid, with_x=False):
    rows, width = part.shape[-2] // 2, part.shape[-1]
    shape = part.shape[:-2] + (2, rows, width)
    V = lambda *s: pltpu.VMEM(s, BF)
    D = pltpu.SemaphoreType.DMA
    vm = pl.BlockSpec(memory_space=pltpu.VMEM)
    out = pl.pallas_call(
        functools.partial(sum_kernel, with_x),
        out_shape=jax.ShapeDtypeStruct((2, rows, width), F32),
        in_specs=[vm],
        out_specs=vm,
        scratch_shapes=[V(2, rows, width), V(2, rows, width)] + [V(rows, width)] * 5 + [D((4,)), D((4,))],
        compiler_params=pltpu.CompilerParams(collective_id=cid, has_side_effects=True),
        name="slot_sum",
    )(part.reshape(shape))
    return out.reshape(2 * rows, width)


def slot_gather_kernel(p_ref, o_ref, sy, ss, rs):
    dp = lax.axis_index(DP)
    slot = lax.axis_index(SLOT)
    y, c = slot // 2, slot % 2
    ydev = (dp, (1 - y) * 2 + c)
    cdev = (dp, y * 2 + 1 - c)
    bar = pltpu.get_barrier_semaphore()
    for d in (ydev, cdev):
        pl.semaphore_signal(bar, inc=1, device_id=d, device_id_type=MESH)
    pl.semaphore_wait(bar, 2)

    def rc_(src, dst, i, dev):
        return pltpu.make_async_remote_copy(src_ref=src, dst_ref=dst, send_sem=ss.at[i], recv_sem=rs.at[i], device_id=dev, device_id_type=MESH)

    a = rc_(p_ref, o_ref.at[slot], 0, ydev)
    b = rc_(p_ref, o_ref.at[slot], 1, cdev)
    a.start()
    b.start()
    o_ref[slot] = p_ref[...]
    theirs = o_ref.at[ydev[1]]
    a.wait_recv()
    e = rc_(theirs, theirs, 2, cdev)
    e.start()
    b.wait_recv()
    e.wait_recv()
    for k in (a, b, e):
        k.wait_send()


def slot_gather(part, cid):
    D = pltpu.SemaphoreType.DMA
    vm = pl.BlockSpec(memory_space=pltpu.VMEM)
    out = pl.pallas_call(
        slot_gather_kernel,
        out_shape=jax.ShapeDtypeStruct((4,) + part.shape, part.dtype),
        in_specs=[vm],
        out_specs=vm,
        scratch_shapes=[pltpu.VMEM((8, 128), BF), D((3,)), D((3,))],
        compiler_params=pltpu.CompilerParams(collective_id=cid, has_side_effects=True),
        name="slot_gather",
    )(part)
    return out.reshape(4 * part.shape[0], part.shape[1])


class SlotSum:
    def __init__(self, g, part, rc, s1, ry, fin, rf, ss, rs):
        self.g, self.part, self.rc, self.s1, self.ry, self.fin, self.rf, self.ss, self.rs = g, part, rc, s1, ry, fin, rf, ss, rs
        self.cps = []

    def go(self, src, dst, i, dev):
        k = self.g.cp(src, dst, self.ss.at[i], self.rs.at[i], dev)
        k.start()
        self.cps.append(k)
        return k

    def run(self, value, out, idle=lambda: None):
        g, c = self.g, self.g.c
        rows = value.shape[0] // 2
        self.part[...] = value.astype(BF).reshape(2, rows, value.shape[1])
        b = self.go(self.part.at[1 - c], self.rc, 0, g.cdev)
        b.wait_recv()
        self.s1[...] = (self.part[c].astype(F32) + self.rc[...].astype(F32)).astype(BF)
        d = self.go(self.s1, self.ry, 1, g.ydev)
        idle()
        d.wait_recv()
        total = (self.s1[...].astype(F32) + self.ry[...].astype(F32)).astype(BF)
        self.fin[...] = total
        e = self.go(self.fin, self.rf, 2, g.cdev)
        out[c] = total.astype(F32)
        e.wait_recv()
        out[1 - c] = self.rf[...].astype(F32)

    def drain(self):
        for k in self.cps:
            k.wait_send()
        self.cps = []


def normed(v):
    shifted = v - jnp.mean(v, axis=-1, keepdims=True)
    scale = lax.rsqrt(jnp.mean(shifted * shifted, axis=-1, keepdims=True) + EPSILON)
    return shifted * scale, scale


def dot(a, b, ca=1, cb=0):
    return lax.dot_general(a, b, (((ca,), (cb,)), ((), ())), preferred_element_type=F32)


def gains_kernel_rows(parts):
    rows = lax.broadcasted_iota(jnp.int32, (128, DIM), 0)
    cols = lax.broadcasted_iota(jnp.int32, (128, DIM), 1)
    total = None
    for i in range(8):
        sel = ((cols == rows + i * 96) & (rows < 96)).astype(BF)
        t = dot(parts[i], sel)
        total = t if total is None else total + t
    return total


def softmax_rows(scores, allowed):
    scores = jnp.where(allowed, scores, MASKED)
    e = jnp.exp(scores - jnp.max(scores, axis=-1, keepdims=True))
    return e / jnp.sum(e, axis=-1, keepdims=True)


def head_lanes(width, h):
    lane = lax.broadcasted_iota(jnp.int32, (1, width), 1)
    return (lane >= h * HEAD_DIM) & (lane < (h + 1) * HEAD_DIM)


def forward_kernel(plan, nin, *refs):
    ins = refs[:nin]
    allow_ref = refs[nin]
    outs = refs[nin + 1 : 2 * nin + 1]
    start_o, joined_o, mixture_o, middle_o, expanded_o, patch_o, gains_o = refs[2 * nin + 1 : 2 * nin + 8]
    rest = list(refs[2 * nin + 8 :])
    bounce, rest = rest[:nin], rest[nin:]
    (lookup_v, ids_v, gains_v, proj_v, wh_v, wm_v, wu_v, wd_v) = rest[:8]
    (xp, rx, part, rc, s1, ry, fin, rf) = rest[8:16]
    (xsem, ss, rs, vsem) = rest[16:20]
    zs, zr, xs, xr, ys, yr, cs, cr, ls = rest[20:]
    sems = NS(zs=zs, zr=zr, xs=xs, xr=xr, ys=ys, yr=yr, cs=cs, cr=cr, ls=ls)
    g = Gather(gather_chunks(plan, ins, outs), sems)
    gather_enter(g)
    st = g.steps()
    next(st)
    own_start, own_turn, own_wait = gather_own(g, plan, ins, outs, bounce, sems)
    own_start()
    proj_v[...] = jnp.zeros_like(proj_v)
    own_turn()
    done = [0]

    def pump(n=1):
        for _ in range(n):
            if done[0] < len(plan) + YD:
                next(st)
                done[0] += 1

    pump()
    own_wait()
    where = {}
    for t, p in enumerate(plan):
        where.setdefault(p[0], []).append(t)

    def until(a):
        last = max(where[a])
        kind = plan[last][1]
        need = last + (2 * SP if kind == ZONLY else YD if kind == SHARED else XD) + 1
        pump(max(0, need - done[0]))
        if kind == SHARED:
            for t in where[a]:
                g.finish(t)

    def take(src, dst, i):
        k = pltpu.make_async_copy(src, dst, vsem.at[i])
        k.start()
        return k

    E, I, GN, PJ, PH, PE, PR, PM = range(8)
    until(I)
    k1 = take(outs[I].at[0, g.z], ids_v, 0)
    until(GN)
    k2 = take(outs[GN].at[0], gains_v, 1)
    until(PJ)
    k3 = take(outs[PJ], proj_v.at[:, :, g.x], 2)
    until(E)
    k4 = [take(outs[E].at[:, :, 0, i // 2, i % 2], lookup_v.at[:, :, pl.ds(i * 8, 8), :], 3 + i) for i in range(4)]
    for k in [k1, k2, k3] + k4:
        k.wait()
    gains = gains_kernel_rows(gains_v[...].reshape(8, 16, 128))
    gains_o[...] = gains
    lookup = lookup_v[...].reshape(256, DIM)
    vocab_row = lax.broadcasted_iota(jnp.int32, (256, 128), 0)
    proj = proj_v[...].reshape(2, DIM, DIM)
    for xx in range(2):
        total = None
        for p in range(2):
            hot = (vocab_row == ids_v[xx, pl.ds(g.slot * 2 + p, 1), :]).astype(BF)
            tokens = dot(hot, lookup, 0, 0).astype(BF)
            t = dot(tokens, proj[p])
            total = t if total is None else total + t
        xp[xx] = total.astype(BF)
    kx = g.cp(xp.at[1 - g.x], rx, xsem.at[0], xsem.at[1], g.xdev)
    kx.start()
    until(PH)
    k5 = take(outs[PH].at[0], wh_v, 0)
    kx.wait_recv()
    sums = [SlotSum(g, part.at[i], rc.at[i], s1.at[i], ry.at[i], fin.at[i], rf.at[i], ss.at[i], rs.at[i]) for i in range(3)]
    sums[0].run(xp[g.x].astype(F32) + rx[...].astype(F32), start_o)
    start = start_o[...].reshape(128, DIM)
    norm_one = (normed(start)[0] * gains[0:1]).astype(BF)
    k5.wait()
    joined = dot(norm_one, wh_v[...].reshape(DIM, 576))
    joined_o[...] = joined.astype(BF)
    joined = joined.astype(BF).astype(F32)
    q = joined[:, 0:192].astype(BF)
    k = joined[:, 192:384].astype(BF)
    v = joined[:, 384:576].astype(BF)
    allowed = allow_ref[...] > 0
    mixture = jnp.zeros((128, 192), F32)
    for h in range(3):
        lanes = head_lanes(192, h)
        s = dot(jnp.where(lanes, q, jnp.zeros_like(q)), k, 1, 1) * HEAD_DIM ** (-0.5)
        soft = softmax_rows(s, allowed).astype(BF)
        mixture = jnp.where(lanes, dot(soft, v), mixture)
    mixture = mixture.astype(BF)
    mixture_o[...] = mixture
    until(PM)
    take(outs[PM].at[0], wm_v, 1).wait()
    sums[1].run(dot(mixture, wm_v[...].reshape(192, DIM)), patch_o)
    middle = start + patch_o[...].reshape(128, DIM)
    middle_o[...] = middle
    norm_two = (normed(middle)[0] * gains[1:2]).astype(BF)
    until(PE)
    take(outs[PE].at[0], wu_v, 0).wait()
    expanded = dot(norm_two, wu_v[...].reshape(DIM, DIM))
    expanded_o[...] = expanded
    hidden = gelu_tanh(expanded).astype(BF)
    until(PR)
    take(outs[PR].at[0], wd_v, 1).wait()
    sums[2].run(dot(hidden, wd_v[...].reshape(DIM, DIM)), patch_o)
    patch_o[...] = patch_o[...] + middle.reshape(2, 64, DIM)
    pump(len(plan) + YD)
    for t in range(len(plan)):
        if plan[t][0] != E:
            g.finish(t)
    for t in range(len(plan)):
        g.drain(t)
    kx.wait_send()
    for s in sums:
        s.drain()


def forward_call(arrs, kinds, plan, allow):
    outs, bounce = gather_shapes(arrs, kinds)
    hbm = pl.BlockSpec(memory_space=pl.ANY)
    vm = pl.BlockSpec(memory_space=pltpu.VMEM)
    S = jax.ShapeDtypeStruct
    V = lambda *s: pltpu.VMEM(s, BF)
    D = pltpu.SemaphoreType.DMA
    extra = [S((2, 64, DIM), F32), S((128, 576), BF), S((128, 192), BF), S((128, DIM), F32), S((128, DIM), F32), S((2, 64, DIM), F32), S((16, DIM), F32)]
    scratch = [V(4, 2, 32, DIM), pltpu.VMEM((2, 8, 128), jnp.int32), V(4, 2, 16, 128), V(2, 4, 2, 96, DIM), V(4, 2, 96, 576), V(2, 96, DIM), V(4, 2, 96, DIM), V(4, 2, 96, DIM)]
    scratch += [V(2, 128, DIM), V(128, DIM), V(3, 2, 64, DIM)] + [V(3, 64, DIM)] * 5
    scratch += [D((2,)), D((3, 3)), D((3, 3)), D((7,))]
    return pl.pallas_call(
        functools.partial(forward_kernel, plan, len(arrs)),
        out_shape=outs + extra,
        in_specs=[hbm] * len(arrs) + [vm],
        out_specs=[hbm] * len(outs) + [vm] * len(extra),
        scratch_shapes=bounce + scratch + gather_sems(plan, len(arrs)),
        compiler_params=pltpu.CompilerParams(collective_id=0, has_side_effects=True, vmem_limit_bytes=60 * 2**20),
        name="gather_forward",
    )(*arrs, allow)


def mm(spec, a, b):
    return jnp.einsum(spec, a, b, preferred_element_type=F32)


def local(
    byte_ids,
    seg_ids,
    embed_table,
    slot_project,
    patch_prenorm,
    patch_heads,
    patch_mixer,
    patch_midnorm,
    patch_expand,
    patch_reduce,
    byte_prenorm,
    byte_heads,
    byte_mixer,
    byte_midnorm,
    byte_expand,
    byte_reduce,
    d_output,
):
    dp = lax.axis_index(DP)
    slot = lax.axis_index(SLOT)
    x = dp % 2
    group_rows, patch_len = byte_ids.shape
    own_rows = group_rows // 4
    vocab_part, width = embed_table.shape
    vocab = vocab_part * 8
    share = width // 8
    ff = patch_expand.shape[1]
    quarter = share // 4
    pick = lambda v, axis: lax.dynamic_index_in_dim(v, slot, axis, keepdims=False)
    gains = jnp.stack([patch_prenorm, patch_midnorm, byte_prenorm, byte_midnorm])
    gains = jnp.pad(gains, ((0, 12), (0, 128 - share)))[None]
    heads_own = pick(patch_heads.reshape(share, 3, 4, width // 4), 2).reshape(1, share, 3 * width // 4)
    expand_own = pick(patch_expand.reshape(share, 8, 4, share), 2).reshape(1, share, width)
    reduce_own = pick(patch_reduce.reshape(4, share, width), 0)[None]
    shared = lambda v: v.reshape(v.shape[0] // share, 2, 2, quarter, v.shape[1])
    arrs = [
        embed_table.reshape(1, 2, 2, vocab_part // 4, width), byte_ids.T[None], gains, slot_project,
        heads_own, expand_own, reduce_own, patch_mixer[None],
        shared(byte_heads), shared(byte_mixer), shared(byte_expand), shared(byte_reduce),
    ]
    kinds = [SHARED, PRIVATE, PRIVATE, ZONLY, PRIVATE, PRIVATE, PRIVATE, SINGLE] + [SHARED] * 4
    wide = [(8, SHARED, 0, i * width, width) for i in range(3)] + [(9, SHARED, 0, 0, width)]
    wide += [(10, SHARED, 0, i * width, width) for i in range(4)] + [(11, SHARED, i, 0, width) for i in range(4)]
    plan = [(1, PRIVATE, 0, 0, 0), (2, PRIVATE, 0, 0, 0), (0, SHARED, 0, 0, width)] + wide[:2]
    plan += [(3, ZONLY, 0, 0, 0), (3, ZONLY, 1, 0, 0), (4, PRIVATE, 0, 0, 0)] + wide[2:4] + [(7, SINGLE, 0, 0, 0)]
    plan += wide[4:5] + [(5, PRIVATE, 0, 0, 0)] + wide[5:7] + [(6, PRIVATE, 0, 0, 0)] + wide[7:]
    segments = seg_ids[0]
    pos = jnp.arange(group_rows, dtype=jnp.int32)
    allowed_patch = ((pos[:, None] >= pos[None, :]) & (segments[:, None] == segments[None, :]))[None]
    full = forward_call(arrs, kinds, plan, allowed_patch[0].astype(F32))
    start, joined, mixture, middle, expanded, patch_out, gains_all = full[12:]
    lookup = full[0].reshape(vocab, width)
    ids_all = full[1].reshape(8, patch_len, group_rows)
    p_heads = full[4].reshape(width, 3 * width // 4)
    p_expand = full[5].reshape(width, width)
    p_reduce = full[6].reshape(width, width)
    p_mixer = full[7].reshape(width // 4, width)
    b_heads = full[8].reshape(width, 3 * width)
    b_mixer = full[9].reshape(width, width)
    b_expand = full[10].reshape(width, ff)
    b_reduce = full[11].reshape(ff, width)
    vocab_iota = jnp.arange(vocab, dtype=jnp.int32)
    hot = lambda ids: (ids[..., None] == vocab_iota).astype(BF)
    patch_out = patch_out.reshape(group_rows, width)
    start = start.reshape(group_rows, width)
    heads = 3 * width // 4
    head_count = width // 4 // HEAD_DIM
    norm_one, back_one = jax.vjp(norm_rows, start, gains_all[0])
    norm_one = norm_one.astype(BF)
    joined = joined.reshape(1, group_rows, 3, head_count, HEAD_DIM)
    norm_two, back_two = jax.vjp(norm_rows, middle, gains_all[1])
    norm_two = norm_two.astype(BF)
    hidden, back_gelu = jax.vjp(gelu_tanh, expanded)
    hidden = hidden.astype(BF)
    logsum = attention(joined[:, :, 0], joined[:, :, 1], joined[:, :, 2], allowed_patch)[1]

    first_row = slot * own_rows
    own_out = lax.dynamic_slice_in_dim(patch_out, first_row, own_rows, 0)
    local_bytes = lax.dynamic_slice_in_dim(byte_ids, first_row, own_rows, 0)
    local_onehot = hot(local_bytes)
    local_embed = mm("rpv,vd->rpd", local_onehot, lookup)
    fine_input = local_embed + own_out[:, None, :]
    tile_len = math.gcd(own_rows * patch_len, 128)
    tile_count = own_rows * patch_len // tile_len
    fine_input = fine_input.reshape(tile_count, tile_len, width)
    positions = jnp.arange(tile_len, dtype=jnp.int32)
    allowed_byte = (
        (positions[:, None] >= positions[None, :])
        & (positions[:, None] // patch_len == positions[None, :] // patch_len)
    )[None]

    def attend_byte(queries, keyset, valueset):
        return attention(queries, keyset, valueset, allowed_byte)

    def attend_byte_back(queries, keyset, valueset, kept, d_mixture):
        return attention_back(queries, keyset, valueset, allowed_byte, kept, d_mixture)

    byte_weights = (gains_all[2], b_heads, b_mixer, gains_all[3], b_expand, b_reduce)
    byte_out, byte_saved = block_forward(fine_input, byte_weights, attend_byte)
    out_bytes = byte_out.reshape(own_rows, patch_len, width).astype(BF)
    d_fine, byte_grads = block_backward(
        d_output.astype(F32).reshape(tile_count, tile_len, width), byte_weights, byte_saved, attend_byte_back
    )
    d_fine = d_fine.reshape(own_rows, patch_len, width)

    g_low = slot_gather(jnp.sum(d_fine, axis=1).astype(BF), 7)
    grad = g_low.astype(F32)
    g_reduce = mm("nf,nd->fd", hidden, g_low).astype(BF)
    (d_expanded,) = back_gelu(mm("nd,fd->nf", g_low, p_reduce))
    d_expanded = d_expanded.astype(BF)
    g_expand = mm("nd,nf->df", norm_two, d_expanded).astype(BF)
    d_norm_two = slot_sum(mm("nf,df->nd", d_expanded, p_expand).astype(BF), 5)
    d_middle_part, g_midnorm = back_two(d_norm_two)
    d_middle = grad + d_middle_part
    middle_low = d_middle.astype(BF)
    g_mixer = mm("nf,nd->fd", mixture, middle_low).astype(BF)
    d_mixture = mm("nd,fd->nf", middle_low, p_mixer).astype(BF).reshape(1, group_rows, head_count, HEAD_DIM)
    d_joined = attention_back(joined[:, :, 0], joined[:, :, 1], joined[:, :, 2], allowed_patch, logsum, d_mixture)
    d_joined = jnp.stack(d_joined, axis=2).reshape(group_rows, heads).astype(BF)
    g_heads = mm("nd,nf->df", norm_one, d_joined).astype(BF)
    d_norm_one = slot_sum(mm("nf,df->nd", d_joined, p_heads).astype(BF), 6)
    d_start_part, g_prenorm = back_one(d_norm_one)
    d_start = (d_middle + d_start_part).astype(BF)

    rows_all = gather_all(
        [d_start.reshape(1, 2, 2, group_rows // 4, width)], [SHARED],
        [(0, SHARED, 0, i * (width // 3), width // 3) for i in range(3)], 8, "gather_d_start",
    )[0].reshape(8 * group_rows, width)
    slot_ids = lax.dynamic_slice_in_dim(ids_all, slot * 2, 2, 1).transpose(1, 0, 2).reshape(2, 8 * group_rows)
    by_value = mm("pgv,ge->pve", hot(slot_ids), rows_all).astype(BF)
    lookup_own = lax.dynamic_index_in_dim(lookup.reshape(vocab, 8, share), dp, 1, keepdims=False)
    project_grad = mm("vf,pve->pfe", lookup_own, by_value)
    project_wide = lax.dynamic_update_slice_in_dim(jnp.zeros((2, width, width), BF), slot_project, dp * share, 1)
    table_grad = mm("pve,pfe->vf", by_value, project_wide)
    low_fine = d_fine.astype(BF)
    rest_fine = (d_fine - low_fine.astype(F32)).astype(BF)
    table_grad = table_grad + mm("rpv,rpd->vd", local_onehot, low_fine) + mm("rpv,rpd->vd", local_onehot, rest_fine)

    first = (slot == 0).astype(F32)
    byte_pre, byte_qkv, byte_mix, byte_mid, byte_exp, byte_red = byte_grads
    gain_grads = jnp.stack([g_prenorm * first, g_midnorm * first, byte_pre, byte_mid])
    gain_grads = gain_grads.reshape(4, 8, share).transpose(1, 0, 2).reshape(8, 1, 4 * share)
    gain_grads = jnp.pad(gain_grads, ((0, 0), (0, share - vocab_part - 1), (0, width - 4 * share)))
    misc_grad = jnp.concatenate([table_grad.reshape(8, vocab_part, width), gain_grads], axis=1)
    grouped = lambda v: v.astype(BF).reshape(4, 2, v.shape[0] // width, 2, 2, quarter, v.shape[1])
    private = lambda v: v.reshape(1, 4, 2, share, v.shape[1])
    garr = [
        misc_grad.astype(BF).reshape(4, 2, 1, 2, 2, quarter, width),
        grouped(byte_qkv), grouped(byte_mix), grouped(byte_exp), grouped(byte_red),
        private(g_heads), private(g_expand), private(g_reduce),
    ]
    gkinds = [SHARED] * 5 + [PRIVATE] * 3
    bplan = [(4, SHARED, i, 0) for i in range(4)] + [(3, SHARED, 0, i) for i in range(4)]
    bplan += [(2, SHARED, 0, 0)] + [(1, SHARED, 0, i) for i in range(3)]
    gplan = bplan[:3] + [(7, PRIVATE, 0, 0)] + bplan[3:6] + [(6, PRIVATE, 0, 0)] + bplan[6:9]
    gplan += [(5, PRIVATE, 0, 0)] + bplan[9:] + [(0, SHARED, 0, 0)]
    res = reduce_all(garr, gkinds, gplan, g_mixer.reshape(2, share, width))
    misc_out = res[0].reshape(share, width).astype(F32)
    gain_out = misc_out[vocab_part, : 4 * share].reshape(4, share)
    out_heads = res[5].reshape(4, share, 3, width // 4).transpose(1, 2, 0, 3).reshape(share, 3 * width)
    out_expand = res[6].reshape(4, share, 8, share).transpose(1, 2, 0, 3).reshape(share, ff)
    return (
        out_bytes,
        misc_out[:vocab_part],
        project_grad,
        gain_out[0],
        out_heads.astype(F32),
        res[8].astype(F32),
        gain_out[1],
        out_expand.astype(F32),
        res[7].reshape(4 * share, width).astype(F32),
        gain_out[2],
        res[1].reshape(share, 3 * width).astype(F32),
        res[2].reshape(share, width).astype(F32),
        gain_out[3],
        res[3].reshape(share, ff).astype(F32),
        res[4].reshape(4 * share, width).astype(F32),
    )


def solution(mesh):
    if (mesh.shape[DP], mesh.shape[SLOT]) != (8, 4):
        return generic_solution(mesh)
    placed = (P(DP, None), P(DP, None), P(DP, None), P(SLOT, DP, None)) + (
        P(DP), P(DP, None), P(DP, None), P(DP), P(DP, None), P(DP, None),
    ) * 2 + (P((DP, SLOT), None, None),)
    outs = (P((DP, SLOT), None, None), P(DP, None), P(SLOT, DP, None)) + (
        P(DP), P(DP, None), P(DP, None), P(DP), P(DP, None), P(DP, None),
    ) * 2
    return jax.shard_map(local, mesh=mesh, in_specs=placed, out_specs=outs, check_vma=False)
```

```python
import functools
import math
from types import SimpleNamespace as NS

import jax
import jax.numpy as jnp
from jax import lax
from jax.experimental import pallas as pl
from jax.experimental.pallas import tpu as pltpu
from jax.sharding import PartitionSpec as P

MESH = pl.DeviceIdType.MESH
BF = jnp.bfloat16
F32 = jnp.float32
DP, SLOT = "dp", "slot"
SHARED, PRIVATE, ZONLY, SINGLE, LATE = range(5)

HEAD_DIM = 64


EPSILON = 1e-05
MASKED = -1000000000.0


def norm_rows(values, gain_vec):
    center = jnp.mean(values, axis=-1, keepdims=True)
    shifted = values - center
    spread = jnp.mean(shifted * shifted, axis=-1, keepdims=True)
    return shifted * lax.rsqrt(spread + EPSILON) * gain_vec


def gelu_tanh(values):
    inside = 0.7978845608028654 * (values + 0.044715 * values * values * values)
    return 0.5 * values * (1.0 + jnp.tanh(inside))


def attention(queries, keyset, valueset, allowed):
    scores = jnp.einsum(
        "bnhe,bmhe->bhnm", queries, keyset, preferred_element_type=jnp.float32
    ) * HEAD_DIM ** (-0.5)
    scores = jnp.where(allowed[:, None], scores, MASKED)
    highest = jnp.max(scores, axis=-1, keepdims=True)
    exponents = jnp.exp(scores - highest)
    totals = jnp.sum(exponents, axis=-1, keepdims=True)
    softened = (exponents / totals).astype(jnp.bfloat16)
    mixture = jnp.einsum("bhnm,bmhe->bnhe", softened, valueset, preferred_element_type=jnp.float32)
    return (mixture, highest + jnp.log(totals))


def attention_back(queries, keyset, valueset, allowed, logsum, d_mixture):
    scale_value = HEAD_DIM ** (-0.5)
    scores = (
        jnp.einsum("bnhe,bmhe->bhnm", queries, keyset, preferred_element_type=jnp.float32)
        * scale_value
    )
    scores = jnp.where(allowed[:, None], scores, MASKED)
    softened = jnp.exp(scores - logsum)
    d_soft = jnp.einsum("bnhe,bmhe->bhnm", d_mixture, valueset, preferred_element_type=jnp.float32)
    inside = jnp.sum(d_soft * softened, axis=-1, keepdims=True)
    d_scores = (softened * (d_soft - inside)).astype(jnp.bfloat16)
    d_queries = (
        jnp.einsum("bhnm,bmhe->bnhe", d_scores, keyset, preferred_element_type=jnp.float32)
        * scale_value
    )
    d_keys = (
        jnp.einsum("bhnm,bnhe->bmhe", d_scores, queries, preferred_element_type=jnp.float32)
        * scale_value
    )
    d_values = jnp.einsum(
        "bhnm,bnhe->bmhe",
        softened.astype(jnp.bfloat16),
        d_mixture,
        preferred_element_type=jnp.float32,
    )
    return (d_queries, d_keys, d_values)


def block_forward(values, weights, attend):
    gain_one, w_heads, w_mixer, gain_two, w_expand, w_reduce = weights
    batch, row_count, width = values.shape
    head_count = width // HEAD_DIM
    norm_one, back_one = jax.vjp(norm_rows, values, gain_one.astype(jnp.float32))
    norm_one = norm_one.astype(jnp.bfloat16)
    joined = jnp.einsum(
        "bnd,df->bnf", norm_one, w_heads, preferred_element_type=jnp.float32
    ).astype(jnp.bfloat16)
    joined = joined.reshape(batch, row_count, 3, head_count, HEAD_DIM)
    mixture, kept = attend(joined[:, :, 0], joined[:, :, 1], joined[:, :, 2])
    mixture = mixture.astype(jnp.bfloat16).reshape(batch, row_count, width)
    middle = values + jnp.einsum(
        "bnf,fd->bnd", mixture, w_mixer, preferred_element_type=jnp.float32
    )
    norm_two, back_two = jax.vjp(norm_rows, middle, gain_two.astype(jnp.float32))
    norm_two = norm_two.astype(jnp.bfloat16)
    expanded = jnp.einsum("bnd,df->bnf", norm_two, w_expand, preferred_element_type=jnp.float32)
    hidden, back_gelu = jax.vjp(gelu_tanh, expanded)
    hidden = hidden.astype(jnp.bfloat16)
    result = middle + jnp.einsum(
        "bnf,fd->bnd", hidden, w_reduce, preferred_element_type=jnp.float32
    )
    saved = (back_one, norm_one, joined, kept, mixture, back_two, norm_two, back_gelu, hidden)
    return (result, saved)


def block_backward(grad_out, weights, saved, attend_back):
    gain_one, w_heads, w_mixer, gain_two, w_expand, w_reduce = weights
    back_one, norm_one, joined, kept, mixture, back_two, norm_two, back_gelu, hidden = saved
    batch, row_count, width = grad_out.shape
    grad_low = grad_out.astype(jnp.bfloat16)
    reduce_grad = jnp.einsum("bnf,bnd->fd", hidden, grad_low, preferred_element_type=jnp.float32)
    d_hidden = jnp.einsum("bnd,fd->bnf", grad_low, w_reduce, preferred_element_type=jnp.float32)
    (d_expanded,) = back_gelu(d_hidden)
    d_expanded = d_expanded.astype(jnp.bfloat16)
    expand_grad = jnp.einsum(
        "bnd,bnf->df", norm_two, d_expanded, preferred_element_type=jnp.float32
    )
    d_norm_two = jnp.einsum("bnf,df->bnd", d_expanded, w_expand, preferred_element_type=jnp.float32)
    d_middle_part, midnorm_grad = back_two(d_norm_two)
    d_middle = grad_out + d_middle_part
    middle_low = d_middle.astype(jnp.bfloat16)
    mixer_grad = jnp.einsum("bnf,bnd->fd", mixture, middle_low, preferred_element_type=jnp.float32)
    d_mixture = jnp.einsum(
        "bnd,fd->bnf", middle_low, w_mixer, preferred_element_type=jnp.float32
    ).astype(jnp.bfloat16)
    d_mixture = d_mixture.reshape(batch, row_count, width // HEAD_DIM, HEAD_DIM)
    d_queries, d_keys, d_values = attend_back(
        joined[:, :, 0], joined[:, :, 1], joined[:, :, 2], kept, d_mixture
    )
    d_joined = (
        jnp.stack([d_queries, d_keys, d_values], axis=2)
        .reshape(batch, row_count, 3 * width)
        .astype(jnp.bfloat16)
    )
    heads_grad = jnp.einsum("bnd,bnf->df", norm_one, d_joined, preferred_element_type=jnp.float32)
    d_norm_one = jnp.einsum("bnf,df->bnd", d_joined, w_heads, preferred_element_type=jnp.float32)
    d_input_part, prenorm_grad = back_one(d_norm_one)
    return (
        d_middle + d_input_part,
        (prenorm_grad, heads_grad, mixer_grad, midnorm_grad, expand_grad, reduce_grad),
    )


def generic_local(
    byte_ids,
    seg_ids,
    embed_table,
    slot_project,
    patch_prenorm,
    patch_heads,
    patch_mixer,
    patch_midnorm,
    patch_expand,
    patch_reduce,
    byte_prenorm,
    byte_heads,
    byte_mixer,
    byte_midnorm,
    byte_expand,
    byte_reduce,
    d_output,
):
    slot_count = lax.axis_size(SLOT)
    slot_index = lax.axis_index(SLOT)
    group_rows = byte_ids.shape[0]
    own_rows = group_rows // slot_count
    patch_len = byte_ids.shape[1]
    slot_share = patch_len // slot_count
    gathered = (
        lax.all_gather(embed_table, DP, axis=0, tiled=True),
        lax.all_gather(slot_project, DP, axis=1, tiled=True),
        lax.all_gather(patch_prenorm, DP, axis=0, tiled=True),
        lax.all_gather(patch_heads, DP, axis=0, tiled=True),
        lax.all_gather(patch_mixer, DP, axis=0, tiled=True),
        lax.all_gather(patch_midnorm, DP, axis=0, tiled=True),
        lax.all_gather(patch_expand, DP, axis=0, tiled=True),
        lax.all_gather(patch_reduce, DP, axis=0, tiled=True),
        lax.all_gather(byte_prenorm, DP, axis=0, tiled=True),
        lax.all_gather(byte_heads, DP, axis=0, tiled=True),
        lax.all_gather(byte_mixer, DP, axis=0, tiled=True),
        lax.all_gather(byte_midnorm, DP, axis=0, tiled=True),
        lax.all_gather(byte_expand, DP, axis=0, tiled=True),
        lax.all_gather(byte_reduce, DP, axis=0, tiled=True),
    )
    lookup = gathered[0]
    project = gathered[1]
    patch_weights = gathered[2:8]
    byte_weights = gathered[8:14]
    vocab_size = lookup.shape[0]
    width = lookup.shape[1]
    head_count = width // HEAD_DIM
    vocab_iota = jnp.arange(vocab_size, dtype=jnp.int32)
    slot_bytes = lax.dynamic_slice_in_dim(byte_ids, slot_index * slot_share, slot_share, 1)
    slot_onehot = (slot_bytes[:, :, None] == vocab_iota).astype(jnp.bfloat16)
    slot_embed = jnp.einsum(
        "gpv,vd->gpd", slot_onehot, lookup, preferred_element_type=jnp.float32
    ).astype(jnp.bfloat16)
    rows_embed = slot_embed
    patch_start = lax.psum_scatter(
        jnp.einsum("cpd,pde->ce", rows_embed, project, preferred_element_type=jnp.float32).astype(
            jnp.bfloat16
        ),
        SLOT,
        scatter_dimension=0,
        tiled=True,
    ).astype(jnp.float32)
    segments = seg_ids[0]
    first_row = slot_index * own_rows
    query_pos = first_row + jnp.arange(own_rows, dtype=jnp.int32)
    key_pos = jnp.arange(group_rows, dtype=jnp.int32)
    query_seg = lax.dynamic_slice_in_dim(segments, first_row, own_rows, 0)
    allowed_patch = (
        (query_pos[:, None] >= key_pos[None, :]) & (query_seg[:, None] == segments[None, :])
    )[None]

    def attend_patch(queries, keyset, valueset):
        all_keys, all_values = (
            lax.all_gather(keyset.reshape(own_rows, width), SLOT, axis=0, tiled=True),
            lax.all_gather(valueset.reshape(own_rows, width), SLOT, axis=0, tiled=True),
        )
        all_keys = all_keys.reshape(1, group_rows, head_count, HEAD_DIM)
        all_values = all_values.reshape(1, group_rows, head_count, HEAD_DIM)
        mixture, logsum = attention(queries, all_keys, all_values, allowed_patch)
        return (mixture, (all_keys, all_values, logsum))

    def attend_patch_back(queries, keyset, valueset, kept, d_mixture):
        all_keys, all_values, logsum = kept
        d_queries, d_keys, d_values = attention_back(
            queries, all_keys, all_values, allowed_patch, logsum, d_mixture
        )
        own_keys, own_values = (
            lax.psum_scatter(
                d_keys.reshape(group_rows, width).astype(jnp.bfloat16),
                SLOT,
                scatter_dimension=0,
                tiled=True,
            ).astype(jnp.float32),
            lax.psum_scatter(
                d_values.reshape(group_rows, width).astype(jnp.bfloat16),
                SLOT,
                scatter_dimension=0,
                tiled=True,
            ).astype(jnp.float32),
        )
        return (d_queries, own_keys.reshape(keyset.shape), own_values.reshape(valueset.shape))

    patch_out, patch_saved = block_forward(patch_start[None], patch_weights, attend_patch)
    local_bytes = lax.dynamic_slice_in_dim(byte_ids, first_row, own_rows, 0)
    local_onehot = (local_bytes[:, :, None] == vocab_iota).astype(jnp.bfloat16)
    local_embed = jnp.einsum(
        "rpv,vd->rpd", local_onehot, lookup, preferred_element_type=jnp.float32
    )
    fine_input = local_embed + patch_out[0][:, None, :]
    tile_len = math.gcd(own_rows * patch_len, 128)
    tile_count = own_rows * patch_len // tile_len
    fine_input = fine_input.reshape(tile_count, tile_len, width)
    positions = jnp.arange(tile_len, dtype=jnp.int32)
    allowed_byte = (
        (positions[:, None] >= positions[None, :])
        & (positions[:, None] // patch_len == positions[None, :] // patch_len)
    )[None]

    def attend_byte(queries, keyset, valueset):
        return attention(queries, keyset, valueset, allowed_byte)

    def attend_byte_back(queries, keyset, valueset, kept, d_mixture):
        return attention_back(queries, keyset, valueset, allowed_byte, kept, d_mixture)

    byte_out, byte_saved = block_forward(fine_input, byte_weights, attend_byte)
    out_bytes = byte_out.reshape(own_rows, patch_len, width).astype(jnp.bfloat16)
    d_fine, byte_grads = block_backward(
        d_output.astype(jnp.float32).reshape(tile_count, tile_len, width),
        byte_weights,
        byte_saved,
        attend_byte_back,
    )
    d_fine = d_fine.reshape(own_rows, patch_len, width)
    d_patch = jnp.sum(d_fine, axis=1)[None]
    d_start, patch_grads = block_backward(d_patch, patch_weights, patch_saved, attend_patch_back)
    embed_local = jnp.einsum(
        "rpv,rpd->vd", local_onehot.astype(jnp.float32), d_fine, precision=lax.Precision.HIGHEST
    )
    portion = lax.all_gather(d_start[0].astype(jnp.bfloat16), SLOT, axis=0, tiled=True)
    rows_embed = slot_embed
    rows_hot = slot_onehot.astype(jnp.float32)
    proj_sum = jnp.einsum("cpd,ce->pde", rows_embed, portion, preferred_element_type=jnp.float32)
    d_rows = jnp.einsum("ce,pde->cpd", portion, project, preferred_element_type=jnp.float32)
    table_sum = jnp.einsum("cpv,cpd->vd", rows_hot, d_rows, precision=lax.Precision.HIGHEST)
    table_grad = embed_local + table_sum
    patch_pre, patch_qkv_grad, patch_mix, patch_mid, patch_exp, patch_red = patch_grads
    byte_pre, byte_qkv_grad, byte_mix, byte_mid, byte_exp, byte_red = byte_grads
    reduced = (
        lax.psum_scatter(table_grad, DP, scatter_dimension=0, tiled=True),
        lax.psum_scatter(patch_pre, DP, scatter_dimension=0, tiled=True),
        lax.psum_scatter(patch_qkv_grad, DP, scatter_dimension=0, tiled=True),
        lax.psum_scatter(patch_mix, DP, scatter_dimension=0, tiled=True),
        lax.psum_scatter(patch_mid, DP, scatter_dimension=0, tiled=True),
        lax.psum_scatter(patch_exp, DP, scatter_dimension=0, tiled=True),
        lax.psum_scatter(patch_red, DP, scatter_dimension=0, tiled=True),
        lax.psum_scatter(byte_pre, DP, scatter_dimension=0, tiled=True),
        lax.psum_scatter(byte_qkv_grad, DP, scatter_dimension=0, tiled=True),
        lax.psum_scatter(byte_mix, DP, scatter_dimension=0, tiled=True),
        lax.psum_scatter(byte_mid, DP, scatter_dimension=0, tiled=True),
        lax.psum_scatter(byte_exp, DP, scatter_dimension=0, tiled=True),
        lax.psum_scatter(byte_red, DP, scatter_dimension=0, tiled=True),
        lax.psum_scatter(proj_sum, DP, scatter_dimension=1, tiled=True),
    )
    shares = (
        lax.psum_scatter(
            reduced[0].astype(jnp.bfloat16), SLOT, scatter_dimension=0, tiled=True
        ).astype(jnp.float32),
        lax.psum_scatter(
            reduced[1].astype(jnp.bfloat16), SLOT, scatter_dimension=0, tiled=True
        ).astype(jnp.float32),
        lax.psum_scatter(
            reduced[2].astype(jnp.bfloat16), SLOT, scatter_dimension=0, tiled=True
        ).astype(jnp.float32),
        lax.psum_scatter(
            reduced[3].astype(jnp.bfloat16), SLOT, scatter_dimension=0, tiled=True
        ).astype(jnp.float32),
        lax.psum_scatter(
            reduced[4].astype(jnp.bfloat16), SLOT, scatter_dimension=0, tiled=True
        ).astype(jnp.float32),
        lax.psum_scatter(
            reduced[5].astype(jnp.bfloat16), SLOT, scatter_dimension=0, tiled=True
        ).astype(jnp.float32),
        lax.psum_scatter(
            reduced[6].astype(jnp.bfloat16), SLOT, scatter_dimension=0, tiled=True
        ).astype(jnp.float32),
        lax.psum_scatter(
            reduced[7].astype(jnp.bfloat16), SLOT, scatter_dimension=0, tiled=True
        ).astype(jnp.float32),
        lax.psum_scatter(
            reduced[8].astype(jnp.bfloat16), SLOT, scatter_dimension=0, tiled=True
        ).astype(jnp.float32),
        lax.psum_scatter(
            reduced[9].astype(jnp.bfloat16), SLOT, scatter_dimension=0, tiled=True
        ).astype(jnp.float32),
        lax.psum_scatter(
            reduced[10].astype(jnp.bfloat16), SLOT, scatter_dimension=0, tiled=True
        ).astype(jnp.float32),
        lax.psum_scatter(
            reduced[11].astype(jnp.bfloat16), SLOT, scatter_dimension=0, tiled=True
        ).astype(jnp.float32),
        lax.psum_scatter(
            reduced[12].astype(jnp.bfloat16), SLOT, scatter_dimension=0, tiled=True
        ).astype(jnp.float32),
    )
    summed = (
        lax.all_gather(shares[0].astype(jnp.bfloat16), SLOT, axis=0, tiled=True).astype(
            jnp.float32
        ),
        lax.all_gather(shares[1].astype(jnp.bfloat16), SLOT, axis=0, tiled=True).astype(
            jnp.float32
        ),
        lax.all_gather(shares[2].astype(jnp.bfloat16), SLOT, axis=0, tiled=True).astype(
            jnp.float32
        ),
        lax.all_gather(shares[3].astype(jnp.bfloat16), SLOT, axis=0, tiled=True).astype(
            jnp.float32
        ),
        lax.all_gather(shares[4].astype(jnp.bfloat16), SLOT, axis=0, tiled=True).astype(
            jnp.float32
        ),
        lax.all_gather(shares[5].astype(jnp.bfloat16), SLOT, axis=0, tiled=True).astype(
            jnp.float32
        ),
        lax.all_gather(shares[6].astype(jnp.bfloat16), SLOT, axis=0, tiled=True).astype(
            jnp.float32
        ),
        lax.all_gather(shares[7].astype(jnp.bfloat16), SLOT, axis=0, tiled=True).astype(
            jnp.float32
        ),
        lax.all_gather(shares[8].astype(jnp.bfloat16), SLOT, axis=0, tiled=True).astype(
            jnp.float32
        ),
        lax.all_gather(shares[9].astype(jnp.bfloat16), SLOT, axis=0, tiled=True).astype(
            jnp.float32
        ),
        lax.all_gather(shares[10].astype(jnp.bfloat16), SLOT, axis=0, tiled=True).astype(
            jnp.float32
        ),
        lax.all_gather(shares[11].astype(jnp.bfloat16), SLOT, axis=0, tiled=True).astype(
            jnp.float32
        ),
        lax.all_gather(shares[12].astype(jnp.bfloat16), SLOT, axis=0, tiled=True).astype(
            jnp.float32
        ),
    )
    proj_final = reduced[13]
    return (
        out_bytes,
        summed[0],
        proj_final,
        summed[1],
        summed[2],
        summed[3],
        summed[4],
        summed[5],
        summed[6],
        summed[7],
        summed[8],
        summed[9],
        summed[10],
        summed[11],
        summed[12],
    )


def generic_solution(mesh):
    placed = (
        P(DP, None),
        P(DP, None),
        P(DP, None),
        P(SLOT, DP, None),
        P(DP),
        P(DP, None),
        P(DP, None),
        P(DP),
        P(DP, None),
        P(DP, None),
        P(DP),
        P(DP, None),
        P(DP, None),
        P(DP),
        P(DP, None),
        P(DP, None),
        P((DP, SLOT), None, None),
    )
    return jax.shard_map(
        generic_local,
        mesh=mesh,
        in_specs=placed,
        out_specs=(
            P((DP, SLOT), None, None),
            P(DP, None),
            P(SLOT, DP, None),
            P(DP),
            P(DP, None),
            P(DP, None),
            P(DP),
            P(DP, None),
            P(DP, None),
            P(DP),
            P(DP, None),
            P(DP, None),
            P(DP),
            P(DP, None),
            P(DP, None),
        ),
        check_vma=False,
    )


W, SP = 4, 2
XD = 3 * SP
YD = XD + SP


class Gather:
    def __init__(self, chunks, sems):
        self.ch = chunks
        self.s = sems
        dp = lax.axis_index(DP); slot = lax.axis_index(SLOT)
        self.dp, self.slot = dp, slot
        self.z, self.x = dp // 2, dp % 2
        self.y, self.c = slot // 2, slot % 2
        self.xdev = (self.z * 2 + 1 - self.x, slot)
        self.ydev = (dp, (1 - self.y) * 2 + self.c)
        self.cdev = (dp, self.y * 2 + 1 - self.c)
        self.sent = []
    def zdev(self, d): return ((self.z + d) * 2 + self.x, self.slot)
    def barrier_peers(self):
        z = self.z
        return [(None, self.xdev), (None, self.ydev), (None, self.cdev), (z > 0, self.zdev(-1)), (z < 3, self.zdev(1))]
    def cp(self, src, dst, ss, rs, dev):
        return pltpu.make_async_remote_copy(src_ref=src, dst_ref=dst, send_sem=ss, recv_sem=rs, device_id=dev, device_id_type=MESH)
    def send(self, pred, *a):
        if pred is None: self.cp(*a).start()
        else:
            @pl.when(pred)
            def _(): self.cp(*a).start()
    def reg(self, t, oz, ox, y, c):
        k = self.ch[t]
        return k.dst(oz, ox, y, c)
    def start(self, t):
        k = self.ch[t]; z, x, y, c = self.z, self.x, self.y, self.c
        zs, zr, xs, xr = self.s.zs, self.s.zr, self.s.xs, self.s.xr
        src = k.src(y, c); dst = self.reg(t, z, x, y, c)
        one = k.kind == SINGLE
        mine = z == self.slot
        self.send((z < 3) & mine if one else z < 3, src, dst, zs.at[t, 0, z], zr.at[t, z], self.zdev(1))
        self.send((z > 0) & mine if one else z > 0, src, dst, zs.at[t, 1, z], zr.at[t, z], self.zdev(-1))
        if k.kind != ZONLY:
            self.send(mine if one else None, src, dst, xs.at[t, 0], xr.at[t, 0], self.xdev)
    def wait(self, ref, rs, ss):
        self.cp(ref, ref, ss, rs, (self.dp, self.slot)).wait_recv()
    def zarr(self, t, d):
        k = self.ch[t]; z, x, y, c = self.z, self.x, self.y, self.c; S = self.s
        for side in (-1, 1):
            oz = z + side * d
            ok = oz == self.slot if k.kind == SINGLE else (oz >= 0) & (oz <= 3)
            nxt = -side
            nok = (z + nxt >= 0) & (z + nxt <= 3)
            @pl.when(ok)
            def _():
                r = self.reg(t, oz, x, y, c)
                self.wait(r, S.zr.at[t, oz], S.zs.at[t, 0, z])
                if d < 3:
                    @pl.when(nok)
                    def _(): self.cp(r, r, S.zs.at[t, 0 if nxt == 1 else 1, oz], S.zr.at[t, oz], self.zdev(nxt)).start()
                if k.kind != ZONLY:
                    self.cp(r, r, S.xs.at[t, 0], S.xr.at[t, 0], self.xdev).start()
                if k.kind == SHARED:
                    q = k.pos
                    self.cp(r, r, S.ys.at[q, 0], S.yr.at[q, 0], self.ydev).start()
    def xarr(self, t):
        k = self.ch[t]; x, y, c = self.x, self.y, self.c; S = self.s
        if k.kind == ZONLY: return
        r = k.xall(1 - x, y, c)
        self.wait(r, S.xr.at[t, 0], S.xs.at[t, 0])
        if k.kind == SHARED:
            q = k.pos
            self.cp(r, r, S.ys.at[q, 1], S.yr.at[q, 1], self.ydev).start()
            r = k.all(y, c)
            self.cp(r, r, S.cs.at[q, 0], S.cr.at[q, 0], self.cdev).start()
    def yarr(self, t):
        k = self.ch[t]; x, y, c = self.x, self.y, self.c; S = self.s
        if k.kind != SHARED: return
        q = k.pos
        self.wait(k.three(1 - y, c), S.yr.at[q, 0], S.ys.at[q, 0])
        self.wait(k.xall(1 - x, 1 - y, c), S.yr.at[q, 1], S.ys.at[q, 1])
        r = k.all(1 - y, c)
        self.cp(r, r, S.cs.at[q, 1], S.cr.at[q, 1], self.cdev).start()
    def finish(self, t):
        k = self.ch[t]; y, c = self.y, self.c; S = self.s
        if k.kind != SHARED: return
        q = k.pos
        for h in (0, 1):
            self.wait(k.all(y if h == 0 else 1 - y, 1 - c), S.cr.at[q, h], S.cs.at[q, h])
    def drain(self, t):
        k = self.ch[t]; z, x, y, c = self.z, self.x, self.y, self.c; S = self.s
        r = self.reg(t, z, x, y, c)
        def ws(ss, r): self.cp(r, r, ss, ss, (self.dp, self.slot)).wait_send()
        if k.kind == SINGLE:
            @pl.when((z < 3) & (self.slot <= z))
            def _(): ws(S.zs.at[t, 0, self.slot], r)
            @pl.when((z > 0) & (self.slot >= z))
            def _(): ws(S.zs.at[t, 1, self.slot], r)
        else:
            for i in range(4):
                @pl.when((z < 3) & (i <= z))
                def _(): ws(S.zs.at[t, 0, i], r)
                @pl.when((z > 0) & (i >= z))
                def _(): ws(S.zs.at[t, 1, i], r)
        if k.kind != ZONLY: ws(S.xs.at[t, 0], k.xall(x, y, c))
        if k.kind == SHARED:
            q = k.pos
            ws(S.ys.at[q, 0], k.three(y, c)); ws(S.ys.at[q, 1], k.xall(1 - x, y, c))
            for h in (0, 1): ws(S.cs.at[q, h], k.all(y, c))
    def steps(self):
        n = len(self.ch)
        for t in range(min(W, n)): self.start(t)
        yield
        for i in range(n + YD):
            for d in (1, 2, 3):
                t = i - SP * (d - 1)
                if 0 <= t < n: self.zarr(t, d)
            if i + W < n: self.start(i + W)
            t = i - XD
            if 0 <= t < n: self.xarr(t)
            t = i - YD
            if 0 <= t < n: self.yarr(t)
            yield


def gather_sems(plan, count):
    T = len(plan)
    Q = max(1, sum(p[1] == SHARED for p in plan))
    D = pltpu.SemaphoreType.DMA
    return [D((T, 2, 4)), D((T, 4)), D((T, 1)), D((T, 1)), D((Q, 2)), D((Q, 2)), D((Q, 2)), D((Q, 2)), D((count,))]


def gather_chunks(plan, ins, outs):
    chunks = []
    pos = 0
    for (a, kind, j, c0, cw) in plan:
        i, o = ins[a], outs[a]
        if kind == SHARED:
            col = pl.ds(c0, cw)
            src = lambda y, c, i=i, j=j, col=col: i.at[j, y, c, :, col]
            dst = lambda oz, ox, y, c, o=o, j=j, col=col: o.at[oz, ox, j, y, c, :, col]
            xall = lambda ox, y, c, o=o, j=j, col=col: o.at[:, ox, j, y, c, :, col]
            al = lambda y, c, o=o, j=j, col=col: o.at[:, :, j, y, c, :, col]
            three = lambda y, c, o=o, j=j, col=col: o.at[pl.ds(0, 3), 0, j, y, c, :, col]
            chunks.append(NS(kind=kind, src=src, dst=dst, pos=pos, xall=xall, all=al, three=three))
            pos += 1
            continue
        src = lambda y, c, i=i, j=j: i.at[j]
        if kind == PRIVATE:
            dst = lambda oz, ox, y, c, o=o, j=j: o.at[j, oz, ox]
            xall = lambda ox, y, c, o=o, j=j: o.at[j, :, ox]
        elif kind == ZONLY:
            dst = lambda oz, ox, y, c, o=o, j=j: o.at[j, oz]
            xall = None
        else:
            dst = lambda oz, ox, y, c, o=o, j=j: o.at[j, ox]
            xall = lambda ox, y, c, o=o, j=j: o.at[j, ox]
        chunks.append(NS(kind=kind, src=src, dst=dst, xall=xall))
    return chunks


def gather_enter(g, peers=()):
    bar = pltpu.get_barrier_semaphore()
    for pred, dev in g.barrier_peers():
        def sig(dev=dev): pl.semaphore_signal(bar, inc=1, device_id=dev, device_id_type=MESH)
        if pred is None: sig()
        else: pl.when(pred)(sig)
    inner = (g.z > 0) & (g.z < 3)
    @pl.when(inner)
    def _(): pl.semaphore_wait(bar, 5)
    @pl.when(jnp.logical_not(inner))
    def _(): pl.semaphore_wait(bar, 4)


def gather_own(g, plan, ins, outs, bounce, sems):
    kinds = {p[0]: p[1] for p in plan}
    def inside(a):
        i = ins[a].at[:, :, g.c] if kinds[a] == SHARED else ins[a]
        return pltpu.make_async_copy(i, bounce[a], sems.ls.at[a])
    def outside(a):
        o, kind = outs[a], kinds[a]
        if kind == SHARED: o = o.at[g.z, g.x, :, :, g.c]
        elif kind == PRIVATE: o = o.at[:, g.z, g.x]
        elif kind == ZONLY: o = o.at[:, g.z]
        else: o = o.at[:, g.x]
        return pltpu.make_async_copy(bounce[a], o, sems.ls.at[a])
    def each(fn):
        for a in range(len(ins)):
            if kinds[a] == SINGLE:
                @pl.when(g.z == g.slot)
                def _(): fn(a)
            else: fn(a)
    def turn(a):
        inside(a).wait()
        outside(a).start()
    return (lambda: each(lambda a: inside(a).start())), (lambda: each(turn)), (lambda: each(lambda a: outside(a).wait()))


def gather_shapes(arrs, kinds):
    outs = []
    bounce = []
    for a, k in zip(arrs, kinds):
        bounce.append(pltpu.VMEM(a.shape[:2] + a.shape[3:] if k == SHARED else a.shape, a.dtype))
        if k == SHARED: s = (4, 2) + a.shape
        elif k == PRIVATE: s = (a.shape[0], 4, 2) + a.shape[1:]
        elif k == ZONLY: s = (a.shape[0], 4) + a.shape[1:]
        else: s = (a.shape[0], 2) + a.shape[1:]
        outs.append(jax.ShapeDtypeStruct(s, a.dtype))
    return outs, bounce


DIM = 768
SPR = 2


class Reduce:
    def __init__(self, chunks):
        self.ch = chunks
        dp = lax.axis_index(DP); slot = lax.axis_index(SLOT)
        self.dp, self.slot = dp, slot
        self.z, self.x = dp // 2, dp % 2
        self.y, self.c = slot // 2, slot % 2
        self.xdev = (self.z * 2 + 1 - self.x, slot)
        self.ydev = (dp, (1 - self.y) * 2 + self.c)
        self.cdev = (dp, self.y * 2 + 1 - self.c)
        self.ycdev = (dp, (1 - self.y) * 2 + 1 - self.c)
    def zdev(self, k): return (((self.z + k) % 4) * 2 + self.x, self.slot)
    def peers(self): return [self.xdev, self.ydev, self.cdev, self.ycdev, self.zdev(1), self.zdev(2), self.zdev(3)]
    def cp(self, src, dst, sems, i, dev):
        return pltpu.make_async_remote_copy(src_ref=src, dst_ref=dst, send_sem=sems[0].at[i], recv_sem=sems[1].at[i], device_id=dev, device_id_type=MESH)
    def ccopy(self, k): return self.cp(k.g(1 - self.c), k.rc, k.sem, 0, self.cdev)
    def ycopy(self, k): return self.cp(k.own.at[:, :, 1 - self.y], k.ry, k.sem, 1, self.ydev)
    def cur(self, k, oz, ox):
        return k.own.at[oz, ox] if k.kind == PRIVATE else k.own.at[oz, ox, self.y]
    def xcopy(self, k):
        src = k.own.at[:, 1 - self.x] if k.kind == PRIVATE else k.own.at[:, 1 - self.x, self.y]
        return self.cp(src, k.rx, k.sem, 2, self.xdev)
    def zcopy(self, k, d):
        return self.cp(self.cur(k, (self.z + d) % 4, self.x), k.rz.at[d - 1], k.sem, 2 + d, self.zdev(d))
    def fcopy(self, k, i):
        y, c = self.y, self.c
        if i == 0: return self.cp(k.fin, k.out(y, c), k.sem, 6, self.ydev)
        if i == 1: return self.cp(k.fin, k.out(y, c), k.sem, 7, self.cdev)
        return self.cp(k.out(1 - y, c), k.out(1 - y, c), k.sem, 8, self.cdev)
    def put(self, k): return pltpu.make_async_copy(k.fin, k.out(self.y, self.c), k.lsem.at[1])
    def s0(self, k):
        if k.kind == SHARED:
            pltpu.make_async_copy(k.g(self.c), k.own, k.lsem.at[0]).start()
            self.ccopy(k).start()
    def s1(self, k):
        if k.kind == PRIVATE: return
        own, rc = k.own, k.rc
        if k.kind == SHARED:
            pltpu.make_async_copy(k.g(self.c), k.own, k.lsem.at[0]).wait()
            self.ccopy(k).wait_recv()
            @pl.loop(0, 4)
            def _(i):
                own[i] = own[i] + rc[i]
        else:
            self.ccopy(k).start()
            self.ccopy(k).wait_recv()
            src = k.src
            @pl.loop(0, 4)
            def _(i):
                own[i] = src[i, :, :, self.c] + rc[i]
        self.ycopy(k).start()
    def s2(self, k):
        if k.kind != PRIVATE:
            self.ycopy(k).wait_recv()
            own, ry = k.own, k.ry
            @pl.loop(0, 4)
            def _(i):
                own[i, :, self.y] = own[i, :, self.y] + ry[i]
        self.xcopy(k).start()
    def s3(self, k):
        self.xcopy(k).wait_recv()
        rx = k.rx
        @pl.loop(0, 4)
        def _(i):
            r = self.cur(k, i, self.x)
            r[...] = r[...] + rx[i]
        for d in (1, 3, 2): self.zcopy(k, d).start()
    def s4(self, k):
        for d in (1, 3, 2): self.zcopy(k, d).wait_recv()
        rz = k.rz; f = jnp.float32
        k.fin[...] = (self.cur(k, self.z, self.x)[...].astype(f) + rz[0].astype(f) + rz[1].astype(f) + rz[2].astype(f)).astype(jnp.bfloat16)
        self.put(k).start()
        self.fcopy(k, 0).start(); self.fcopy(k, 1).start()
    def s5(self, k):
        self.fcopy(k, 0).wait_recv()
        self.fcopy(k, 2).start()
    def s6(self, k):
        self.fcopy(k, 1).wait_recv(); self.fcopy(k, 2).wait_recv()
        if k.kind != PRIVATE: self.ccopy(k).wait_send(); self.ycopy(k).wait_send()
        self.xcopy(k).wait_send()
        for d in (1, 2, 3): self.zcopy(k, d).wait_send()
        for i in range(3): self.fcopy(k, i).wait_send()
        self.put(k).wait()
    def steps(self):
        n = len(self.ch)
        for k in self.ch: self.s0(k)
        yield
        st = [self.s1, self.s2, self.s3, self.s4, self.s5]
        for i in range(n + SPR * 4):
            for q, fn in enumerate(st):
                t = i - SPR * q
                if 0 <= t < n: fn(self.ch[t])
            yield
        for k in self.ch: self.s6(k)
    def count(self): return len(self.ch) + SPR * 4

class Mixer:
    def __init__(self, r, g, own, rx, rz, fin, out, ss, rs, ls):
        self.r, self.g, self.own, self.rx, self.rz, self.fin, self.out, self.ss, self.rs, self.ls = r, g, own, rx, rz, fin, out, ss, rs, ls
    def xc(self):
        r = self.r
        return r.cp(self.own.at[1 - r.x], self.rx, (self.ss, self.rs), 0, r.xdev)
    def zc(self, d):
        r = self.r
        return r.cp(self.own.at[r.x], self.rz.at[d - 1], (self.ss, self.rs), d, (r.slot * 2 + r.x, r.slot))
    def bc(self, i):
        r = self.r
        return r.cp(self.fin, self.out, (self.ss, self.rs), 4 + i, (r.ydev, r.cdev, r.ycdev)[i])
    def steps(self):
        r = self.r
        self.xc().start(); yield
        self.xc().wait_recv()
        self.own[r.x] = self.own[r.x] + self.rx[...]
        for d in (1, 2, 3):
            @pl.when((r.z + d) % 4 == r.slot)
            def _(): self.zc(d).start()
        yield; yield; yield
        put = pltpu.make_async_copy(self.fin, self.out, self.ls.at[1])
        @pl.when(r.z == r.slot)
        def _():
            f = jnp.float32
            for d in (1, 2, 3): self.zc(d).wait_recv()
            self.fin[...] = (self.own[r.x].astype(f) + self.rz[0].astype(f) + self.rz[1].astype(f) + self.rz[2].astype(f)).astype(jnp.bfloat16)
            put.start()
            for i in range(3): self.bc(i).start()
        yield; yield
        self.xc().wait_send()
        for d in (1, 2, 3):
            @pl.when((r.z + d) % 4 == r.slot)
            def _(): self.zc(d).wait_send()
        @pl.when(r.z == r.slot)
        def _():
            for i in range(3): self.bc(i).wait_send()
            put.wait()
        for i, s in enumerate((r.ydev[1], r.cdev[1], r.ycdev[1])):
            @pl.when(r.z == s)
            def _(): self.bc(i).wait_recv()

class SlotSum:
    def __init__(self, g, part, rc, s1, ry, fin, rf, ss, rs):
        self.g, self.part, self.rc, self.s1, self.ry, self.fin, self.rf, self.ss, self.rs = g, part, rc, s1, ry, fin, rf, ss, rs
        self.cps = []

    def go(self, src, dst, i, dev):
        k = self.g.cp(src, dst, self.ss.at[i], self.rs.at[i], dev)
        k.start()
        self.cps.append(k)
        return k

    def run(self, value, out, idle=lambda: None):
        g, c = self.g, self.g.c
        rows = value.shape[0] // 2
        self.part[...] = value.astype(BF).reshape(2, rows, value.shape[1])
        b = self.go(self.part.at[1 - c], self.rc, 0, g.cdev)
        b.wait_recv()
        self.s1[...] = (self.part[c].astype(F32) + self.rc[...].astype(F32)).astype(BF)
        d = self.go(self.s1, self.ry, 1, g.ydev)
        idle()
        d.wait_recv()
        total = (self.s1[...].astype(F32) + self.ry[...].astype(F32)).astype(BF)
        self.fin[...] = total
        e = self.go(self.fin, self.rf, 2, g.cdev)
        out[c] = total.astype(F32)
        e.wait_recv()
        out[1 - c] = self.rf[...].astype(F32)

    def drain(self):
        for k in self.cps:
            k.wait_send()
        self.cps = []


def normed(v):
    shifted = v - jnp.mean(v, axis=-1, keepdims=True)
    scale = lax.rsqrt(jnp.mean(shifted * shifted, axis=-1, keepdims=True) + EPSILON)
    return shifted * scale, scale


def dot(a, b, ca=1, cb=0):
    return lax.dot_general(a, b, (((ca,), (cb,)), ((), ())), preferred_element_type=F32)


def gains_kernel_rows(parts):
    rows = lax.broadcasted_iota(jnp.int32, (128, DIM), 0)
    cols = lax.broadcasted_iota(jnp.int32, (128, DIM), 1)
    total = None
    for i in range(8):
        sel = ((cols == rows + i * 96) & (rows < 96)).astype(BF)
        t = dot(parts[i], sel)
        total = t if total is None else total + t
    return total


def softmax_rows(scores, allowed):
    scores = jnp.where(allowed, scores, MASKED)
    e = jnp.exp(scores - jnp.max(scores, axis=-1, keepdims=True))
    return e / jnp.sum(e, axis=-1, keepdims=True)


def head_lanes(width, h):
    lane = lax.broadcasted_iota(jnp.int32, (1, width), 1)
    return (lane >= h * HEAD_DIM) & (lane < (h + 1) * HEAD_DIM)


def forward_kernel(plan, nin, *refs):
    ins = refs[:nin]
    allow_ref = refs[nin]
    outs = refs[nin + 1 : 2 * nin + 1]
    start_o, joined_o, mixture_o, middle_o, expanded_o, patch_o, gains_o = refs[2 * nin + 1 : 2 * nin + 8]
    rest = list(refs[2 * nin + 8 :])
    bounce, rest = rest[:nin], rest[nin:]
    (lookup_v, ids_v, gains_v, proj_v, wh_v, wm_v, wu_v, wd_v) = rest[:8]
    (xp, rx, part, rc, s1, ry, fin, rf) = rest[8:16]
    (xsem, ss, rs, vsem) = rest[16:20]
    zs, zr, xs, xr, ys, yr, cs, cr, ls = rest[20:]
    sems = NS(zs=zs, zr=zr, xs=xs, xr=xr, ys=ys, yr=yr, cs=cs, cr=cr, ls=ls)
    g = Gather(gather_chunks(plan, ins, outs), sems)
    gather_enter(g)
    st = g.steps()
    next(st)
    own_start, own_turn, own_wait = gather_own(g, plan, ins, outs, bounce, sems)
    own_start()
    proj_v[...] = jnp.zeros_like(proj_v)
    own_turn()
    done = [0]

    def pump(n=1):
        for _ in range(n):
            if done[0] < len(plan) + YD:
                next(st)
                done[0] += 1

    pump()
    own_wait()
    where = {}
    for t, p in enumerate(plan):
        where.setdefault(p[0], []).append(t)

    def until(a):
        last = max(where[a])
        kind = plan[last][1]
        need = last + (2 * SP if kind == ZONLY else YD if kind == SHARED else XD) + 1
        pump(max(0, need - done[0]))
        if kind == SHARED:
            for t in where[a]:
                g.finish(t)

    def take(src, dst, i):
        k = pltpu.make_async_copy(src, dst, vsem.at[i])
        k.start()
        return k

    E, I, GN, PJ, PH, PE, PR, PM = range(8)
    until(I)
    k1 = take(outs[I].at[0, g.z], ids_v, 0)
    until(GN)
    k2 = take(outs[GN].at[0], gains_v, 1)
    until(PJ)
    k3 = take(outs[PJ], proj_v.at[:, :, g.x], 2)
    until(E)
    k4 = [take(outs[E].at[:, :, 0, i // 2, i % 2], lookup_v.at[:, :, pl.ds(i * 8, 8), :], 3 + i) for i in range(4)]
    for k in [k1, k2, k3] + k4:
        k.wait()
    gains = gains_kernel_rows(gains_v[...].reshape(8, 16, 128))
    gains_o[...] = gains
    lookup = lookup_v[...].reshape(256, DIM)
    vocab_row = lax.broadcasted_iota(jnp.int32, (256, 128), 0)
    proj = proj_v[...].reshape(2, DIM, DIM)
    for xx in range(2):
        total = None
        for p in range(2):
            hot = (vocab_row == ids_v[xx, pl.ds(g.slot * 2 + p, 1), :]).astype(BF)
            tokens = dot(hot, lookup, 0, 0).astype(BF)
            t = dot(tokens, proj[p])
            total = t if total is None else total + t
        xp[xx] = total.astype(BF)
    kx = g.cp(xp.at[1 - g.x], rx, xsem.at[0], xsem.at[1], g.xdev)
    kx.start()
    until(PH)
    k5 = take(outs[PH].at[0], wh_v, 0)
    kx.wait_recv()
    sums = [SlotSum(g, part.at[i], rc.at[i], s1.at[i], ry.at[i], fin.at[i], rf.at[i], ss.at[i], rs.at[i]) for i in range(3)]
    sums[0].run(xp[g.x].astype(F32) + rx[...].astype(F32), start_o)
    start = start_o[...].reshape(128, DIM)
    norm_one = (normed(start)[0] * gains[0:1]).astype(BF)
    k5.wait()
    joined = dot(norm_one, wh_v[...].reshape(DIM, 576))
    joined_o[...] = joined.astype(BF)
    joined = joined.astype(BF).astype(F32)
    q = joined[:, 0:192].astype(BF)
    k = joined[:, 192:384].astype(BF)
    v = joined[:, 384:576].astype(BF)
    allowed = allow_ref[...] > 0
    mixture = jnp.zeros((128, 192), F32)
    for h in range(3):
        lanes = head_lanes(192, h)
        s = dot(jnp.where(lanes, q, jnp.zeros_like(q)), k, 1, 1) * HEAD_DIM ** (-0.5)
        soft = softmax_rows(s, allowed).astype(BF)
        mixture = jnp.where(lanes, dot(soft, v), mixture)
    mixture = mixture.astype(BF)
    mixture_o[...] = mixture
    until(PM)
    take(outs[PM].at[0], wm_v, 1).wait()
    sums[1].run(dot(mixture, wm_v[...].reshape(192, DIM)), patch_o)
    middle = start + patch_o[...].reshape(128, DIM)
    middle_o[...] = middle
    norm_two = (normed(middle)[0] * gains[1:2]).astype(BF)
    until(PE)
    take(outs[PE].at[0], wu_v, 0).wait()
    expanded = dot(norm_two, wu_v[...].reshape(DIM, DIM))
    expanded_o[...] = expanded
    hidden = gelu_tanh(expanded).astype(BF)
    until(PR)
    take(outs[PR].at[0], wd_v, 1).wait()
    sums[2].run(dot(hidden, wd_v[...].reshape(DIM, DIM)), patch_o)
    patch_o[...] = patch_o[...] + middle.reshape(2, 64, DIM)
    pump(len(plan) + YD)
    for t in range(len(plan)):
        if plan[t][0] != E:
            g.finish(t)
    for t in range(len(plan)):
        g.drain(t)
    kx.wait_send()
    for s in sums:
        s.drain()


def forward_call(arrs, kinds, plan, allow):
    outs, bounce = gather_shapes(arrs, kinds)
    hbm = pl.BlockSpec(memory_space=pl.ANY)
    vm = pl.BlockSpec(memory_space=pltpu.VMEM)
    S = jax.ShapeDtypeStruct
    V = lambda *s: pltpu.VMEM(s, BF)
    D = pltpu.SemaphoreType.DMA
    extra = [S((2, 64, DIM), F32), S((128, 576), BF), S((128, 192), BF), S((128, DIM), F32), S((128, DIM), F32), S((2, 64, DIM), F32), S((16, DIM), F32)]
    scratch = [V(4, 2, 32, DIM), pltpu.VMEM((2, 8, 128), jnp.int32), V(4, 2, 16, 128), V(2, 4, 2, 96, DIM), V(4, 2, 96, 576), V(2, 96, DIM), V(4, 2, 96, DIM), V(4, 2, 96, DIM)]
    scratch += [V(2, 128, DIM), V(128, DIM), V(3, 2, 64, DIM)] + [V(3, 64, DIM)] * 5
    scratch += [D((2,)), D((3, 3)), D((3, 3)), D((7,))]
    return pl.pallas_call(
        functools.partial(forward_kernel, plan, len(arrs)),
        out_shape=outs + extra,
        in_specs=[hbm] * len(arrs) + [vm],
        out_specs=[hbm] * len(outs) + [vm] * len(extra),
        scratch_shapes=bounce + scratch + gather_sems(plan, len(arrs)),
        compiler_params=pltpu.CompilerParams(collective_id=0, has_side_effects=True, vmem_limit_bytes=60 * 2**20),
        name="gather_forward",
    )(*arrs, allow)


def norm_back(d, normal, scale, gain):
    dy = d * gain
    inner = dy - jnp.mean(dy, axis=-1, keepdims=True) - normal * jnp.mean(dy * normal, axis=-1, keepdims=True)
    return scale * inner, jnp.sum(d * normal, axis=0, keepdims=True)


def gelu_slope(v):
    t = jnp.tanh(0.7978845608028654 * (v + 0.044715 * v * v * v))
    return 0.5 * (1.0 + t) + 0.5 * v * (1.0 - t * t) * (0.7978845608028654 * (1.0 + 3 * 0.044715 * v * v))


def backward_kernel(plan, nbyte, *refs):
    rest = list(refs)
    def some(n):
        out = rest[:n]
        del rest[:n]
        return out
    ins = some(nbyte)
    wh_h, wm_h, wu_h, wd_h, ids_h, lookup_h, own_proj_h = some(7)
    (d_ref, start_r, joined_r, mixture_r, middle_r, expanded_r, gains_r, allow_r, table_r, bgain_r) = some(10)
    outs = some(nbyte)
    o_heads, o_expand, o_reduce, o_mixer, o_table, o_gains = some(6)
    (pgrad_o,) = some(1)
    s_own, s_rc, s_ry, s_rx, s_rz, s_fin = some(6)
    pv = [some(4) for _ in range(3)]
    m_own, m_rx, m_rz, m_fin = some(4)
    late = [some(7) for _ in range(2)]
    wh_v, wm_v, wu_v, wd_v, ids_v, lookup_v, lookup_t, projz = some(8)
    gall, part, rc, s1, ry, fin, rf, dn_v, dj_v, ds_v, dall, bv = some(12)
    ss, rs_, ls, mss, mrs, mls, sss, srs, gss, grs, vsem = some(11)
    zs, zr, xs, xr, ys, yr, cs, cr = some(8)

    chunks = []
    a = 0
    for t, (i, kind, j, cb) in enumerate(plan):
        sem = dict(sem=(ss.at[t], rs_.at[t]), lsem=ls.at[t])
        if kind == SHARED:
            col = pl.ds(cb * DIM, DIM)
            gi, o = ins[i], outs[i]
            chunks.append(NS(kind=kind, g=lambda c, gi=gi, j=j, col=col: gi.at[:, :, j, :, c, :, col], out=lambda y, c, o=o, j=j, col=col: o.at[j, y, c, :, col],
                             own=s_own.at[a], rc=s_rc.at[a], ry=s_ry.at[a], rx=s_rx.at[a], rz=s_rz.at[a], fin=s_fin.at[a], **sem))
            a += 1
        elif kind == PRIVATE:
            p, o = pv[i], (o_heads, o_expand, o_reduce)[i]
            chunks.append(NS(kind=kind, out=lambda y, c, o=o: o.at[0, y, c], own=p[0], rx=p[1], rz=p[2], fin=p[3], **sem))
        else:
            p, o = late[i], (o_table, o_gains)[i]
            chunks.append(NS(kind=kind, src=p[0], g=lambda c, p=p: p[0].at[:, :, :, c], out=lambda y, c, o=o: o.at[0, y, c],
                             own=p[1], rc=p[2], ry=p[3], rx=p[4], rz=p[5], fin=p[6], **sem))
    r = Reduce(chunks)
    bar = pltpu.get_barrier_semaphore()
    for dev in r.peers(): pl.semaphore_signal(bar, inc=1, device_id=dev, device_id_type=MESH)
    pl.semaphore_wait(bar, 7)
    st = r.steps()
    next(st)
    done = [0]
    total_steps = r.count()

    def pump(n=1):
        for _ in range(n):
            if done[0] < total_steps:
                next(st)
                done[0] += 1

    gs = NS(zs=zs, zr=zr, xs=xs, xr=xr, ys=ys, yr=yr, cs=cs, cr=cr)
    gplan = [(0, SHARED, 0, 0, DIM)]
    g = Gather(gather_chunks(gplan, [ds_v], [dall]), gs)

    def take(src, dst, i):
        k = pltpu.make_async_copy(src, dst, vsem.at[i])
        k.start()
        return k

    ga = g.cp(d_ref, gall.at[g.slot], gss.at[0], grs.at[0], g.ydev)
    gb = g.cp(d_ref, gall.at[g.slot], gss.at[1], grs.at[1], g.cdev)
    ga.start()
    gb.start()
    loads = [take(wd_h, wd_v, 0), take(wu_h, wu_v, 1), take(wm_h, wm_v, 2), take(wh_h, wh_v, 3), take(ids_h.at[0], ids_v, 4), take(lookup_h, lookup_v, 5)]
    gall[g.slot] = d_ref[...]
    gains = gains_r[...]
    expanded = expanded_r[...]
    hidden = gelu_tanh(expanded).astype(BF)
    normal_two, scale_two = normed(middle_r[...])
    norm_two = (normal_two * gains[1:2]).astype(BF)
    ga.wait_recv()
    there = gall.at[g.ydev[1]]
    gc = g.cp(there, there, gss.at[2], grs.at[2], g.cdev)
    gc.start()
    pump(1)
    gb.wait_recv()
    gc.wait_recv()
    g_low = gall[...].reshape(128, DIM)
    grad = g_low.astype(F32)
    for k in loads[:4]:
        k.wait()
    wd = wd_v[...].reshape(DIM, DIM)
    d_expanded = (dot(g_low, wd, 1, 1) * gelu_slope(expanded)).astype(BF)
    sums = [SlotSum(g, part.at[i], rc.at[i], s1.at[i], ry.at[i], fin.at[i], rf.at[i], sss.at[i], srs.at[i]) for i in range(2)]

    def reduce_grad():
        pv[2][0][...] = dot(hidden, g_low, 0, 0).astype(BF).reshape(4, 2, 96, DIM)
        pump(2)

    sums[0].run(dot(d_expanded, wu_v[...].reshape(DIM, DIM), 1, 1), dn_v, reduce_grad)
    pv[1][0][...] = dot(norm_two, d_expanded, 0, 0).astype(BF).reshape(4, 2, 96, DIM)
    d_part, g_midnorm = norm_back(dn_v[...].reshape(128, DIM), normal_two, scale_two, gains[1:2])
    d_middle = grad + d_part
    middle_low = d_middle.astype(BF)
    mixture = mixture_r[...]
    m_own[...] = dot(mixture, middle_low, 0, 0).astype(BF).reshape(2, 96, DIM)
    m = Mixer(r, None, m_own, m_rx, m_rz, m_fin, o_mixer, mss, mrs, mls)
    ms = m.steps()
    next(ms)
    d_mixture = dot(middle_low, wm_v[...].reshape(192, DIM), 1, 1).astype(BF)
    pump(1)
    joined = joined_r[...].astype(F32)
    q = joined[:, 0:192].astype(BF)
    k = joined[:, 192:384].astype(BF)
    v = joined[:, 384:576].astype(BF)
    allowed = allow_r[...] > 0
    zero = jnp.zeros_like(q)
    dq = dk = dv = jnp.zeros((128, 192), F32)
    for h in range(3):
        lanes = head_lanes(192, h)
        soft = softmax_rows(dot(jnp.where(lanes, q, zero), k, 1, 1) * HEAD_DIM ** (-0.5), allowed)
        d_soft = dot(jnp.where(lanes, d_mixture, zero), v, 1, 1)
        d_s = (soft * (d_soft - jnp.sum(d_soft * soft, axis=-1, keepdims=True))).astype(BF)
        dq = jnp.where(lanes, dot(d_s, k), dq)
        dk = jnp.where(lanes, dot(d_s, q, 0, 0), dk)
        dv = jnp.where(lanes, dot(soft.astype(BF), d_mixture, 0, 0), dv)
    dj_v[:, 0:192] = (dq * HEAD_DIM ** (-0.5)).astype(BF)
    dj_v[:, 192:384] = (dk * HEAD_DIM ** (-0.5)).astype(BF)
    dj_v[:, 384:576] = dv.astype(BF)
    d_joined = dj_v[...]
    normal_one, scale_one = normed(start_r[...])
    norm_one = (normal_one * gains[0:1]).astype(BF)

    def heads_grad():
        pv[0][0][...] = dot(norm_one, d_joined, 0, 0).astype(BF).reshape(4, 2, 96, 576)
        pump(2)

    sums[1].run(dot(d_joined, wh_v[...].reshape(DIM, 576), 1, 1), dn_v, heads_grad)
    d_part, g_prenorm = norm_back(dn_v[...].reshape(128, DIM), normal_one, scale_one, gains[0:1])
    ds_v[...] = (d_middle + d_part).astype(BF).reshape(1, 2, 2, 32, DIM)
    next(ms)
    gst = g.steps()
    next(gst)
    for yy in range(2):
        dall[g.z, g.x, 0, yy, g.c] = ds_v[0, yy, g.c]
    first = jnp.where(g.slot == 0, 1.0, 0.0)
    rows = jnp.concatenate([g_prenorm * first, g_midnorm * first, bgain_r[0:2, :], jnp.zeros((12, DIM), F32)], axis=0).astype(BF)
    fr = lax.broadcasted_iota(jnp.int32, (DIM, 128), 0)
    fc = lax.broadcasted_iota(jnp.int32, (DIM, 128), 1)
    gsrc = late[1][0]
    gsrc[...] = jnp.zeros_like(gsrc)
    for i in range(8):
        sel = ((fr == fc + i * 96) & (fc < 96)).astype(BF)
        gsrc[i // 2, i % 2, 0, 0] = dot(rows, sel)[0:8].astype(BF)
    for k in loads[4:6]:
        k.wait()
    lookup = lookup_v[...].reshape(256, DIM)
    lookup_t[...] = lookup.astype(F32).T.astype(BF)
    projz[...] = jnp.zeros_like(projz)
    take(own_proj_h, projz.at[:, pl.ds(pl.multiple_of(g.dp * 96, 32), 96), :], 6).wait()
    for i, _ in enumerate(gst):
        if i % 3 == 2:
            pump(1)
    g.finish(0)
    next(ms)
    vocab_row = lax.broadcasted_iota(jnp.int32, (256, 128), 0)
    table = table_r[...]
    mine = lookup_t[pl.ds(pl.multiple_of(g.dp * 96, 32), 96), :]
    for p in range(2):
        bv[...] = jnp.zeros_like(bv)

        @pl.loop(0, 4)
        def _(i):
            for xx in range(2):
                hot = (vocab_row == ids_v[i, xx, pl.ds(g.slot * 2 + p, 1), :]).astype(BF)
                bv[...] += dot(hot, dall[i, xx].reshape(128, DIM))

        low = bv[...].astype(BF)
        pgrad_o[p] = dot(mine, low)
        table = table + dot(low, projz[p], 1, 1)
        pump(1)
    tsrc = late[0][0]
    tsrc[...] = table.astype(BF).reshape(4, 2, 2, 2, 8, DIM)
    while done[0] < total_steps:
        pump(1)
        next(ms, 0)
    for _ in ms: pass
    for _ in st: pass
    g.drain(0)
    for k in (ga, gb, gc): k.wait_send()
    for s in sums: s.drain()


def backward_call(grads, hbm_in, vm_in, plan):
    hbm = pl.BlockSpec(memory_space=pl.ANY)
    vm = pl.BlockSpec(memory_space=pltpu.VMEM)
    S = lambda *s: jax.ShapeDtypeStruct(s, BF)
    V = lambda *s: pltpu.VMEM(s, BF)
    VF = lambda *s: pltpu.VMEM(s, F32)
    D = pltpu.SemaphoreType.DMA
    outs = [S(*v.shape[2:]) for v in grads]
    outs += [S(1, 2, 2, 96, 576), S(1, 2, 2, 96, DIM), S(1, 2, 2, 96, DIM), S(96, DIM), S(1, 2, 2, 8, DIM), S(1, 2, 2, 8, 128)]
    u = 24
    ns = sum(p[1] == SHARED for p in plan)
    scr = [V(ns, 4, 2, 2, u, DIM), V(ns, 4, 2, 2, u, DIM), V(ns, 4, 2, u, DIM), V(ns, 4, u, DIM), V(ns, 3, u, DIM), V(ns, u, DIM)]
    for C in (576, DIM, DIM):
        scr += [V(4, 2, 96, C), V(4, 96, C), V(3, 96, C), V(96, C)]
    scr += [V(2, 96, DIM), V(96, DIM), V(3, 96, DIM), V(96, DIM)]
    for C in (DIM, 128):
        scr += [V(4, 2, 2, 2, 8, C), V(4, 2, 2, 8, C), V(4, 2, 2, 8, C), V(4, 2, 8, C), V(4, 8, C), V(3, 8, C), V(8, C)]
    scr += [V(4, 2, 96, 576), V(2, 96, DIM), V(4, 2, 96, DIM), V(4, 2, 96, DIM), pltpu.VMEM((4, 2, 8, 128), jnp.int32), V(256, DIM), V(DIM, 256), V(2, DIM, DIM)]
    scr += [V(4, 32, DIM), V(2, 2, 64, DIM)] + [V(2, 64, DIM)] * 5 + [VF(2, 64, DIM), V(128, 576), V(1, 2, 2, 32, DIM), V(4, 2, 1, 2, 2, 32, DIM), VF(256, DIM)]
    T = len(plan)
    scr += [D((T, 9)), D((T, 9)), D((T, 2)), D((7,)), D((7,)), D((2,)), D((2, 3)), D((2, 3)), D((3,)), D((3,)), D((7,))]
    scr += gather_sems([(0, SHARED)], 1)[:8]
    return pl.pallas_call(
        functools.partial(backward_kernel, plan, len(grads)),
        out_shape=outs + [jax.ShapeDtypeStruct((2, 96, DIM), F32)],
        in_specs=[hbm] * (len(grads) + len(hbm_in)) + [vm] * len(vm_in),
        out_specs=[hbm] * len(outs) + [vm],
        scratch_shapes=scr,
        compiler_params=pltpu.CompilerParams(collective_id=1, has_side_effects=True, vmem_limit_bytes=62 * 2**20),
        name="reduce_backward",
    )(*grads, *hbm_in, *vm_in)


def mm(spec, a, b):
    return jnp.einsum(spec, a, b, preferred_element_type=F32)


def local(
    byte_ids,
    seg_ids,
    embed_table,
    slot_project,
    patch_prenorm,
    patch_heads,
    patch_mixer,
    patch_midnorm,
    patch_expand,
    patch_reduce,
    byte_prenorm,
    byte_heads,
    byte_mixer,
    byte_midnorm,
    byte_expand,
    byte_reduce,
    d_output,
):
    dp = lax.axis_index(DP)
    slot = lax.axis_index(SLOT)
    x = dp % 2
    group_rows, patch_len = byte_ids.shape
    own_rows = group_rows // 4
    vocab_part, width = embed_table.shape
    vocab = vocab_part * 8
    share = width // 8
    ff = patch_expand.shape[1]
    quarter = share // 4
    pick = lambda v, axis: lax.dynamic_index_in_dim(v, slot, axis, keepdims=False)
    gains = jnp.stack([patch_prenorm, patch_midnorm, byte_prenorm, byte_midnorm])
    gains = jnp.pad(gains, ((0, 12), (0, 128 - share)))[None]
    heads_own = pick(patch_heads.reshape(share, 3, 4, width // 4), 2).reshape(1, share, 3 * width // 4)
    expand_own = pick(patch_expand.reshape(share, 8, 4, share), 2).reshape(1, share, width)
    reduce_own = pick(patch_reduce.reshape(4, share, width), 0)[None]
    shared = lambda v: v.reshape(v.shape[0] // share, 2, 2, quarter, v.shape[1])
    arrs = [
        embed_table.reshape(1, 2, 2, vocab_part // 4, width), byte_ids.T[None], gains, slot_project,
        heads_own, expand_own, reduce_own, patch_mixer[None],
        shared(byte_heads), shared(byte_mixer), shared(byte_expand), shared(byte_reduce),
    ]
    kinds = [SHARED, PRIVATE, PRIVATE, ZONLY, PRIVATE, PRIVATE, PRIVATE, SINGLE] + [SHARED] * 4
    wide = [(8, SHARED, 0, i * width, width) for i in range(3)] + [(9, SHARED, 0, 0, width)]
    wide += [(10, SHARED, 0, i * width, width) for i in range(4)] + [(11, SHARED, i, 0, width) for i in range(4)]
    plan = [(1, PRIVATE, 0, 0, 0), (2, PRIVATE, 0, 0, 0), (0, SHARED, 0, 0, width)] + wide[:2]
    plan += [(3, ZONLY, 0, 0, 0), (3, ZONLY, 1, 0, 0), (4, PRIVATE, 0, 0, 0)] + wide[2:4] + [(7, SINGLE, 0, 0, 0)]
    plan += wide[4:5] + [(5, PRIVATE, 0, 0, 0)] + wide[5:7] + [(6, PRIVATE, 0, 0, 0)] + wide[7:]
    segments = seg_ids[0]
    pos = jnp.arange(group_rows, dtype=jnp.int32)
    allowed_patch = ((pos[:, None] >= pos[None, :]) & (segments[:, None] == segments[None, :]))[None]
    full = forward_call(arrs, kinds, plan, allowed_patch[0].astype(F32))
    start, joined, mixture, middle, expanded, patch_out, gains_all = full[12:]
    lookup = full[0].reshape(vocab, width)
    ids_all = full[1].reshape(8, patch_len, group_rows)
    p_heads = full[4].reshape(width, 3 * width // 4)
    p_expand = full[5].reshape(width, width)
    p_reduce = full[6].reshape(width, width)
    p_mixer = full[7].reshape(width // 4, width)
    b_heads = full[8].reshape(width, 3 * width)
    b_mixer = full[9].reshape(width, width)
    b_expand = full[10].reshape(width, ff)
    b_reduce = full[11].reshape(ff, width)
    vocab_iota = jnp.arange(vocab, dtype=jnp.int32)
    hot = lambda ids: (ids[..., None] == vocab_iota).astype(BF)
    patch_out = patch_out.reshape(group_rows, width)
    start = start.reshape(group_rows, width)
    first_row = slot * own_rows
    own_out = lax.dynamic_slice_in_dim(patch_out, first_row, own_rows, 0)
    local_bytes = lax.dynamic_slice_in_dim(byte_ids, first_row, own_rows, 0)
    local_onehot = hot(local_bytes)
    local_embed = mm("rpv,vd->rpd", local_onehot, lookup)
    fine_input = local_embed + own_out[:, None, :]
    tile_len = math.gcd(own_rows * patch_len, 128)
    tile_count = own_rows * patch_len // tile_len
    fine_input = fine_input.reshape(tile_count, tile_len, width)
    positions = jnp.arange(tile_len, dtype=jnp.int32)
    allowed_byte = (
        (positions[:, None] >= positions[None, :])
        & (positions[:, None] // patch_len == positions[None, :] // patch_len)
    )[None]

    def attend_byte(queries, keyset, valueset):
        return attention(queries, keyset, valueset, allowed_byte)

    def attend_byte_back(queries, keyset, valueset, kept, d_mixture):
        return attention_back(queries, keyset, valueset, allowed_byte, kept, d_mixture)

    byte_weights = (gains_all[2], b_heads, b_mixer, gains_all[3], b_expand, b_reduce)
    byte_out, byte_saved = block_forward(fine_input, byte_weights, attend_byte)
    out_bytes = byte_out.reshape(own_rows, patch_len, width).astype(BF)
    d_fine, byte_grads = block_backward(
        d_output.astype(F32).reshape(tile_count, tile_len, width), byte_weights, byte_saved, attend_byte_back
    )
    d_fine = d_fine.reshape(own_rows, patch_len, width)

    byte_pre, byte_qkv, byte_mix, byte_mid, byte_exp, byte_red = byte_grads
    d_own = jnp.sum(d_fine, axis=1).astype(BF)
    low_fine = d_fine.astype(BF)
    rest_fine = (d_fine - low_fine.astype(F32)).astype(BF)
    table = mm("rpv,rpd->vd", local_onehot, low_fine) + mm("rpv,rpd->vd", local_onehot, rest_fine)
    grouped = lambda v: v.astype(BF).reshape(4, 2, v.shape[0] // width, 2, 2, quarter, v.shape[1])
    grads = [grouped(byte_qkv), grouped(byte_mix), grouped(byte_exp), grouped(byte_red)]
    wide = [(3, SHARED, i, 0) for i in range(4)] + [(2, SHARED, 0, i) for i in range(4)]
    wide += [(1, SHARED, 0, 0)] + [(0, SHARED, 0, i) for i in range(3)]
    gplan = wide[:3] + [(2, PRIVATE, 0, 0)] + wide[3:5] + [(1, PRIVATE, 0, 0)] + wide[5:9] + [(0, PRIVATE, 0, 0)] + wide[9:]
    gplan += [(0, LATE, 0, 0), (1, LATE, 0, 0)]
    hbm_in = [full[4][0], full[7][0], full[5][0], full[6][0], full[1], lookup, slot_project]
    vm_in = [d_own, start.reshape(group_rows, width), joined, mixture, middle, expanded, gains_all, allowed_patch[0].astype(F32), table, jnp.stack([byte_pre, byte_mid])]
    res = backward_call(grads, hbm_in, vm_in, gplan)
    r_heads, r_expand, r_reduce, r_mixer, r_table, r_gains, project_grad = res[4:]
    gain_out = r_gains[0, 0, 0, :4, :share].astype(F32)
    out_heads = r_heads.reshape(4, share, 3, width // 4).transpose(1, 2, 0, 3).reshape(share, 3 * width)
    out_expand = r_expand.reshape(4, share, 8, share).transpose(1, 2, 0, 3).reshape(share, ff)
    return (
        out_bytes,
        r_table.reshape(vocab_part, width).astype(F32),
        project_grad,
        gain_out[0],
        out_heads.astype(F32),
        r_mixer.astype(F32),
        gain_out[1],
        out_expand.astype(F32),
        r_reduce.reshape(4 * share, width).astype(F32),
        gain_out[2],
        res[0].reshape(share, 3 * width).astype(F32),
        res[1].reshape(share, width).astype(F32),
        gain_out[3],
        res[2].reshape(share, ff).astype(F32),
        res[3].reshape(4 * share, width).astype(F32),
    )


def solution(mesh):
    if (mesh.shape[DP], mesh.shape[SLOT]) != (8, 4):
        return generic_solution(mesh)
    placed = (P(DP, None), P(DP, None), P(DP, None), P(SLOT, DP, None)) + (
        P(DP), P(DP, None), P(DP, None), P(DP), P(DP, None), P(DP, None),
    ) * 2 + (P((DP, SLOT), None, None),)
    outs = (P((DP, SLOT), None, None), P(DP, None), P(SLOT, DP, None)) + (
        P(DP), P(DP, None), P(DP, None), P(DP), P(DP, None), P(DP, None),
    ) * 2
    return jax.shard_map(local, mesh=mesh, in_specs=placed, out_specs=outs, check_vma=False)
```
